32 devices in a mesh: rep: 16 (over z, y, core), shard: 2 (over x).
Axes of the slice: x: 2, y: 2, z: 4, core: 2. Of those that a mesh axis runs over, the one named last changes fastest.
Arguments:
- inputs: bfloat16 [4096, 1024], P(('rep', 'shard')), may hold values from -6 to 6
- attn_gain: bfloat16 [1024], P('shard'), may hold values from 0.25 to 1.75
- attn_shift: bfloat16 [1024], P('shard'), may hold values from -3 to 3
- feed_gain: bfloat16 [1024], P('shard'), may hold values from 0.25 to 1.75
- feed_shift: bfloat16 [1024], P('shard'), may hold values from -3 to 3
- qkv_weight: bfloat16 [1024, 3072], P(None, 'shard'), may hold values from -0.1875 to 0.1875
- qkv_bias: bfloat16 [3072], P('shard'), may hold values from -3 to 3
- out_weight: bfloat16 [1024, 1024], P(None, 'shard'), may hold values from -0.75 to 0.75
- out_bias: bfloat16 [1024], P('shard'), may hold values from -3 to 3
- up_weight: bfloat16 [1024, 4096], P(None, 'shard'), may hold values from -0.1875 to 0.1875
- up_bias: bfloat16 [4096], P('shard'), may hold values from -3 to 3
- down_weight: bfloat16 [4096, 1024], P('shard'), may hold values from -0.09375 to 0.09375
- down_bias: bfloat16 [1024], P('shard'), may hold values from -3 to 3
- cotangent: bfloat16 [4096, 1024], P(('rep', 'shard')), may hold values from -6 to 6
Outputs:
- outputs: bfloat16 [4096, 1024], P(('rep', 'shard'))
- input_grad: float32 [4096, 1024], P(('rep', 'shard'))
- grad_attn_gain: float32 [1024], P('shard')
- grad_attn_shift: float32 [1024], P('shard')
- grad_feed_gain: float32 [1024], P('shard')
- grad_feed_shift: float32 [1024], P('shard')
- grad_qkv_weight: float32 [1024, 3072], P(None, 'shard')
- grad_qkv_bias: float32 [3072], P('shard')
- grad_out_weight: float32 [1024, 1024], P(None, 'shard')
- grad_out_bias: float32 [1024], P('shard')
- grad_up_weight: float32 [1024, 4096], P(None, 'shard')
- grad_up_bias: float32 [4096], P('shard')
- grad_down_weight: float32 [4096, 1024], P('shard')
- grad_down_bias: float32 [1024], P('shard')
The draws below stay inside these ranges and needn't reach their ends.
All inputs are finite; a program needn't handle non-finite values.
Results may differ from the reference program's by a relative error of at most 0.012.
Values may be sent and summed in bfloat16 or wider, within the bound.
No kernel may reach another device: no remote copies, remote signals or barrier semaphores. Data moves between devices by JAX's collectives and lax.ppermute only.
A program may use at most 192 MiB of HBM per device.

```python
import math
import jax
import jax.numpy as jnp
from jax import lax

D = 1024
H = 16
HD = 64
ROT = 16
FF = 4096
LEN = 128
TOKENS = 4096


def spiked(entries, own_key, source, target, blocks, factor):
    owner, partner = [(jnp.arange(entries.shape[dim]) // (entries.shape[dim] // blocks)).reshape([-1 if axis == dim else 1 for axis in range(entries.ndim)]) for dim in (source, target)]
    chosen = jax.random.permutation(own_key, blocks)[partner]
    strong = (owner == chosen) | (owner == (partner + blocks // 2) % blocks)
    return jnp.where(strong, factor * entries, entries)


def levels(stream_key, extent, cuts, least, top_value):
    def one(position, parts):
        heights = jax.random.uniform(jax.random.fold_in(jax.random.fold_in(stream_key, 6), position), (parts,), jnp.float32, least / len(cuts), top_value / len(cuts))
        return jnp.repeat(jnp.exp(heights), extent[position] // parts).reshape((-1,) + (1,) * (len(extent) - position - 1))

    loudness = one(*cuts[0])
    for cut in cuts[1:]:
        loudness = loudness * one(*cut)
    return loudness


def bell_draw(rng, dims, spread, reach, shards=(), dtype=jnp.bfloat16):
    level = levels(rng, dims, shards, -0.22, 0.18) if shards else 1.0
    values = jax.random.normal(rng, dims, jnp.float32) * spread * level
    return jnp.minimum(jnp.maximum(values, -reach), reach).astype(dtype)


def gaussian_with(stream_key, dims, width, bound, cuts, heavy, held_as=jnp.bfloat16):
    entries = width * jax.random.normal(stream_key, dims, jnp.float32)
    if cuts:
        entries = entries * levels(stream_key, dims, cuts, -0.22, 0.18)
    return jnp.clip(spiked(entries, jax.random.fold_in(stream_key, 3), *heavy), -bound, bound).astype(held_as)


def setup_inputs(seed: int = 0) -> dict:
    key_of = jax.random.split(jax.random.key(seed), 15)
    return {
        "inputs": bell_draw(key_of[0], (TOKENS, D), 1.0, 6.0, ((0, 32),)),
        "attn_gain": jnp.clip(1.0 + 0.15 * jax.random.normal(key_of[1], (D,), jnp.float32), 0.25, 1.75).astype(jnp.bfloat16),
        "attn_shift": bell_draw(key_of[2], (D,), 0.5, 3.0, ((0, 2),)),
        "feed_gain": jnp.clip(1.0 + 0.15 * jax.random.normal(key_of[3], (D,), jnp.float32), 0.25, 1.75).astype(jnp.bfloat16),
        "feed_shift": bell_draw(key_of[4], (D,), 0.5, 3.0, ((0, 2),)),
        "qkv_weight": bell_draw(key_of[5], (D, 3 * D), D ** -0.5, 0.1875, ((1, 2),)),
        "qkv_bias": bell_draw(key_of[6], (3 * D,), 0.5, 3.0, ((0, 2),)),
        "out_weight": bell_draw(key_of[7], (D, D), (D // 16) ** -0.5, 0.75, ((1, 2),)),
        "out_bias": bell_draw(key_of[8], (D,), 0.5, 3.0, ((0, 2),)),
        "up_weight": bell_draw(key_of[9], (D, FF), D ** -0.5, 0.1875, ((1, 2),)),
        "up_bias": bell_draw(key_of[10], (FF,), 0.5, 3.0, ((0, 2),)),
        "down_weight": bell_draw(key_of[11], (FF, D), FF ** -0.5, 0.09375, ((0, 2),)),
        "down_bias": bell_draw(key_of[12], (D,), 0.5, 3.0, ((0, 2),)),
        "cotangent": gaussian_with(key_of[13], (TOKENS, D), 1.0, 6.0, ((0, 32),), (0, 1, 32, 2.75)),
    }


norm_eps = 1e-05
base_freq = 10000.0

def round_trip(values):
    return lax.optimization_barrier(values.astype(jnp.bfloat16)).astype(jnp.float32)

def rotary_tables(length, rotary_dims):
    half_dims = rotary_dims // 2
    positions = jnp.arange(length).astype(jnp.float32)
    inverse = jnp.exp(jnp.arange(half_dims).astype(jnp.float32) * (-2.0 * math.log(base_freq) / rotary_dims))
    angles = positions[:, None] * inverse[None, :]
    return (jnp.cos(angles), jnp.sin(angles))

def rotate(values, cosine, sine_table, rotary_dims, direction):
    half_dims = rotary_dims // 2
    lower_half = values[..., :half_dims]
    upper_half = values[..., half_dims:rotary_dims]
    cosine_row = cosine[:, None, :]
    sine_row = sine_table[:, None, :] * direction
    return jnp.concatenate([lower_half * cosine_row - upper_half * sine_row, upper_half * cosine_row + lower_half * sine_row, values[..., rotary_dims:]], axis=-1)

def gelu_slope(preact):
    normal_cdf = 0.5 * (1.0 + jax.scipy.special.erf(preact * (1.0 / math.sqrt(2.0))))
    return normal_cdf + preact * jnp.exp(-0.5 * preact * preact) * (1.0 / math.sqrt(2.0 * math.pi))

def sequences_pass(x_rows, dy_rows, weights):
    attn_gain, attn_shift, feed_gain, feed_shift, qkv_weight, qkv_bias, out_weight, out_bias, up_weight, up_bias, down_weight, down_bias = weights
    total_rows = x_rows.shape[0]
    seq_count = total_rows // LEN
    gain_one = attn_gain.astype(jnp.float32)
    gain_two = feed_gain.astype(jnp.float32)
    resid = x_rows.astype(jnp.float32)
    row_mean = lax.optimization_barrier(jnp.mean(resid, -1, keepdims=True))
    centered = resid - row_mean
    inv_std = lax.rsqrt(lax.optimization_barrier(jnp.mean(centered * centered, -1, keepdims=True)) + norm_eps)
    normed = centered * inv_std
    attn_in = (normed * gain_one + attn_shift.astype(jnp.float32)).astype(jnp.bfloat16)
    feed_in = (normed * gain_two + feed_shift.astype(jnp.float32)).astype(jnp.bfloat16)
    projected = jnp.dot(attn_in, qkv_weight, preferred_element_type=jnp.float32) + qkv_bias.astype(jnp.float32)
    projected = projected.reshape(seq_count, LEN, 3, H, HD)
    cosine, sine_table = rotary_tables(LEN, ROT)
    query_f = round_trip(rotate(projected[:, :, 0], cosine, sine_table, ROT, 1.0))
    keys_f = round_trip(rotate(projected[:, :, 1], cosine, sine_table, ROT, 1.0))
    values_f = round_trip(projected[:, :, 2])
    score_scale = 1.0 / math.sqrt(HD)
    causal = jnp.arange(LEN)[:, None] >= jnp.arange(LEN)[None, :]
    scores = jnp.einsum('bqhd,bkhd->bhqk', query_f, keys_f) * score_scale
    scores = jnp.where(causal[None, None], scores, -jnp.inf)
    row_max = lax.optimization_barrier(jnp.max(scores, -1, keepdims=True))
    log_total = row_max + jnp.log(lax.optimization_barrier(jnp.sum(jnp.exp(scores - row_max), -1, keepdims=True)))
    probs_f = jnp.exp(scores - log_total)
    probs_b = round_trip(probs_f)
    attended = jnp.einsum('bhqk,bkhd->bqhd', probs_b, values_f).astype(jnp.bfloat16).reshape(total_rows, D)
    attn_out = jnp.dot(attended, out_weight, preferred_element_type=jnp.float32) + out_bias.astype(jnp.float32)
    preact = jnp.dot(feed_in, up_weight, preferred_element_type=jnp.float32) + up_bias.astype(jnp.float32)
    hidden = jax.nn.gelu(preact, approximate=False).astype(jnp.bfloat16)
    feed_out = jnp.dot(hidden, down_weight, preferred_element_type=jnp.float32) + down_bias.astype(jnp.float32)
    outputs = (resid + attn_out + feed_out).astype(jnp.bfloat16)
    grad_top = dy_rows.astype(jnp.float32)
    grad_bias = lax.optimization_barrier(jnp.sum(grad_top, 0))
    grad_out_w = jnp.dot(attended.T, dy_rows, preferred_element_type=jnp.float32)
    grad_attended = jnp.dot(dy_rows, out_weight.T, preferred_element_type=jnp.float32).astype(jnp.bfloat16)
    grad_down = jnp.dot(hidden.T, dy_rows, preferred_element_type=jnp.float32)
    grad_preact = jnp.dot(dy_rows, down_weight.T, preferred_element_type=jnp.float32) * gelu_slope(preact)
    grad_up_b = lax.optimization_barrier(jnp.sum(grad_preact, 0))
    grad_preact_b = grad_preact.astype(jnp.bfloat16)
    grad_up = jnp.dot(feed_in.T, grad_preact_b, preferred_element_type=jnp.float32)
    grad_feed_in = jnp.dot(grad_preact_b, up_weight.T, preferred_element_type=jnp.float32)
    grad_att_f = grad_attended.astype(jnp.float32).reshape(seq_count, LEN, H, HD)
    grad_values = jnp.einsum('bhqk,bqhd->bkhd', probs_b, grad_att_f)
    grad_probs = jnp.einsum('bqhd,bkhd->bhqk', grad_att_f, values_f)
    grad_scores = probs_f * (grad_probs - lax.optimization_barrier(jnp.sum(probs_f * grad_probs, -1, keepdims=True))) * score_scale
    grad_scores_f = round_trip(grad_scores)
    grad_qrot = jnp.einsum('bhqk,bkhd->bqhd', grad_scores_f, keys_f)
    grad_krot = jnp.einsum('bhqk,bqhd->bkhd', grad_scores_f, query_f)
    grad_query = rotate(grad_qrot, cosine, sine_table, ROT, -1.0)
    grad_keys = rotate(grad_krot, cosine, sine_table, ROT, -1.0)
    grad_proj = jnp.stack([grad_query, grad_keys, grad_values], axis=2).reshape(total_rows, 3 * D)
    grad_qkv_b = lax.optimization_barrier(jnp.sum(grad_proj, 0))
    grad_proj_b = grad_proj.astype(jnp.bfloat16)
    grad_qkv = jnp.dot(attn_in.T, grad_proj_b, preferred_element_type=jnp.float32)
    grad_attn_in = jnp.dot(grad_proj_b, qkv_weight.T, preferred_element_type=jnp.float32)
    grad_gain_one = lax.optimization_barrier(jnp.sum(grad_attn_in * normed, 0))
    grad_shift_one = lax.optimization_barrier(jnp.sum(grad_attn_in, 0))
    grad_gain_two = lax.optimization_barrier(jnp.sum(grad_feed_in * normed, 0))
    grad_shift_two = lax.optimization_barrier(jnp.sum(grad_feed_in, 0))
    grad_normed = grad_attn_in * gain_one + grad_feed_in * gain_two
    input_grad = grad_top + inv_std * (grad_normed - lax.optimization_barrier(jnp.mean(grad_normed, -1, keepdims=True)) - normed * lax.optimization_barrier(jnp.mean(grad_normed * normed, -1, keepdims=True)))
    grads = (grad_gain_one, grad_shift_one, grad_gain_two, grad_shift_two, grad_qkv, grad_qkv_b, grad_out_w, grad_bias, grad_up, grad_up_b, grad_down, grad_bias)
    return (outputs, input_grad, grads)

def reference(inputs, attn_gain, attn_shift, feed_gain, feed_shift, qkv_weight, qkv_bias, out_weight, out_bias, up_weight, up_bias, down_weight, down_bias, cotangent):
    seqs_block = math.gcd(TOKENS // LEN, max(1, 4096 // LEN))
    block_rows = seqs_block * LEN
    block_count = TOKENS // block_rows
    weights = (attn_gain, attn_shift, feed_gain, feed_shift, qkv_weight, qkv_bias, out_weight, out_bias, up_weight, up_bias, down_weight, down_bias)
    x_blocks = inputs.reshape(block_count, block_rows, D)
    dy_blocks = cotangent.reshape(block_count, block_rows, D)
    initial = tuple((jnp.zeros(w.shape, jnp.float32) for w in weights))

    def step_block(carry, pair):
        outputs, input_grad, grads = sequences_pass(pair[0], pair[1], weights)
        return (tuple((a + b for a, b in zip(carry, grads))), (outputs, input_grad))
    grads, (out_blocks, grad_blocks) = lax.scan(step_block, initial, (x_blocks, dy_blocks))
    return (out_blocks.reshape(TOKENS, D), grad_blocks.reshape(TOKENS, D), grads[0], grads[1], grads[2], grads[3], grads[4], grads[5], grads[6], grads[7], grads[8], grads[9], grads[10], grads[11])
```

```python
import math

import jax
import jax.numpy as jnp
from jax import lax
from jax.experimental import pallas as pl
from jax.experimental.pallas import tpu as pltpu
from jax.sharding import PartitionSpec as P

D = 1024
H = 16
HD = 64
ROT = 16


norm_eps = 1e-05
base_freq = 10000.0


def rotary_tables(length, rotary_dims):
    half_dims = rotary_dims // 2
    positions = jnp.arange(length).astype(jnp.float32)
    inverse = jnp.exp(
        jnp.arange(half_dims).astype(jnp.float32) * (-2.0 * math.log(base_freq) / rotary_dims)
    )
    angles = positions[:, None] * inverse[None, :]
    return (jnp.cos(angles), jnp.sin(angles))


def rotate(values, cosine, sine_table, rotary_dims, direction):
    half_dims = rotary_dims // 2
    lower_half = values[..., :half_dims]
    upper_half = values[..., half_dims:rotary_dims]
    cosine_row = cosine[:, None, :]
    sine_row = sine_table[:, None, :] * direction
    return jnp.concatenate(
        [
            lower_half * cosine_row - upper_half * sine_row,
            upper_half * cosine_row + lower_half * sine_row,
            values[..., rotary_dims:],
        ],
        axis=-1,
    )


def gelu_slope(preact):
    normal_cdf = 0.5 * (1.0 + jax.scipy.special.erf(preact * (1.0 / math.sqrt(2.0))))
    return normal_cdf + preact * jnp.exp(-0.5 * preact * preact) * (1.0 / math.sqrt(2.0 * math.pi))


def general_body(
    inputs,
    attn_gain,
    attn_shift,
    feed_gain,
    feed_shift,
    qkv_weight,
    qkv_bias,
    out_weight,
    out_bias,
    up_weight,
    up_bias,
    down_weight,
    down_bias,
    cotangent,
):
    (
        gain_one,
        shift_one,
        gain_two,
        shift_two,
        out_bias_all,
        down_bias_all,
        qkv_all,
        qkv_bias_all,
        out_all,
    ) = (
        lax.all_gather(attn_gain, "shard", axis=0, tiled=True),
        lax.all_gather(attn_shift, "shard", axis=0, tiled=True),
        lax.all_gather(feed_gain, "shard", axis=0, tiled=True),
        lax.all_gather(feed_shift, "shard", axis=0, tiled=True),
        lax.all_gather(out_bias, "shard", axis=0, tiled=True),
        lax.all_gather(down_bias, "shard", axis=0, tiled=True),
        lax.all_gather(qkv_weight, "shard", axis=1, tiled=True),
        lax.all_gather(qkv_bias, "shard", axis=0, tiled=True),
        lax.all_gather(out_weight, "shard", axis=1, tiled=True),
    )
    gain_one = gain_one.astype(jnp.float32)
    gain_two = gain_two.astype(jnp.float32)
    length = inputs.shape[0]
    resid = inputs.astype(jnp.float32)
    row_mean = jnp.mean(resid, -1, keepdims=True)
    centered = resid - row_mean
    inv_std = lax.rsqrt(jnp.mean(centered * centered, -1, keepdims=True) + norm_eps)
    normed = centered * inv_std
    attn_in = (normed * gain_one + shift_one.astype(jnp.float32)).astype(jnp.bfloat16)
    feed_in = (normed * gain_two + shift_two.astype(jnp.float32)).astype(jnp.bfloat16)
    projected = jnp.dot(attn_in, qkv_all, preferred_element_type=jnp.float32) + qkv_bias_all.astype(
        jnp.float32
    )
    projected = projected.reshape(length, 3, H, HD)
    cosine, sine_table = rotary_tables(length, ROT)
    query_rot = rotate(projected[:, 0], cosine, sine_table, ROT, 1.0).astype(jnp.bfloat16)
    keys_rot = rotate(projected[:, 1], cosine, sine_table, ROT, 1.0).astype(jnp.bfloat16)
    values_b = projected[:, 2].astype(jnp.bfloat16)
    score_scale = 1.0 / math.sqrt(HD)
    row_block = min(512, length)
    block_count = length // row_block
    key_positions = jnp.arange(length)

    def block_scores(row_start, q_rows):
        scores = (
            jnp.einsum("qhd,khd->hqk", q_rows, keys_rot, preferred_element_type=jnp.float32)
            * score_scale
        )
        causal = (row_start + jnp.arange(row_block))[:, None] >= key_positions[None, :]
        return jnp.where(causal[None], scores, -jnp.inf)

    def forward_block(block_index):
        row_start = block_index * row_block
        scores = block_scores(row_start, query_rot)
        row_max = jnp.max(scores, -1, keepdims=True)
        log_total = row_max + jnp.log(jnp.sum(jnp.exp(scores - row_max), -1, keepdims=True))
        attn_probs = jnp.exp(scores - log_total).astype(jnp.bfloat16)
        block_out = jnp.einsum(
            "hqk,khd->qhd", attn_probs, values_b, preferred_element_type=jnp.float32
        )
        return (block_out.astype(jnp.bfloat16), log_total)

    attended, log_totals = lax.map(forward_block, jnp.arange(block_count))
    attended = attended.reshape(length, D)
    attn_out = jnp.dot(attended, out_all, preferred_element_type=jnp.float32) + out_bias_all.astype(
        jnp.float32
    )
    group_in = lax.all_gather(feed_in, "shard", axis=0, tiled=True)
    preact = jnp.dot(group_in, up_weight, preferred_element_type=jnp.float32) + up_bias.astype(
        jnp.float32
    )
    hidden = jax.nn.gelu(preact, approximate=False).astype(jnp.bfloat16)
    rows_in = hidden
    feed_out = lax.psum_scatter(
        jnp.dot(rows_in, down_weight, preferred_element_type=jnp.float32),
        "shard",
        scatter_dimension=0,
        tiled=True,
    ) + down_bias_all.astype(jnp.float32)
    outputs = (resid + attn_out + feed_out).astype(jnp.bfloat16)
    grad_top = cotangent.astype(jnp.float32)
    attn_group, attended_group, out_back = (
        lax.all_gather(attn_in, "shard", axis=0, tiled=True),
        lax.all_gather(attended, "shard", axis=0, tiled=True),
        lax.all_gather(out_weight, "shard", axis=1, tiled=True),
    )
    grad_cols = lax.all_to_all(cotangent, "shard", split_axis=1, concat_axis=0, tiled=True)
    grad_bias = jnp.sum(grad_cols.astype(jnp.float32), 0)
    grad_out_w = jnp.dot(attended_group.T, grad_cols, preferred_element_type=jnp.float32)
    grad_attended = (
        jnp.dot(cotangent, out_back.T, preferred_element_type=jnp.float32)
        .astype(jnp.bfloat16)
        .reshape(length, H, HD)
    )
    group_grad = lax.all_gather(cotangent, "shard", axis=0, tiled=True)
    grad_down = jnp.dot(hidden.T, group_grad, preferred_element_type=jnp.float32)
    grad_preact = jnp.dot(
        group_grad, down_weight.T, preferred_element_type=jnp.float32
    ) * gelu_slope(preact)
    grad_up_b = jnp.sum(grad_preact, 0)
    grad_preact_b = grad_preact.astype(jnp.bfloat16)
    grad_up = jnp.dot(group_in.T, grad_preact_b, preferred_element_type=jnp.float32)
    rows_in = grad_preact_b
    grad_feed_in = lax.psum_scatter(
        jnp.dot(rows_in, up_weight.T, preferred_element_type=jnp.float32),
        "shard",
        scatter_dimension=0,
        tiled=True,
    )

    def backward_block(carry, block_index):
        grad_keys, grad_values = carry
        row_start = block_index * row_block
        scores = block_scores(row_start, query_rot)
        probs_f = jnp.exp(scores - log_totals[block_index])
        probs_b = probs_f.astype(jnp.bfloat16)
        grad_values = grad_values + jnp.einsum(
            "hqk,qhd->khd", probs_b, grad_attended, preferred_element_type=jnp.float32
        )
        grad_probs = jnp.einsum(
            "qhd,khd->hqk", grad_attended, values_b, preferred_element_type=jnp.float32
        )
        grad_scores = (
            probs_f * (grad_probs - jnp.sum(probs_f * grad_probs, -1, keepdims=True)) * score_scale
        )
        grad_scores_b = grad_scores.astype(jnp.bfloat16)
        grad_qrot = jnp.einsum(
            "hqk,khd->qhd", grad_scores_b, keys_rot, preferred_element_type=jnp.float32
        )
        grad_keys = grad_keys + jnp.einsum(
            "hqk,qhd->khd", grad_scores_b, query_rot, preferred_element_type=jnp.float32
        )
        return ((grad_keys, grad_values), grad_qrot)

    empty_heads = jnp.zeros((length, H, HD), jnp.float32)
    (grad_krot, grad_values), grad_qrot = lax.scan(
        backward_block, (empty_heads, empty_heads), jnp.arange(block_count)
    )
    grad_qrot = grad_qrot.reshape(length, H, HD)
    grad_query = rotate(grad_qrot, cosine, sine_table, ROT, -1.0)
    grad_keys = rotate(grad_krot, cosine, sine_table, ROT, -1.0)
    grad_proj = jnp.stack([grad_query, grad_keys, grad_values], axis=1).reshape(length, 3 * D)
    grad_qkv_b = jnp.sum(grad_proj, 0)
    grad_proj_b = grad_proj.astype(jnp.bfloat16)
    proj_cols = lax.all_to_all(grad_proj_b, "shard", split_axis=1, concat_axis=0, tiled=True)
    grad_qkv = jnp.dot(attn_group.T, proj_cols, preferred_element_type=jnp.float32)
    rows_in = proj_cols
    grad_attn_in = lax.psum_scatter(
        jnp.dot(rows_in, qkv_weight.T, preferred_element_type=jnp.float32),
        "shard",
        scatter_dimension=0,
        tiled=True,
    )
    grad_gain_one = jnp.sum(grad_attn_in * normed, 0)
    grad_shift_one = jnp.sum(grad_attn_in, 0)
    grad_gain_two = jnp.sum(grad_feed_in * normed, 0)
    grad_shift_two = jnp.sum(grad_feed_in, 0)
    grad_normed = grad_attn_in * gain_one + grad_feed_in * gain_two
    input_grad = grad_top + inv_std * (
        grad_normed
        - jnp.mean(grad_normed, -1, keepdims=True)
        - normed * jnp.mean(grad_normed * normed, -1, keepdims=True)
    )
    grad_qkv_b, grad_gain_one, grad_shift_one, grad_gain_two, grad_shift_two = (
        lax.psum_scatter(grad_qkv_b, "shard", scatter_dimension=0, tiled=True),
        lax.psum_scatter(grad_gain_one, "shard", scatter_dimension=0, tiled=True),
        lax.psum_scatter(grad_shift_one, "shard", scatter_dimension=0, tiled=True),
        lax.psum_scatter(grad_gain_two, "shard", scatter_dimension=0, tiled=True),
        lax.psum_scatter(grad_shift_two, "shard", scatter_dimension=0, tiled=True),
    )
    (
        grad_gain_one,
        grad_shift_one,
        grad_gain_two,
        grad_shift_two,
        grad_qkv,
        grad_qkv_b,
        grad_out_w,
        grad_bias,
        grad_up,
        grad_up_b,
        grad_down,
    ) = lax.psum(
        (
            grad_gain_one,
            grad_shift_one,
            grad_gain_two,
            grad_shift_two,
            grad_qkv,
            grad_qkv_b,
            grad_out_w,
            grad_bias,
            grad_up,
            grad_up_b,
            grad_down,
        ),
        "rep",
    )
    return (
        outputs,
        input_grad,
        grad_gain_one,
        grad_shift_one,
        grad_gain_two,
        grad_shift_two,
        grad_qkv,
        grad_qkv_b,
        grad_out_w,
        grad_bias,
        grad_up,
        grad_up_b,
        grad_down,
        grad_bias,
    )


AXES = ("rep", "shard")
Z, Y, C, X = 4, 2, 2, 2
BLOCKS = 8


def moves(target):
    pairs = []
    for z in range(Z):
        for y in range(Y):
            for c in range(C):
                for x in range(X):
                    to = target(z, y, c, x)
                    if to is not None:
                        to_z, to_y, to_c, to_x = to
                        source = ((z * Y + y) * C + c) * X + x
                        pairs.append((source, ((to_z * Y + to_y) * C + to_c) * X + to_x))
    return pairs


TO_CORE = moves(lambda z, y, c, x: (z, y, 1 - c, x))
TO_X = moves(lambda z, y, c, x: (z, y, c, 1 - x))
TO_Y = moves(lambda z, y, c, x: (z, 1 - y, c, x))
TO_XY = moves(lambda z, y, c, x: (z, 1 - y, c, 1 - x))
INWARD = moves(lambda z, y, c, x: {0: (1, y, c, x), 3: (2, y, c, x)}.get(z))
MIDDLE = moves(lambda z, y, c, x: {1: (2, y, c, x), 2: (1, y, c, x)}.get(z))
OUTWARD = moves(lambda z, y, c, x: {1: (0, y, c, x), 2: (3, y, c, x)}.get(z))


def send(value, pairs):
    return lax.ppermute(value, AXES, pairs)


def project_kernel(rows_ref, weight_ref, bias_ref, keep_ref, up_ref, down_ref, out_ref):
    width = weight_ref.shape[1]
    value = jnp.dot(rows_ref[...], weight_ref[...], preferred_element_type=jnp.float32)
    value = value + bias_ref[...]
    half = ROT // 2
    turned = (
        value * keep_ref[...]
        + pltpu.roll(value, width - half, 1) * up_ref[...]
        + pltpu.roll(value, half, 1) * down_ref[...]
    )
    out_ref[...] = turned.astype(jnp.bfloat16)


def project(rows, weight, bias, keep, up, down, length):
    count, width = rows.shape[0], weight.shape[1]
    whole = lambda i: (0, 0)
    return pl.pallas_call(
        project_kernel,
        grid=(count // length,),
        in_specs=[
            pl.BlockSpec((length, rows.shape[1]), lambda i: (i, 0)),
            pl.BlockSpec(weight.shape, whole),
            pl.BlockSpec((1, width), whole),
            pl.BlockSpec((length, width), whole),
            pl.BlockSpec((length, width), whole),
            pl.BlockSpec((length, width), whole),
        ],
        out_specs=pl.BlockSpec((length, width), lambda i: (i, 0)),
        out_shape=jax.ShapeDtypeStruct((count, width), jnp.bfloat16),
        cost_estimate=pl.CostEstimate(
            flops=2 * count * width * rows.shape[1],
            bytes_accessed=2 * (rows.size + weight.size + count * width),
            transcendentals=0,
        ),
    )(rows, weight, bias, keep, up, down)


def dot_tt(a, b, dims):
    return lax.dot_general(a, b, ((dims[:1], dims[1:]), ((), ())), preferred_element_type=jnp.float32)


def attention_kernel(
    query_ref, keys_ref, values_ref, grad_ref, keep_ref, up_ref, down_ref,
    attended_ref, grad_query_ref, grad_keys_ref, grad_values_ref, sums_ref,
):
    length, width = query_ref.shape
    query, keys, values, grad = query_ref[...], keys_ref[...], values_ref[...], grad_ref[...]
    lane = lax.broadcasted_iota(jnp.int32, (length, width), 1)
    causal = lax.broadcasted_iota(jnp.int32, (length, length), 0) >= lax.broadcasted_iota(
        jnp.int32, (length, length), 1
    )
    scale = 1.0 / math.sqrt(HD)
    zero = jnp.zeros_like(query)
    found = []
    for head in range(width // HD):
        mine = (lane >= head * HD) & (lane < (head + 1) * HD)
        scores = dot_tt(jnp.where(mine, query, zero), keys, (1, 1)) * scale
        scores = jnp.where(causal, scores, -jnp.inf)
        row_max = jnp.max(scores, -1, keepdims=True)
        log_total = row_max + jnp.log(jnp.sum(jnp.exp(scores - row_max), -1, keepdims=True))
        probs = jnp.exp(scores - log_total)
        probs_b = probs.astype(jnp.bfloat16)
        attended = jnp.dot(probs_b, values, preferred_element_type=jnp.float32)
        grad_values = dot_tt(probs_b, grad, (0, 0))
        grad_probs = dot_tt(jnp.where(mine, grad, zero), values, (1, 1))
        inner = jnp.sum(probs * grad_probs, -1, keepdims=True)
        grad_scores = (probs * (grad_probs - inner) * scale).astype(jnp.bfloat16)
        grad_query = jnp.dot(grad_scores, keys, preferred_element_type=jnp.float32)
        grad_keys = dot_tt(grad_scores, query, (0, 0))
        new = (attended, grad_query, grad_keys, grad_values)
        found = new if not found else tuple(jnp.where(mine, n, o) for n, o in zip(new, found))
    attended, grad_query, grad_keys, grad_values = found
    half = ROT // 2

    def back(value):
        return (
            value * keep_ref[...]
            - pltpu.roll(value, width - half, 1) * up_ref[...]
            - pltpu.roll(value, half, 1) * down_ref[...]
        )

    grad_query, grad_keys = back(grad_query), back(grad_keys)
    attended_ref[...] = attended.astype(jnp.bfloat16)
    grad_query_ref[...] = grad_query.astype(jnp.bfloat16)
    grad_keys_ref[...] = grad_keys.astype(jnp.bfloat16)
    grad_values_ref[...] = grad_values.astype(jnp.bfloat16)


def attention(query, keys, values, grad, keep, up, down, length):
    count, width = query.shape
    block = pl.BlockSpec((length, width), lambda i: (i, 0))
    table = pl.BlockSpec((length, width), lambda i: (0, 0))
    shape = jax.ShapeDtypeStruct((count, width), jnp.bfloat16)

    def kernel(*refs):
        attention_kernel(*refs, None)

    return pl.pallas_call(
        kernel,
        grid=(count // length,),
        in_specs=[block] * 4 + [table] * 3,
        out_specs=[block] * 4,
        out_shape=[shape] * 4,
        cost_estimate=pl.CostEstimate(
            flops=12 * count * length * width * 2,
            bytes_accessed=16 * count * width,
            transcendentals=4 * count * length,
        ),
    )(query, keys, values, grad, keep, up, down)


def across(value, middle):
    first = send(value, INWARD)
    value = (value.astype(jnp.float32) + first.astype(jnp.float32)).astype(value.dtype)
    second = send(value, MIDDLE)
    value = (value.astype(jnp.float32) + second.astype(jnp.float32)).astype(value.dtype)
    return jnp.where(middle, value, send(value, OUTWARD))


def fast_body(
    inputs,
    attn_gain,
    attn_shift,
    feed_gain,
    feed_shift,
    qkv_weight,
    qkv_bias,
    out_weight,
    out_bias,
    up_weight,
    up_bias,
    down_weight,
    down_bias,
    cotangent,
):
    f32, bf16 = jnp.float32, jnp.bfloat16
    length = inputs.shape[0]
    rep, x = lax.axis_index("rep"), lax.axis_index("shard")
    z, y, c = rep // 4, rep // 2 % 2, rep % 2
    part = y * 2 + c
    on_low = x == 0
    middle = (z == 1) | (z == 2)
    hidden_own = up_weight.shape[1] // 4
    wide = 2 * HD

    vectors = jnp.stack([attn_gain, attn_shift, feed_gain, feed_shift, out_bias, down_bias])
    other = send(vectors, TO_X)
    vectors = jnp.where(
        on_low,
        jnp.concatenate([vectors, other], 1),
        jnp.concatenate([other, vectors], 1),
    ).astype(f32)
    gain_one, shift_one, gain_two, shift_two, out_bias_all, down_bias_all = vectors

    def gather(rows):
        four = jnp.concatenate([rows, send(rows, TO_Y), send(rows, TO_X), send(rows, TO_XY)], 0)
        return jnp.concatenate([four, send(four, TO_CORE)], 0)

    rows_all = gather(inputs)
    cot = gather(cotangent)

    def other_order(rows):
        blocks = rows.reshape(2, 2, 2 * length, rows.shape[1])
        return jnp.stack([blocks[:, 1], blocks[:, 0]], 1).reshape(rows.shape)

    out_mine = lax.dynamic_slice(out_weight, (512 * x + wide * part, 0), (wide, out_weight.shape[1]))
    out_theirs = lax.dynamic_slice(
        out_weight, (512 * (1 - x) + wide * part, 0), (wide, out_weight.shape[1])
    )
    out_other = send(out_theirs, TO_X)
    out_rows = jnp.where(
        on_low,
        jnp.concatenate([out_mine, out_other], 1),
        jnp.concatenate([out_other, out_mine], 1),
    )

    up_own = lax.dynamic_slice(up_weight, (0, hidden_own * part), (D, hidden_own))
    down_own = lax.dynamic_slice(down_weight, (hidden_own * part, 0), (hidden_own, D))
    up_bias_own = lax.dynamic_slice(up_bias, (hidden_own * part,), (hidden_own,)).astype(f32)
    qkv_own = lax.dynamic_slice(
        qkv_weight.reshape(D, 3, 4, wide), (0, 0, part, 0), (D, 3, 1, wide)
    ).reshape(D, 3 * wide)
    qkv_bias_own = (
        lax.dynamic_slice(qkv_bias.reshape(3, 4, wide), (0, part, 0), (3, 1, wide))
        .reshape(1, 3 * wide)
        .astype(f32)
    )

    resid = rows_all.astype(f32)
    row_mean = jnp.mean(resid, -1, keepdims=True)
    centered = resid - row_mean
    inv_std = lax.rsqrt(jnp.mean(centered * centered, -1, keepdims=True) + norm_eps)
    normed = centered * inv_std
    attn_in = (normed * gain_one + shift_one).astype(bf16)
    feed_in = (normed * gain_two + shift_two).astype(bf16)

    preact = jnp.dot(feed_in, up_own, preferred_element_type=f32) + up_bias_own
    normal_cdf = 0.5 * (1.0 + lax.erf(preact * (1.0 / math.sqrt(2.0))))
    hidden = (preact * normal_cdf).astype(bf16)
    slope = normal_cdf + preact * jnp.exp(-0.5 * preact * preact) * (1.0 / math.sqrt(2.0 * math.pi))
    grad_preact = jnp.dot(cot, down_own.T, preferred_element_type=f32) * slope
    grad_preact_b = grad_preact.astype(bf16)
    grad_up_b = jnp.sum(grad_preact, 0)
    grad_down = jnp.dot(hidden.T, cot, preferred_element_type=f32).astype(bf16)
    grad_up = jnp.dot(feed_in.T, grad_preact_b, preferred_element_type=f32).astype(bf16)

    cosine, sine_table = rotary_tables(length, ROT)
    ones = jnp.ones((length, HD - ROT), f32)
    zeros = jnp.zeros((length, ROT // 2), f32)
    rest = jnp.zeros((length, HD - ROT), f32)
    keep = jnp.tile(jnp.concatenate([cosine, cosine, ones], 1), (1, 2))
    up = jnp.tile(jnp.concatenate([-sine_table, zeros, rest], 1), (1, 2))
    down = jnp.tile(jnp.concatenate([zeros, sine_table, rest], 1), (1, 2))

    def for_columns(table, still):
        second = jnp.where(on_low, table, still)
        return jnp.concatenate([table, second, second], 1)

    projected = project(
        attn_in,
        qkv_own,
        qkv_bias_own,
        for_columns(keep, 1.0),
        for_columns(up, 0.0),
        for_columns(down, 0.0),
        length,
    )
    first, passed, third = (projected[:, i * wide : (i + 1) * wide] for i in range(3))
    taken = other_order(send(passed, TO_X))
    query = jnp.where(on_low, first, taken)
    keys = jnp.where(on_low, third, first)
    values = jnp.where(on_low, taken, third)
    grad_attended = jnp.dot(cot, out_rows.T, preferred_element_type=f32).astype(bf16)
    attended, grad_query, grad_keys, grad_values = attention(
        query, keys, values, grad_attended, keep, up, down, length
    )
    attended_other = other_order(send(attended, TO_X))
    grad_taken = other_order(send(jnp.where(on_low, grad_values, grad_query), TO_X))
    attended_two = jnp.where(
        on_low,
        jnp.concatenate([attended, attended_other], 1),
        jnp.concatenate([attended_other, attended], 1),
    )
    grad_proj = jnp.concatenate(
        [
            jnp.where(on_low, grad_query, grad_keys),
            grad_taken,
            jnp.where(on_low, grad_keys, grad_values),
        ],
        1,
    )
    half_d = D // 2
    cot_columns = lax.dynamic_slice(cot, (0, half_d * x), (cot.shape[0], half_d))
    grad_out_w = jnp.dot(attended_two.T, cot_columns, preferred_element_type=f32).astype(bf16)
    grad_qkv = jnp.dot(attn_in.T, grad_proj, preferred_element_type=f32).astype(bf16)
    grad_qkv_b = jnp.sum(grad_proj.astype(f32), 0)

    def to_owner(rows):
        for pairs in (TO_CORE, TO_X, TO_Y):
            count = rows.shape[0] // 2
            got = send(rows[count:].astype(bf16), pairs)
            rows = rows[:count] + got.astype(f32)
        return rows

    branches = jnp.dot(hidden, down_own, preferred_element_type=f32) + jnp.dot(
        attended, out_rows, preferred_element_type=f32
    )
    outputs = (
        inputs.astype(f32) + to_owner(branches) + (out_bias_all + down_bias_all)
    ).astype(bf16)

    grad_attn_in = jnp.dot(grad_proj, qkv_own.T, preferred_element_type=f32)
    grad_feed_in = jnp.dot(grad_preact_b, up_own.T, preferred_element_type=f32)
    sums = jnp.stack(
        [
            jnp.sum(grad_attn_in * normed, 0),
            jnp.sum(grad_attn_in, 0),
            jnp.sum(grad_feed_in * normed, 0),
            jnp.sum(grad_feed_in, 0),
            jnp.sum(cotangent.astype(f32), 0),
        ]
    )
    grad_normed = to_owner(grad_attn_in * gain_one + grad_feed_in * gain_two)
    normed_own, inv_std_own = normed[:length], inv_std[:length]
    input_grad = cotangent.astype(f32) + inv_std_own * (
        grad_normed
        - jnp.mean(grad_normed, -1, keepdims=True)
        - normed_own * jnp.mean(grad_normed * normed_own, -1, keepdims=True)
    )

    for pairs in (TO_CORE, TO_X, TO_Y):
        sums = sums + send(sums, pairs)
    small = jnp.concatenate([sums.reshape(-1), grad_up_b, grad_qkv_b])
    small = across(small.reshape(-1, 128), middle).reshape(-1)
    sums = small[: 5 * D].reshape(5, D)
    own = small[5 * D :].reshape(1, -1)
    own = jnp.concatenate([own, send(own, TO_Y)], 0)
    own = jnp.concatenate([own, send(own, TO_CORE)], 0)
    order = jnp.stack([part, part ^ 2, part ^ 1, part ^ 3])
    own = jnp.stack(
        [sum(jnp.where(order[i] == p, own[i], 0.0) for i in range(4)) for p in range(4)]
    )
    grad_up_b = own[:, :hidden_own].reshape(-1)
    grad_qkv_b = own[:, hidden_own:].reshape(4, 3, wide).transpose(1, 0, 2).reshape(-1)
    halves = lax.dynamic_slice(sums, (0, half_d * x), (5, half_d))

    def place(out, value, starts):
        total = across(value, middle)
        over_y = send(total, TO_Y)
        for piece, flip in (
            (total, 0),
            (over_y, 2),
            (send(total, TO_CORE), 1),
            (send(over_y, TO_CORE), 3),
        ):
            out = starts(out, piece.astype(f32), part ^ flip)
        return out

    def in_rows(first_row):
        return lambda out, piece, p: lax.dynamic_update_slice(
            out, piece, (hidden_own * p + first_row, 0)
        )

    def in_columns(first_row):
        return lambda out, piece, p: lax.dynamic_update_slice(
            out, piece, (first_row, hidden_own * p)
        )

    def in_heads(out, piece, p):
        for side in range(2):
            out = lax.dynamic_update_slice(
                out, piece[side * wide : (side + 1) * wide], (512 * side + wide * p, 0)
            )
        return out

    def in_thirds(first_row):
        def starts(out, piece, p):
            for i in range(3):
                out = lax.dynamic_update_slice(
                    out, piece[:, i * wide : (i + 1) * wide], (first_row, 512 * i + wide * p)
                )
            return out

        return starts

    down_out = jnp.zeros(down_weight.shape, f32)
    for i in range(4):
        size = hidden_own // 4
        down_out = place(down_out, grad_down[i * size : (i + 1) * size], in_rows(i * size))
    up_out = jnp.zeros(up_weight.shape, f32)
    for i in range(4):
        size = D // 4
        up_out = place(up_out, grad_up[i * size : (i + 1) * size], in_columns(i * size))
    out_out = place(jnp.zeros(out_weight.shape, f32), grad_out_w, in_heads)
    qkv_out = jnp.zeros(qkv_weight.shape, f32)
    for i in range(4):
        size = D // 4
        qkv_out = place(qkv_out, grad_qkv[i * size : (i + 1) * size], in_thirds(i * size))

    return (
        outputs,
        input_grad,
        halves[0],
        halves[1],
        halves[2],
        halves[3],
        qkv_out,
        grad_qkv_b,
        out_out,
        halves[4],
        up_out,
        grad_up_b,
        down_out,
        halves[4],
    )


def choose_body(mesh):
    known = {"rep": Z * Y * C, "shard": X}
    return fast_body if dict(mesh.shape) == known else general_body


def solution(mesh):
    return jax.shard_map(
        choose_body(mesh),
        mesh=mesh,
        in_specs=(
            P(("rep", "shard"), None),
            P("shard"),
            P("shard"),
            P("shard"),
            P("shard"),
            P(None, "shard"),
            P("shard"),
            P(None, "shard"),
            P("shard"),
            P(None, "shard"),
            P("shard"),
            P("shard", None),
            P("shard"),
            P(("rep", "shard"), None),
        ),
        out_specs=(
            P(("rep", "shard"), None),
            P(("rep", "shard"), None),
            P("shard"),
            P("shard"),
            P("shard"),
            P("shard"),
            P(None, "shard"),
            P("shard"),
            P(None, "shard"),
            P("shard"),
            P(None, "shard"),
            P("shard"),
            P("shard", None),
            P("shard"),
        ),
        check_vma=False,
    )
```

```python
import math

import jax
import jax.numpy as jnp
import numpy as np
from jax import lax
from jax.experimental import pallas as pl
from jax.experimental.pallas import tpu as pltpu
from jax.sharding import PartitionSpec as P

D = 1024
H = 16
HD = 64
ROT = 16


norm_eps = 1e-05
base_freq = 10000.0


def rotary_tables(length, rotary_dims):
    half_dims = rotary_dims // 2
    positions = jnp.arange(length).astype(jnp.float32)
    inverse = jnp.exp(
        jnp.arange(half_dims).astype(jnp.float32) * (-2.0 * math.log(base_freq) / rotary_dims)
    )
    angles = positions[:, None] * inverse[None, :]
    return (jnp.cos(angles), jnp.sin(angles))


def rotate(values, cosine, sine_table, rotary_dims, direction):
    half_dims = rotary_dims // 2
    lower_half = values[..., :half_dims]
    upper_half = values[..., half_dims:rotary_dims]
    cosine_row = cosine[:, None, :]
    sine_row = sine_table[:, None, :] * direction
    return jnp.concatenate(
        [
            lower_half * cosine_row - upper_half * sine_row,
            upper_half * cosine_row + lower_half * sine_row,
            values[..., rotary_dims:],
        ],
        axis=-1,
    )


def gelu_slope(preact):
    normal_cdf = 0.5 * (1.0 + jax.scipy.special.erf(preact * (1.0 / math.sqrt(2.0))))
    return normal_cdf + preact * jnp.exp(-0.5 * preact * preact) * (1.0 / math.sqrt(2.0 * math.pi))


def general_body(
    inputs,
    attn_gain,
    attn_shift,
    feed_gain,
    feed_shift,
    qkv_weight,
    qkv_bias,
    out_weight,
    out_bias,
    up_weight,
    up_bias,
    down_weight,
    down_bias,
    cotangent,
):
    (
        gain_one,
        shift_one,
        gain_two,
        shift_two,
        out_bias_all,
        down_bias_all,
        qkv_all,
        qkv_bias_all,
        out_all,
    ) = (
        lax.all_gather(attn_gain, "shard", axis=0, tiled=True),
        lax.all_gather(attn_shift, "shard", axis=0, tiled=True),
        lax.all_gather(feed_gain, "shard", axis=0, tiled=True),
        lax.all_gather(feed_shift, "shard", axis=0, tiled=True),
        lax.all_gather(out_bias, "shard", axis=0, tiled=True),
        lax.all_gather(down_bias, "shard", axis=0, tiled=True),
        lax.all_gather(qkv_weight, "shard", axis=1, tiled=True),
        lax.all_gather(qkv_bias, "shard", axis=0, tiled=True),
        lax.all_gather(out_weight, "shard", axis=1, tiled=True),
    )
    gain_one = gain_one.astype(jnp.float32)
    gain_two = gain_two.astype(jnp.float32)
    length = inputs.shape[0]
    resid = inputs.astype(jnp.float32)
    row_mean = jnp.mean(resid, -1, keepdims=True)
    centered = resid - row_mean
    inv_std = lax.rsqrt(jnp.mean(centered * centered, -1, keepdims=True) + norm_eps)
    normed = centered * inv_std
    attn_in = (normed * gain_one + shift_one.astype(jnp.float32)).astype(jnp.bfloat16)
    feed_in = (normed * gain_two + shift_two.astype(jnp.float32)).astype(jnp.bfloat16)
    projected = jnp.dot(attn_in, qkv_all, preferred_element_type=jnp.float32) + qkv_bias_all.astype(
        jnp.float32
    )
    projected = projected.reshape(length, 3, H, HD)
    cosine, sine_table = rotary_tables(length, ROT)
    query_rot = rotate(projected[:, 0], cosine, sine_table, ROT, 1.0).astype(jnp.bfloat16)
    keys_rot = rotate(projected[:, 1], cosine, sine_table, ROT, 1.0).astype(jnp.bfloat16)
    values_b = projected[:, 2].astype(jnp.bfloat16)
    score_scale = 1.0 / math.sqrt(HD)
    row_block = min(512, length)
    block_count = length // row_block
    key_positions = jnp.arange(length)

    def block_scores(row_start, q_rows):
        scores = (
            jnp.einsum("qhd,khd->hqk", q_rows, keys_rot, preferred_element_type=jnp.float32)
            * score_scale
        )
        causal = (row_start + jnp.arange(row_block))[:, None] >= key_positions[None, :]
        return jnp.where(causal[None], scores, -jnp.inf)

    def forward_block(block_index):
        row_start = block_index * row_block
        scores = block_scores(row_start, query_rot)
        row_max = jnp.max(scores, -1, keepdims=True)
        log_total = row_max + jnp.log(jnp.sum(jnp.exp(scores - row_max), -1, keepdims=True))
        attn_probs = jnp.exp(scores - log_total).astype(jnp.bfloat16)
        block_out = jnp.einsum(
            "hqk,khd->qhd", attn_probs, values_b, preferred_element_type=jnp.float32
        )
        return (block_out.astype(jnp.bfloat16), log_total)

    attended, log_totals = lax.map(forward_block, jnp.arange(block_count))
    attended = attended.reshape(length, D)
    attn_out = jnp.dot(attended, out_all, preferred_element_type=jnp.float32) + out_bias_all.astype(
        jnp.float32
    )
    group_in = lax.all_gather(feed_in, "shard", axis=0, tiled=True)
    preact = jnp.dot(group_in, up_weight, preferred_element_type=jnp.float32) + up_bias.astype(
        jnp.float32
    )
    hidden = jax.nn.gelu(preact, approximate=False).astype(jnp.bfloat16)
    rows_in = hidden
    feed_out = lax.psum_scatter(
        jnp.dot(rows_in, down_weight, preferred_element_type=jnp.float32),
        "shard",
        scatter_dimension=0,
        tiled=True,
    ) + down_bias_all.astype(jnp.float32)
    outputs = (resid + attn_out + feed_out).astype(jnp.bfloat16)
    grad_top = cotangent.astype(jnp.float32)
    attn_group, attended_group, out_back = (
        lax.all_gather(attn_in, "shard", axis=0, tiled=True),
        lax.all_gather(attended, "shard", axis=0, tiled=True),
        lax.all_gather(out_weight, "shard", axis=1, tiled=True),
    )
    grad_cols = lax.all_to_all(cotangent, "shard", split_axis=1, concat_axis=0, tiled=True)
    grad_bias = jnp.sum(grad_cols.astype(jnp.float32), 0)
    grad_out_w = jnp.dot(attended_group.T, grad_cols, preferred_element_type=jnp.float32)
    grad_attended = (
        jnp.dot(cotangent, out_back.T, preferred_element_type=jnp.float32)
        .astype(jnp.bfloat16)
        .reshape(length, H, HD)
    )
    group_grad = lax.all_gather(cotangent, "shard", axis=0, tiled=True)
    grad_down = jnp.dot(hidden.T, group_grad, preferred_element_type=jnp.float32)
    grad_preact = jnp.dot(
        group_grad, down_weight.T, preferred_element_type=jnp.float32
    ) * gelu_slope(preact)
    grad_up_b = jnp.sum(grad_preact, 0)
    grad_preact_b = grad_preact.astype(jnp.bfloat16)
    grad_up = jnp.dot(group_in.T, grad_preact_b, preferred_element_type=jnp.float32)
    rows_in = grad_preact_b
    grad_feed_in = lax.psum_scatter(
        jnp.dot(rows_in, up_weight.T, preferred_element_type=jnp.float32),
        "shard",
        scatter_dimension=0,
        tiled=True,
    )

    def backward_block(carry, block_index):
        grad_keys, grad_values = carry
        row_start = block_index * row_block
        scores = block_scores(row_start, query_rot)
        probs_f = jnp.exp(scores - log_totals[block_index])
        probs_b = probs_f.astype(jnp.bfloat16)
        grad_values = grad_values + jnp.einsum(
            "hqk,qhd->khd", probs_b, grad_attended, preferred_element_type=jnp.float32
        )
        grad_probs = jnp.einsum(
            "qhd,khd->hqk", grad_attended, values_b, preferred_element_type=jnp.float32
        )
        grad_scores = (
            probs_f * (grad_probs - jnp.sum(probs_f * grad_probs, -1, keepdims=True)) * score_scale
        )
        grad_scores_b = grad_scores.astype(jnp.bfloat16)
        grad_qrot = jnp.einsum(
            "hqk,khd->qhd", grad_scores_b, keys_rot, preferred_element_type=jnp.float32
        )
        grad_keys = grad_keys + jnp.einsum(
            "hqk,qhd->khd", grad_scores_b, query_rot, preferred_element_type=jnp.float32
        )
        return ((grad_keys, grad_values), grad_qrot)

    empty_heads = jnp.zeros((length, H, HD), jnp.float32)
    (grad_krot, grad_values), grad_qrot = lax.scan(
        backward_block, (empty_heads, empty_heads), jnp.arange(block_count)
    )
    grad_qrot = grad_qrot.reshape(length, H, HD)
    grad_query = rotate(grad_qrot, cosine, sine_table, ROT, -1.0)
    grad_keys = rotate(grad_krot, cosine, sine_table, ROT, -1.0)
    grad_proj = jnp.stack([grad_query, grad_keys, grad_values], axis=1).reshape(length, 3 * D)
    grad_qkv_b = jnp.sum(grad_proj, 0)
    grad_proj_b = grad_proj.astype(jnp.bfloat16)
    proj_cols = lax.all_to_all(grad_proj_b, "shard", split_axis=1, concat_axis=0, tiled=True)
    grad_qkv = jnp.dot(attn_group.T, proj_cols, preferred_element_type=jnp.float32)
    rows_in = proj_cols
    grad_attn_in = lax.psum_scatter(
        jnp.dot(rows_in, qkv_weight.T, preferred_element_type=jnp.float32),
        "shard",
        scatter_dimension=0,
        tiled=True,
    )
    grad_gain_one = jnp.sum(grad_attn_in * normed, 0)
    grad_shift_one = jnp.sum(grad_attn_in, 0)
    grad_gain_two = jnp.sum(grad_feed_in * normed, 0)
    grad_shift_two = jnp.sum(grad_feed_in, 0)
    grad_normed = grad_attn_in * gain_one + grad_feed_in * gain_two
    input_grad = grad_top + inv_std * (
        grad_normed
        - jnp.mean(grad_normed, -1, keepdims=True)
        - normed * jnp.mean(grad_normed * normed, -1, keepdims=True)
    )
    grad_qkv_b, grad_gain_one, grad_shift_one, grad_gain_two, grad_shift_two = (
        lax.psum_scatter(grad_qkv_b, "shard", scatter_dimension=0, tiled=True),
        lax.psum_scatter(grad_gain_one, "shard", scatter_dimension=0, tiled=True),
        lax.psum_scatter(grad_shift_one, "shard", scatter_dimension=0, tiled=True),
        lax.psum_scatter(grad_gain_two, "shard", scatter_dimension=0, tiled=True),
        lax.psum_scatter(grad_shift_two, "shard", scatter_dimension=0, tiled=True),
    )
    (
        grad_gain_one,
        grad_shift_one,
        grad_gain_two,
        grad_shift_two,
        grad_qkv,
        grad_qkv_b,
        grad_out_w,
        grad_bias,
        grad_up,
        grad_up_b,
        grad_down,
    ) = lax.psum(
        (
            grad_gain_one,
            grad_shift_one,
            grad_gain_two,
            grad_shift_two,
            grad_qkv,
            grad_qkv_b,
            grad_out_w,
            grad_bias,
            grad_up,
            grad_up_b,
            grad_down,
        ),
        "rep",
    )
    return (
        outputs,
        input_grad,
        grad_gain_one,
        grad_shift_one,
        grad_gain_two,
        grad_shift_two,
        grad_qkv,
        grad_qkv_b,
        grad_out_w,
        grad_bias,
        grad_up,
        grad_up_b,
        grad_down,
        grad_bias,
    )


AXES = ("rep", "shard")
Z, Y, C, X = 4, 2, 2, 2


def moves(target):
    pairs = []
    for z in range(Z):
        for y in range(Y):
            for c in range(C):
                for x in range(X):
                    to = target(z, y, c, x)
                    if to is not None:
                        to_z, to_y, to_c, to_x = to
                        source = ((z * Y + y) * C + c) * X + x
                        pairs.append((source, ((to_z * Y + to_y) * C + to_c) * X + to_x))
    return pairs


TO_CORE = moves(lambda z, y, c, x: (z, y, 1 - c, x))
TO_X = moves(lambda z, y, c, x: (z, y, c, 1 - x))
TO_Y = moves(lambda z, y, c, x: (z, 1 - y, c, x))
TO_XY = moves(lambda z, y, c, x: (z, 1 - y, c, 1 - x))
INWARD = moves(lambda z, y, c, x: {0: (1, y, c, x), 3: (2, y, c, x)}.get(z))
MIDDLE = moves(lambda z, y, c, x: {1: (2, y, c, x), 2: (1, y, c, x)}.get(z))
OUTWARD = moves(lambda z, y, c, x: {1: (0, y, c, x), 2: (3, y, c, x)}.get(z))

WIDE = 2 * HD
BF16, F32 = jnp.bfloat16, jnp.float32


def send(value, pairs):
    return lax.ppermute(value, AXES, pairs)


def dot_over(a, b, dims):
    return lax.dot_general(a, b, ((dims[:1], dims[1:]), ((), ())), preferred_element_type=F32)


def shape_of(shape, dtype):
    return jax.ShapeDtypeStruct(tuple(shape), dtype)


def room(mebibytes):
    return pltpu.CompilerParams(vmem_limit_bytes=mebibytes * 2**20)


VMEM = pl.BlockSpec(memory_space=pltpu.VMEM)
SMEM = pl.BlockSpec(memory_space=pltpu.SMEM)


def cost(flops, moved, transcendentals=0):
    return pl.CostEstimate(flops=int(flops), bytes_accessed=int(moved), transcendentals=int(transcendentals))


def rotary_arrays(length):
    half = ROT // 2
    angles = np.arange(length, dtype=np.float32)[:, None] * np.exp(
        np.arange(half, dtype=np.float32) * np.float32(-2.0 * math.log(base_freq) / ROT)
    )
    keep = np.ones((length, HD), np.float32)
    up = np.zeros((length, HD), np.float32)
    down = np.zeros((length, HD), np.float32)
    keep[:, :half] = keep[:, half:ROT] = np.cos(angles)
    up[:, :half] = -np.sin(angles)
    down[:, half:ROT] = np.sin(angles)
    return [jnp.asarray(np.tile(t, (1, 2))) for t in (keep, up, down)]


def pack_kernel(at_ref, rows_ref, a_ref, b_ref, c_ref, d_ref, e_ref, f_ref, out_ref):
    out_ref[:WIDE, :] = rows_ref[...]
    tail = [r[...][None, :] for r in (a_ref, b_ref, c_ref, d_ref, e_ref, f_ref)]
    tail.append(jnp.zeros((10, out_ref.shape[1]), BF16))
    out_ref[WIDE:, :] = jnp.concatenate(tail, 0)


def pack(at, out_weight, vectors):
    columns = out_weight.shape[1]
    return pl.pallas_call(
        pack_kernel,
        grid_spec=pltpu.PrefetchScalarGridSpec(
            num_scalar_prefetch=1,
            grid=(1,),
            in_specs=[pl.BlockSpec((WIDE, columns), lambda i, s: (4 * (1 - s[1]) + s[0], 0))]
            + [pl.BlockSpec((columns,), lambda i, s: (0,))] * 6,
            out_specs=pl.BlockSpec((WIDE + 16, columns), lambda i, s: (0, 0)),
        ),
        out_shape=shape_of((WIDE + 16, columns), BF16),
        compiler_params=room(4),
        cost_estimate=cost(0, 4 * WIDE * columns),
    )(at, out_weight, *vectors)


def normalise(rows):
    resid = rows.astype(F32)
    row_mean = jnp.mean(resid, -1, keepdims=True)
    centered = resid - row_mean
    inv_std = lax.rsqrt(jnp.mean(centered * centered, -1, keepdims=True) + norm_eps)
    return centered * inv_std


def front_kernel(
    at_ref, low_ref, high_ref, theirs_ref, a_ref, b_ref, c_ref, d_ref, e_ref, f_ref, mine_ref,
    up_ref, up_bias_ref, w0_ref, w1_ref, w2_ref, b0_ref, b1_ref, b2_ref, keep_ref, turn_up_ref, turn_down_ref,
    attn_ref, feed_ref, hidden_ref, slope_ref, first_ref, passed_ref, third_ref, own_ref, out_rows_ref, gains_ref,
    weight_ref,
):
    step = pl.program_id(0)
    on_low = at_ref[1] == 0

    @pl.when(step == 0)
    def _():
        weight_ref[...] = jnp.concatenate([w0_ref[...], w1_ref[...], w2_ref[...]], 1)
        own_ref[...] = weight_ref[...]
        own_rows, their_rows = mine_ref[...], theirs_ref[:WIDE, :]
        out_rows_ref[...] = jnp.concatenate(
            [jnp.where(on_low, own_rows, their_rows), jnp.where(on_low, their_rows, own_rows)], 1
        )
        own = jnp.concatenate([r[...][None, :] for r in (a_ref, b_ref, c_ref, d_ref, e_ref, f_ref)], 0).astype(F32)
        other = theirs_ref[WIDE:, :].astype(F32)[:6]
        gains_ref[...] = jnp.concatenate(
            [
                jnp.concatenate([jnp.where(on_low, own, other), jnp.where(on_low, other, own)], 1),
                jnp.zeros((2, 2 * own.shape[1]), F32),
            ],
            0,
        )

    gains = gains_ref[...]
    normed = normalise(jnp.where(step < 2, low_ref[...], high_ref[...]))
    attn_in = (normed * gains[0:1] + gains[1:2]).astype(BF16)
    feed_in = (normed * gains[2:3] + gains[3:4]).astype(BF16)
    attn_ref[...] = attn_in
    feed_ref[...] = feed_in
    preact = jnp.dot(feed_in, up_ref[...], preferred_element_type=F32) + up_bias_ref[...][None, :].astype(F32)
    normal_cdf = 0.5 * (1.0 + lax.erf(preact * (1.0 / math.sqrt(2.0))))
    hidden_ref[...] = (preact * normal_cdf).astype(BF16)
    slope_ref[...] = normal_cdf + preact * jnp.exp(-0.5 * preact * preact) * (1.0 / math.sqrt(2.0 * math.pi))
    bias = jnp.concatenate([r[...] for r in (b0_ref, b1_ref, b2_ref)], 1).astype(F32)
    value = jnp.dot(attn_in, weight_ref[...], preferred_element_type=F32) + bias
    half = ROT // 2
    length = keep_ref.shape[0]

    def turned(part):
        left = pltpu.roll(part, WIDE - half, 1)
        right = pltpu.roll(part, half, 1)
        pieces = []
        for i in range(part.shape[0] // length):
            rows = slice(i * length, (i + 1) * length)
            pieces.append(
                part[rows] * keep_ref[...] + left[rows] * turn_up_ref[...] + right[rows] * turn_down_ref[...]
            )
        return jnp.concatenate(pieces, 0)

    first_ref[...] = turned(value[:, :WIDE]).astype(BF16)
    passed, third = value[:, WIDE : 2 * WIDE], value[:, 2 * WIDE :]
    passed_ref[...] = jnp.where(on_low, turned(passed), passed).astype(BF16)
    third_ref[...] = jnp.where(on_low, turned(third), third).astype(BF16)


def front(at, low, high, theirs, vectors, out_weight, up_weight, up_bias, qkv_weight, qkv_bias, tables):
    count, rows = 2 * low.shape[0], low.shape[0] // 2
    columns, own = out_weight.shape[1], up_weight.shape[1] // 4
    fixed = lambda i, s: (0, 0)
    block = lambda n: pl.BlockSpec((rows, n), lambda i, s: (i, 0))
    third = lambda n: (lambda i, s: (0, 4 * n + s[0]))
    return pl.pallas_call(
        front_kernel,
        grid_spec=pltpu.PrefetchScalarGridSpec(
            num_scalar_prefetch=1,
            grid=(4,),
            in_specs=[
                pl.BlockSpec((rows, D), lambda i, s: (jnp.minimum(i, 1), 0)),
                pl.BlockSpec((rows, D), lambda i, s: (jnp.maximum(i - 2, 0), 0)),
                pl.BlockSpec(theirs.shape, fixed),
            ]
            + [pl.BlockSpec((columns,), lambda i, s: (0,))] * 6
            + [
                pl.BlockSpec((WIDE, columns), lambda i, s: (4 * s[1] + s[0], 0)),
                pl.BlockSpec((D, own), lambda i, s: (0, s[0])),
                pl.BlockSpec((own,), lambda i, s: (s[0],)),
            ]
            + [pl.BlockSpec((D, WIDE), third(n)) for n in range(3)]
            + [pl.BlockSpec((1, WIDE), third(n)) for n in range(3)]
            + [pl.BlockSpec(tables[0].shape, fixed)] * 3,
            out_specs=[block(D), block(D), block(own), block(own), block(WIDE), block(WIDE), block(WIDE)]
            + [pl.BlockSpec((D, 3 * WIDE), fixed), pl.BlockSpec((WIDE, D), fixed), pl.BlockSpec((8, D), fixed)],
            scratch_shapes=[pltpu.VMEM((D, 3 * WIDE), BF16)],
        ),
        out_shape=[shape_of((count, D), BF16)] * 2
        + [shape_of((count, own), BF16), shape_of((count, own), F32)]
        + [shape_of((count, WIDE), BF16)] * 3
        + [shape_of((D, 3 * WIDE), BF16), shape_of((WIDE, D), BF16), shape_of((8, D), F32)],
        compiler_params=room(28),
        cost_estimate=cost(2 * count * D * (own + 3 * WIDE), 14 * count * D, 2 * count * own),
    )(
        at, low, high, theirs, *vectors, out_weight, up_weight, up_bias,
        qkv_weight, qkv_weight, qkv_weight, qkv_bias, qkv_bias, qkv_bias, *tables,
    )


def down_kernel(hidden_ref, low_ref, high_ref, cot_ref, first_ref, second_ref):
    half, half_d = low_ref.shape[0], low_ref.shape[1] // 2
    cot_ref[:half, :] = low_ref[...]
    cot_ref[half:, :] = high_ref[...]
    first_ref[...] = dot_over(hidden_ref[...], cot_ref[:, :half_d], (0, 0)).astype(BF16)
    second_ref[...] = dot_over(hidden_ref[...], cot_ref[:, half_d:], (0, 0)).astype(BF16)


def grad_down_chunks(hidden, low, high):
    count, own = hidden.shape
    return pl.pallas_call(
        down_kernel,
        in_specs=[VMEM] * 3,
        out_specs=[VMEM] * 3,
        out_shape=[shape_of((count, D), BF16)] + [shape_of((own, D // 2), BF16)] * 2,
        compiler_params=room(10),
        cost_estimate=cost(2 * count * own * D, 6 * count * D),
    )(hidden, low, high)


def attention_kernel(
    at_ref, first_ref, third_ref, taken_ref, grad_ref, keep_ref, up_ref, down_ref, away_ref, here_ref
):
    length, width = keep_ref.shape
    on_low = at_ref[1] == 0
    lane = lax.broadcasted_iota(jnp.int32, (length, width), 1)
    causal = lax.broadcasted_iota(jnp.int32, (length, length), 0) >= lax.broadcasted_iota(
        jnp.int32, (length, length), 1
    )
    scale = 1.0 / math.sqrt(HD)
    half = ROT // 2

    def back(value):
        return (
            value * keep_ref[...]
            - pltpu.roll(value, width - half, 1) * up_ref[...]
            - pltpu.roll(value, half, 1) * down_ref[...]
        )

    for i in range(first_ref.shape[0] // length):
        rows = slice(i * length, (i + 1) * length)
        first, third, taken, grad = first_ref[rows, :], third_ref[rows, :], taken_ref[rows, :], grad_ref[rows, :]
        query = jnp.where(on_low, first, taken)
        keys = jnp.where(on_low, third, first)
        values = jnp.where(on_low, taken, third)
        zero = jnp.zeros_like(query)
        found = []
        for head in range(width // HD):
            mine = (lane >= head * HD) & (lane < (head + 1) * HD)
            scores = dot_over(jnp.where(mine, query, zero), keys, (1, 1)) * scale
            scores = jnp.where(causal, scores, -jnp.inf)
            row_max = jnp.max(scores, -1, keepdims=True)
            log_total = row_max + jnp.log(jnp.sum(jnp.exp(scores - row_max), -1, keepdims=True))
            probs = jnp.exp(scores - log_total)
            probs_b = probs.astype(BF16)
            attended = jnp.dot(probs_b, values, preferred_element_type=F32)
            grad_values = dot_over(probs_b, grad, (0, 0))
            grad_probs = dot_over(jnp.where(mine, grad, zero), values, (1, 1))
            inner = jnp.sum(probs * grad_probs, -1, keepdims=True)
            grad_scores = (probs * (grad_probs - inner) * scale).astype(BF16)
            grad_query = jnp.dot(grad_scores, keys, preferred_element_type=F32)
            grad_keys = dot_over(grad_scores, query, (0, 0))
            new = (attended, grad_query, grad_keys, grad_values)
            found = new if not found else tuple(jnp.where(mine, n, o) for n, o in zip(new, found))
        attended, grad_query, grad_keys, grad_values = found
        grad_query, grad_keys = back(grad_query), back(grad_keys)
        away_ref[rows, :width] = attended.astype(BF16)
        away_ref[rows, width:] = jnp.where(on_low, grad_values, grad_query).astype(BF16)
        here_ref[rows, :width] = jnp.where(on_low, grad_query, grad_keys).astype(BF16)
        here_ref[rows, width:] = jnp.where(on_low, grad_keys, grad_values).astype(BF16)


def swapped(i):
    return i + 1 - 2 * (i % 2)


def attention(at, first, third, taken, grad, tables):
    count, width = first.shape
    length = tables[0].shape[0]
    block = pl.BlockSpec((2 * length, width), lambda i, s: (i, 0))
    other = pl.BlockSpec((2 * length, width), lambda i, s: (swapped(i), 0))
    table = pl.BlockSpec((length, width), lambda i, s: (0, 0))
    out = pl.BlockSpec((2 * length, 2 * width), lambda i, s: (i, 0))
    return pl.pallas_call(
        attention_kernel,
        grid_spec=pltpu.PrefetchScalarGridSpec(
            num_scalar_prefetch=1,
            grid=(count // (2 * length),),
            in_specs=[block, block, other, block] + [table] * 3,
            out_specs=[out, out],
        ),
        out_shape=[shape_of((count, 2 * width), BF16)] * 2,
        compiler_params=room(12),
        cost_estimate=cost(24 * count * length * width, 16 * count * width, 4 * count * length),
    )(at, first, third, taken, grad, *tables)


def group_kernel(
    at_ref, low_ref, high_ref, cotangent_ref, hidden_ref, gp_ref, away_ref, here_ref, other_ref,
    down_ref, up_ref, out_rows_ref, qkv_ref, gains_ref,
    kept_ref, sent_ref, sums_ref, proj_ref, att_ref,
):
    step = pl.program_id(0)
    on_low = at_ref[1] == 0
    gains = gains_ref[...]
    away, here, other = away_ref[...], here_ref[...], other_ref[...]
    attended, attended_other = away[:, :WIDE], other[:, :WIDE]
    proj = jnp.concatenate([here[:, :WIDE], other[:, WIDE:], here[:, WIDE:]], 1)
    proj_ref[...] = proj
    att_ref[...] = jnp.concatenate(
        [jnp.where(on_low, attended, attended_other), jnp.where(on_low, attended_other, attended)], 1
    )
    gp = gp_ref[...]
    branches = jnp.dot(hidden_ref[...], down_ref[...], preferred_element_type=F32) + jnp.dot(
        attended, out_rows_ref[...], preferred_element_type=F32
    )
    grad_attn = dot_over(proj, qkv_ref[...], (1, 1))
    grad_feed = dot_over(gp, up_ref[...], (1, 1))
    normed = normalise(jnp.where(step < 2, low_ref[...], high_ref[...]))
    grad_normed = grad_attn * gains[0:1] + grad_feed * gains[2:3]
    own = gp.shape[1]
    total = lambda v: jnp.sum(v.astype(F32), 0, keepdims=True)
    rows = jnp.concatenate(
        [
            total(grad_attn * normed),
            total(grad_attn),
            total(grad_feed * normed),
            total(grad_feed),
            total(cotangent_ref[...]) * jnp.where(step == 0, 1.0, 0.0),
            jnp.concatenate([total(gp), total(proj), jnp.zeros((1, D - own - 3 * WIDE), F32)], 1),
            jnp.zeros((2, D), F32),
        ],
        0,
    )

    @pl.when(step == 0)
    def _():
        sums_ref[...] = rows

    @pl.when(step > 0)
    def _():
        sums_ref[...] = sums_ref[...] + rows

    @pl.when(step < 2)
    def _():
        kept_ref[0] = branches
        kept_ref[1] = grad_normed

    @pl.when(step >= 2)
    def _():
        sent_ref[0] = branches.astype(BF16)
        sent_ref[1] = grad_normed.astype(BF16)


def group_sums(at, low, high, cotangent, hidden, gp, away, here, other, down_weight, up_weight, out_rows, qkv_own, gains):
    count, own = hidden.shape
    rows = count // 4
    fixed = lambda i, s: (0, 0)
    block = lambda n: pl.BlockSpec((rows, n), lambda i, s: (i, 0))
    return pl.pallas_call(
        group_kernel,
        grid_spec=pltpu.PrefetchScalarGridSpec(
            num_scalar_prefetch=1,
            grid=(4,),
            in_specs=[
                pl.BlockSpec((rows, D), lambda i, s: (jnp.minimum(i, 1), 0)),
                pl.BlockSpec((rows, D), lambda i, s: (jnp.maximum(i - 2, 0), 0)),
                pl.BlockSpec(cotangent.shape, fixed),
                block(own),
                block(own),
                block(2 * WIDE),
                block(2 * WIDE),
                pl.BlockSpec((rows, 2 * WIDE), lambda i, s: (swapped(i), 0)),
                pl.BlockSpec((own, D), lambda i, s: (s[0], 0)),
                pl.BlockSpec((D, own), lambda i, s: (0, s[0])),
                pl.BlockSpec(out_rows.shape, fixed),
                pl.BlockSpec(qkv_own.shape, fixed),
                pl.BlockSpec(gains.shape, fixed),
            ],
            out_specs=[
                pl.BlockSpec((2, rows, D), lambda i, s: (0, jnp.minimum(i, 1), 0)),
                pl.BlockSpec((2, rows, D), lambda i, s: (0, jnp.maximum(i - 2, 0), 0)),
                pl.BlockSpec((8, D), fixed),
                block(3 * WIDE),
                block(2 * WIDE),
            ],
        ),
        out_shape=[
            shape_of((2, count // 2, D), F32),
            shape_of((2, count // 2, D), BF16),
            shape_of((8, D), F32),
            shape_of((count, 3 * WIDE), BF16),
            shape_of((count, 2 * WIDE), BF16),
        ],
        compiler_params=room(28),
        cost_estimate=cost(2 * count * D * (2 * own + 4 * WIDE), 20 * count * D),
    )(at, low, high, cotangent, hidden, gp, away, here, other, down_weight, up_weight, out_rows, qkv_own, gains)


def mixed_kernel(at_ref, rows_ref, proj_ref, att_ref, cot_ref, *refs):
    out_ref = refs[-1]
    out_ref[: 4 * WIDE, : 3 * WIDE] = dot_over(rows_ref[...], proj_ref[...], (0, 0)).astype(BF16)
    heads = dot_over(att_ref[...], cot_ref[...], (0, 0)).astype(BF16)
    out_ref[: 2 * WIDE, 3 * WIDE :] = heads[:, :WIDE]
    out_ref[2 * WIDE : 4 * WIDE, 3 * WIDE :] = heads[:, WIDE:]
    if len(refs) > 1:
        sums, other = refs[0][...], refs[1][...]
        row = lax.broadcasted_iota(jnp.int32, sums.shape, 0)
        sums = jnp.where(row < 5, sums + other, sums).astype(BF16)
        out_ref[4 * WIDE :, :] = jnp.concatenate([sums[:, : D // 2], sums[:, D // 2 :]], 0)


def mixed(at, half, rows, proj, att, cot, small):
    count = rows.shape[0]
    fixed = lambda i, s: (0, 0)
    tall = 4 * WIDE + (16 if small else 0)
    return pl.pallas_call(
        mixed_kernel,
        grid_spec=pltpu.PrefetchScalarGridSpec(
            num_scalar_prefetch=1,
            grid=(1,),
            in_specs=[
                pl.BlockSpec((count, 4 * WIDE), lambda i, s: (0, half)),
                pl.BlockSpec(proj.shape, fixed),
                pl.BlockSpec(att.shape, fixed),
                pl.BlockSpec((count, 2 * WIDE), lambda i, s: (0, 2 * s[1] + half)),
            ]
            + [pl.BlockSpec((8, D), fixed)] * len(small),
            out_specs=pl.BlockSpec((tall, 4 * WIDE), fixed),
        ),
        out_shape=shape_of((tall, 4 * WIDE), BF16),
        compiler_params=room(12),
        cost_estimate=cost(2 * count * 16 * WIDE * WIDE, 4 * count * D),
    )(at, rows, proj, att, cot, *small)


def turn(at, middle_at, grad, from_z, first, from_middle, following, carried):
    outs = []
    given = dict(grad=grad, from_z=from_z, first=first, from_middle=from_middle, following=following, carried=carried)
    names = [n for n, v in given.items() if v is not None]
    if grad is not None:
        outs.append(("first", grad.shape))
    if first is not None or following is not None:
        outs.append(("next", (following if following is not None else first).shape))
    if carried is not None:
        outs.append(("total", (512, 512) if carried.shape[0] < 528 or following is not None or grad is not None else carried.shape))

    def kernel(at_ref, *refs):
        values = dict(zip(names, refs))
        results = dict(zip([n for n, _ in outs], refs[len(names) :]))
        middle = at_ref[middle_at] == 1
        if "first" in results:
            results["first"][...] = values["grad"][...] + values["from_z"][...]
        if "next" in results:
            out = results["next"]
            if "first" in values:
                tall = values["first"].shape[0]
                summed = values["first"][...] + values["from_middle"][...]
                if "following" in values:
                    out[:tall, :] = jnp.where(middle, summed, values["following"][:tall, :])
                    if out.shape[0] > tall:
                        out[tall:, :] = values["following"][tall:, :]
                else:
                    out[...] = summed
            else:
                out[...] = values["following"][...]
        if "total" in results:
            tall = results["total"].shape[0]
            results["total"][...] = jnp.where(middle, values["carried"][:tall, :], values["from_z"][:tall, :])

    made = pl.pallas_call(
        kernel,
        in_specs=[SMEM] + [VMEM] * len(names),
        out_specs=[VMEM] * len(outs),
        out_shape=[shape_of(s, BF16) for _, s in outs],
        compiler_params=room(6),
        cost_estimate=cost(len(names) * 2**18, (len(names) + len(outs)) * 2**19),
    )(at, *[given[n] for n in names])
    return dict(zip([n for n, _ in outs], made))


def place(at, pieces, into, shapes, copies):
    count = len(shapes)
    each = len(copies(0))
    tall = 4 * WIDE

    def kernel(at_ref, *refs):
        piece_refs = refs[:4]
        out_refs = refs[4 + (count if into else 0) :][:count]
        wide_ref, sems = refs[-2:]
        started = []
        for i in range(4):
            wide_ref[i] = piece_refs[i][:tall, :].astype(F32)
            for n, (which, at, part) in enumerate(copies(at_ref[3 + i])):
                copy = pltpu.make_async_copy(wide_ref.at[i].at[part], out_refs[which].at[at], sems.at[i * each + n])
                copy.start()
                started.append(copy)
        for copy in started:
            copy.wait()

    any_space = pl.BlockSpec(memory_space=pl.ANY)
    return pl.pallas_call(
        kernel,
        in_specs=[SMEM] + [VMEM] * 4 + [any_space] * len(into or ()),
        out_specs=[any_space] * count,
        scratch_shapes=[pltpu.VMEM((4, tall, tall), F32), pltpu.SemaphoreType.DMA((4 * each,))],
        out_shape=[shape_of(s, F32) for s in shapes],
        compiler_params=room(8),
        input_output_aliases={5 + k: k for k in range(count)} if into else {},
        cost_estimate=cost(0, 24 * tall * tall),
    )(at, *pieces, *(into or ()))


def at_blocks(first, size):
    return pl.ds(pl.multiple_of(first, size), size)


def small_kernel(at_ref, a_ref, b_ref, c_ref, d_ref, g1, s1, g2, s2, ob, up_ref, qkv_ref):
    on_low = at_ref[1] == 0
    parts = [r[...].astype(F32) for r in (a_ref, b_ref, c_ref, d_ref)]
    sums = (parts[0] + parts[1]) + (parts[2] + parts[3])
    sums = jnp.where(on_low, sums[:8], sums[8:])
    for row, ref in enumerate((g1, s1, g2, s2, ob)):
        ref[...] = sums[row : row + 1]
    for i, part in enumerate(parts):
        p = at_ref[3 + i]
        up_ref[pl.ds(p, 1), :] = part[5:6]
        for n in range(3):
            qkv_ref[pl.ds(4 * n + p, 1), :] = part[13:14, n * WIDE : (n + 1) * WIDE]


def small_outputs(at, pieces):
    fixed = lambda i, s: (0, 0)
    half_d = D // 2
    return pl.pallas_call(
        small_kernel,
        grid_spec=pltpu.PrefetchScalarGridSpec(
            num_scalar_prefetch=1,
            grid=(1,),
            in_specs=[pl.BlockSpec((16, half_d), lambda i, s: (32, 0))] * 4,
            out_specs=[pl.BlockSpec((1, half_d), fixed)] * 5
            + [pl.BlockSpec((4, half_d), fixed), pl.BlockSpec((12, WIDE), fixed)],
        ),
        compiler_params=room(2),
        out_shape=[shape_of((1, half_d), F32)] * 5 + [shape_of((4, half_d), F32), shape_of((12, WIDE), F32)],
    )(at, *pieces)


def fast_body(
    inputs,
    attn_gain,
    attn_shift,
    feed_gain,
    feed_shift,
    qkv_weight,
    qkv_bias,
    out_weight,
    out_bias,
    up_weight,
    up_bias,
    down_weight,
    down_bias,
    cotangent,
):
    length = inputs.shape[0]
    rep, x = lax.axis_index("rep"), lax.axis_index("shard")
    z, y, c = rep // 4, rep // 2 % 2, rep % 2
    part = y * 2 + c
    middle = ((z == 1) | (z == 2)).astype(jnp.int32)
    at = jnp.stack([part, x, middle, part, part ^ 2, part ^ 1, part ^ 3, part]).astype(jnp.int32)
    fence = lax.optimization_barrier
    half_d = D // 2
    tables = rotary_arrays(length)
    vectors = [attn_gain, attn_shift, feed_gain, feed_shift, out_bias, down_bias]

    in_parts = [send(inputs, p) for p in (TO_Y, TO_X, TO_XY)]
    theirs = send(pack(at, out_weight, vectors), TO_X)
    own = up_weight.shape[1] // 4
    down_own = lax.dynamic_slice(down_weight, (own * part, 0), (own, D))
    cot_parts = [send(cotangent, p) for p in (TO_Y, TO_X, TO_XY)]
    in_parts, theirs, down_own = fence((in_parts, theirs, down_own))
    low = jnp.concatenate([inputs, *in_parts], 0)
    high = send(low, TO_CORE)
    attn_in, feed_in, hidden, slope, first, passed, third, qkv_own, out_rows, gains = front(
        at, low, high, theirs, vectors, out_weight, up_weight, up_bias, qkv_weight, qkv_bias.reshape(1, -1), tables
    )
    low_cot = jnp.concatenate([cotangent, *cot_parts], 0)
    cot, chunk0, chunk1 = grad_down_chunks(hidden, low_cot, send(low_cot, TO_CORE))
    taken = send(passed, TO_X)

    env = dict(
        attn_in=attn_in, feed_in=feed_in, hidden=hidden, slope=slope, cot=cot, first=first, third=third,
        taken=taken, qkv_own=qkv_own, out_rows=out_rows, gains=gains, low=low, high=high, down_own=down_own,
    )
    chunks = {0: chunk0, 1: chunk1}

    def fold(kept, sent, pairs):
        kept = kept + send(sent, pairs).astype(F32)
        rows = kept.shape[1] // 2
        return kept[:, :rows], kept[:, rows:].astype(BF16)

    def after(step, env):
        e = dict(env)
        if step == 0:
            gp = dot_over(e["cot"], e.pop("down_own"), (1, 1)) * e.pop("slope")
            e["gp"] = gp.astype(BF16)
            e["grad_attended"] = dot_over(e["cot"], e["out_rows"], (1, 1)).astype(BF16)
        if step == 1:
            chunks[2] = dot_over(e["feed_in"][:, :half_d], e["gp"], (0, 0)).astype(BF16)
            e["away"], e["here"] = attention(
                at, e.pop("first"), e.pop("third"), e.pop("taken"), e.pop("grad_attended"), tables
            )
        if step == 2:
            chunks[3] = dot_over(e.pop("feed_in")[:, half_d:], e["gp"], (0, 0)).astype(BF16)
            e["other"] = send(e["away"], TO_X)
        if step == 3:
            e["kept"], e["sent"], e["sums"], e["proj"], e["att"] = group_sums(
                at, e.pop("low"), e.pop("high"), cotangent, e.pop("hidden"), e.pop("gp"), e.pop("away"),
                e.pop("here"), e.pop("other"), down_weight, up_weight, e.pop("out_rows"), e.pop("qkv_own"), e["gains"],
            )
            chunks[4] = mixed(at, 0, e["attn_in"], e["proj"], e["att"], e["cot"], ())
        if step == 4:
            other = send(e["sums"], TO_X)
            chunks[5] = mixed(
                at, 1, e.pop("attn_in"), e.pop("proj"), e.pop("att"), e.pop("cot"), (e.pop("sums"), other)
            )
            e["kept"], e["sent"] = fold(e["kept"], e["sent"], TO_CORE)
        if step == 5:
            e["kept"], e["sent"] = fold(e["kept"], e["sent"], TO_X)
        if step == 6:
            e["kept"] = e["kept"] + send(e.pop("sent"), TO_Y).astype(F32)
        if step == 7:
            kept, gains = e.pop("kept"), e.pop("gains")
            normed = normalise(inputs)
            resid = inputs.astype(F32)
            centered = resid - jnp.mean(resid, -1, keepdims=True)
            inv_std = lax.rsqrt(jnp.mean(centered * centered, -1, keepdims=True) + norm_eps)
            e["outputs"] = (resid + kept[0] + (gains[4] + gains[5])).astype(BF16)
            grad_normed = kept[1]
            e["input_grad"] = cotangent.astype(F32) + inv_std * (
                grad_normed
                - jnp.mean(grad_normed, -1, keepdims=True)
                - normed * jnp.mean(grad_normed * normed, -1, keepdims=True)
            )
        return e

    count = 6
    operand, one, total, over_y, over_core, over_both = {}, {}, {}, {}, {}, {}
    outs = {}
    operand[0] = chunks[0]

    def finish(k):
        pieces = [total.pop(k), over_y.pop(k), over_core.pop(k), over_both.pop(k)]
        h = k % 2
        rows, columns = pl.ds(h * half_d, half_d), pl.ds(h * half_d, half_d)
        everything = (slice(None), slice(None))
        if k < 2:
            outs["down"] = place(
                at, pieces, outs.get("down"), [down_weight.shape],
                lambda p: [(0, (at_blocks(own * p, own), columns), everything)],
            )
        elif k < 4:
            outs["up"] = place(
                at, pieces, outs.get("up"), [up_weight.shape],
                lambda p: [(0, (rows, at_blocks(own * p, own)), everything)],
            )
        else:
            outs["attn"] = place(
                at, pieces, outs.get("attn"), [qkv_weight.shape, out_weight.shape],
                lambda p: [
                    (0, (rows, at_blocks(half_d * n + WIDE * p, WIDE)), (slice(None), pl.ds(n * WIDE, WIDE)))
                    for n in range(3)
                ]
                + [
                    (
                        1,
                        (at_blocks(half_d * side + WIDE * p, WIDE), pl.ds((2 * h + b) * WIDE, WIDE)),
                        (pl.ds((2 * b + side) * WIDE, WIDE), pl.ds(3 * WIDE, WIDE)),
                    )
                    for b in range(2)
                    for side in range(2)
                ],
            )
        if k == count - 1:
            outs["small"] = small_outputs(at, pieces)

    for step in range(count + 5):
        live = (env, chunks, operand, one, total, over_y, over_core, over_both, outs)
        env, chunks, operand, one, total, over_y, over_core, over_both, outs = fence(live)
        got = {}
        if step < count + 2:
            pairs = (INWARD if step < count else []) + (OUTWARD if step >= 2 else [])
            got["z"] = send(operand[step], pairs)
        if 0 <= step - 1 < count:
            got["m"] = send(one[step - 1], MIDDLE)
        if 0 <= step - 3 < count:
            got["y"] = send(total[step - 3], TO_Y)
            got["c"] = send(total[step - 3], TO_CORE)
        if 0 <= step - 4 < count:
            got["b"] = send(over_y[step - 4], TO_CORE)
        env = after(step, env)
        if 0 <= step - 5 < count:
            finish(step - 5)
        if step < count + 2:
            made = turn(
                at, 2,
                chunks.pop(step) if step < count else None,
                got["z"],
                one.pop(step - 1) if 0 <= step - 1 < count else None,
                got.get("m"),
                chunks.get(step + 1),
                operand.pop(step) if step >= 2 else None,
            )
            if "first" in made:
                one[step] = made["first"]
            if "next" in made:
                operand[step + 1] = made["next"]
            if "total" in made:
                total[step - 2] = made["total"]
        if 0 <= step - 3 < count:
            over_y[step - 3], over_core[step - 3] = got["y"], got["c"]
        if 0 <= step - 4 < count:
            over_both[step - 4] = got["b"]

    g1, s1, g2, s2, ob, up_b, qkv_b = outs["small"]
    flat = lambda v: v.reshape(-1)
    return (
        env["outputs"],
        env["input_grad"],
        flat(g1),
        flat(s1),
        flat(g2),
        flat(s2),
        outs["attn"][0],
        flat(qkv_b),
        outs["attn"][1],
        flat(ob),
        outs["up"][0],
        flat(up_b),
        outs["down"][0],
        flat(ob),
    )


def choose_body(mesh):
    known = {"rep": Z * Y * C, "shard": X}
    return fast_body if dict(mesh.shape) == known else general_body


def solution(mesh):
    return jax.shard_map(
        choose_body(mesh),
        mesh=mesh,
        in_specs=(
            P(("rep", "shard"), None),
            P("shard"),
            P("shard"),
            P("shard"),
            P("shard"),
            P(None, "shard"),
            P("shard"),
            P(None, "shard"),
            P("shard"),
            P(None, "shard"),
            P("shard"),
            P("shard", None),
            P("shard"),
            P(("rep", "shard"), None),
        ),
        out_specs=(
            P(("rep", "shard"), None),
            P(("rep", "shard"), None),
            P("shard"),
            P("shard"),
            P("shard"),
            P("shard"),
            P(None, "shard"),
            P("shard"),
            P(None, "shard"),
            P("shard"),
            P(None, "shard"),
            P("shard"),
            P("shard", None),
            P("shard"),
        ),
        check_vma=False,
    )
```

```python
import math

import jax
import jax.numpy as jnp
import numpy as np
from jax import lax
from jax.experimental import pallas as pl
from jax.experimental.pallas import tpu as pltpu
from jax.sharding import PartitionSpec as P

D = 1024
H = 16
HD = 64
ROT = 16


norm_eps = 1e-05
base_freq = 10000.0


def rotary_tables(length, rotary_dims):
    half_dims = rotary_dims // 2
    positions = jnp.arange(length).astype(jnp.float32)
    inverse = jnp.exp(
        jnp.arange(half_dims).astype(jnp.float32) * (-2.0 * math.log(base_freq) / rotary_dims)
    )
    angles = positions[:, None] * inverse[None, :]
    return (jnp.cos(angles), jnp.sin(angles))


def rotate(values, cosine, sine_table, rotary_dims, direction):
    half_dims = rotary_dims // 2
    lower_half = values[..., :half_dims]
    upper_half = values[..., half_dims:rotary_dims]
    cosine_row = cosine[:, None, :]
    sine_row = sine_table[:, None, :] * direction
    return jnp.concatenate(
        [
            lower_half * cosine_row - upper_half * sine_row,
            upper_half * cosine_row + lower_half * sine_row,
            values[..., rotary_dims:],
        ],
        axis=-1,
    )


def gelu_slope(preact):
    normal_cdf = 0.5 * (1.0 + jax.scipy.special.erf(preact * (1.0 / math.sqrt(2.0))))
    return normal_cdf + preact * jnp.exp(-0.5 * preact * preact) * (1.0 / math.sqrt(2.0 * math.pi))


def general_body(
    inputs,
    attn_gain,
    attn_shift,
    feed_gain,
    feed_shift,
    qkv_weight,
    qkv_bias,
    out_weight,
    out_bias,
    up_weight,
    up_bias,
    down_weight,
    down_bias,
    cotangent,
):
    (
        gain_one,
        shift_one,
        gain_two,
        shift_two,
        out_bias_all,
        down_bias_all,
        qkv_all,
        qkv_bias_all,
        out_all,
    ) = (
        lax.all_gather(attn_gain, "shard", axis=0, tiled=True),
        lax.all_gather(attn_shift, "shard", axis=0, tiled=True),
        lax.all_gather(feed_gain, "shard", axis=0, tiled=True),
        lax.all_gather(feed_shift, "shard", axis=0, tiled=True),
        lax.all_gather(out_bias, "shard", axis=0, tiled=True),
        lax.all_gather(down_bias, "shard", axis=0, tiled=True),
        lax.all_gather(qkv_weight, "shard", axis=1, tiled=True),
        lax.all_gather(qkv_bias, "shard", axis=0, tiled=True),
        lax.all_gather(out_weight, "shard", axis=1, tiled=True),
    )
    gain_one = gain_one.astype(jnp.float32)
    gain_two = gain_two.astype(jnp.float32)
    length = inputs.shape[0]
    resid = inputs.astype(jnp.float32)
    row_mean = jnp.mean(resid, -1, keepdims=True)
    centered = resid - row_mean
    inv_std = lax.rsqrt(jnp.mean(centered * centered, -1, keepdims=True) + norm_eps)
    normed = centered * inv_std
    attn_in = (normed * gain_one + shift_one.astype(jnp.float32)).astype(jnp.bfloat16)
    feed_in = (normed * gain_two + shift_two.astype(jnp.float32)).astype(jnp.bfloat16)
    projected = jnp.dot(attn_in, qkv_all, preferred_element_type=jnp.float32) + qkv_bias_all.astype(
        jnp.float32
    )
    projected = projected.reshape(length, 3, H, HD)
    cosine, sine_table = rotary_tables(length, ROT)
    query_rot = rotate(projected[:, 0], cosine, sine_table, ROT, 1.0).astype(jnp.bfloat16)
    keys_rot = rotate(projected[:, 1], cosine, sine_table, ROT, 1.0).astype(jnp.bfloat16)
    values_b = projected[:, 2].astype(jnp.bfloat16)
    score_scale = 1.0 / math.sqrt(HD)
    row_block = min(512, length)
    block_count = length // row_block
    key_positions = jnp.arange(length)

    def block_scores(row_start, q_rows):
        scores = (
            jnp.einsum("qhd,khd->hqk", q_rows, keys_rot, preferred_element_type=jnp.float32)
            * score_scale
        )
        causal = (row_start + jnp.arange(row_block))[:, None] >= key_positions[None, :]
        return jnp.where(causal[None], scores, -jnp.inf)

    def forward_block(block_index):
        row_start = block_index * row_block
        scores = block_scores(row_start, query_rot)
        row_max = jnp.max(scores, -1, keepdims=True)
        log_total = row_max + jnp.log(jnp.sum(jnp.exp(scores - row_max), -1, keepdims=True))
        attn_probs = jnp.exp(scores - log_total).astype(jnp.bfloat16)
        block_out = jnp.einsum(
            "hqk,khd->qhd", attn_probs, values_b, preferred_element_type=jnp.float32
        )
        return (block_out.astype(jnp.bfloat16), log_total)

    attended, log_totals = lax.map(forward_block, jnp.arange(block_count))
    attended = attended.reshape(length, D)
    attn_out = jnp.dot(attended, out_all, preferred_element_type=jnp.float32) + out_bias_all.astype(
        jnp.float32
    )
    group_in = lax.all_gather(feed_in, "shard", axis=0, tiled=True)
    preact = jnp.dot(group_in, up_weight, preferred_element_type=jnp.float32) + up_bias.astype(
        jnp.float32
    )
    hidden = jax.nn.gelu(preact, approximate=False).astype(jnp.bfloat16)
    rows_in = hidden
    feed_out = lax.psum_scatter(
        jnp.dot(rows_in, down_weight, preferred_element_type=jnp.float32),
        "shard",
        scatter_dimension=0,
        tiled=True,
    ) + down_bias_all.astype(jnp.float32)
    outputs = (resid + attn_out + feed_out).astype(jnp.bfloat16)
    grad_top = cotangent.astype(jnp.float32)
    attn_group, attended_group, out_back = (
        lax.all_gather(attn_in, "shard", axis=0, tiled=True),
        lax.all_gather(attended, "shard", axis=0, tiled=True),
        lax.all_gather(out_weight, "shard", axis=1, tiled=True),
    )
    grad_cols = lax.all_to_all(cotangent, "shard", split_axis=1, concat_axis=0, tiled=True)
    grad_bias = jnp.sum(grad_cols.astype(jnp.float32), 0)
    grad_out_w = jnp.dot(attended_group.T, grad_cols, preferred_element_type=jnp.float32)
    grad_attended = (
        jnp.dot(cotangent, out_back.T, preferred_element_type=jnp.float32)
        .astype(jnp.bfloat16)
        .reshape(length, H, HD)
    )
    group_grad = lax.all_gather(cotangent, "shard", axis=0, tiled=True)
    grad_down = jnp.dot(hidden.T, group_grad, preferred_element_type=jnp.float32)
    grad_preact = jnp.dot(
        group_grad, down_weight.T, preferred_element_type=jnp.float32
    ) * gelu_slope(preact)
    grad_up_b = jnp.sum(grad_preact, 0)
    grad_preact_b = grad_preact.astype(jnp.bfloat16)
    grad_up = jnp.dot(group_in.T, grad_preact_b, preferred_element_type=jnp.float32)
    rows_in = grad_preact_b
    grad_feed_in = lax.psum_scatter(
        jnp.dot(rows_in, up_weight.T, preferred_element_type=jnp.float32),
        "shard",
        scatter_dimension=0,
        tiled=True,
    )

    def backward_block(carry, block_index):
        grad_keys, grad_values = carry
        row_start = block_index * row_block
        scores = block_scores(row_start, query_rot)
        probs_f = jnp.exp(scores - log_totals[block_index])
        probs_b = probs_f.astype(jnp.bfloat16)
        grad_values = grad_values + jnp.einsum(
            "hqk,qhd->khd", probs_b, grad_attended, preferred_element_type=jnp.float32
        )
        grad_probs = jnp.einsum(
            "qhd,khd->hqk", grad_attended, values_b, preferred_element_type=jnp.float32
        )
        grad_scores = (
            probs_f * (grad_probs - jnp.sum(probs_f * grad_probs, -1, keepdims=True)) * score_scale
        )
        grad_scores_b = grad_scores.astype(jnp.bfloat16)
        grad_qrot = jnp.einsum(
            "hqk,khd->qhd", grad_scores_b, keys_rot, preferred_element_type=jnp.float32
        )
        grad_keys = grad_keys + jnp.einsum(
            "hqk,qhd->khd", grad_scores_b, query_rot, preferred_element_type=jnp.float32
        )
        return ((grad_keys, grad_values), grad_qrot)

    empty_heads = jnp.zeros((length, H, HD), jnp.float32)
    (grad_krot, grad_values), grad_qrot = lax.scan(
        backward_block, (empty_heads, empty_heads), jnp.arange(block_count)
    )
    grad_qrot = grad_qrot.reshape(length, H, HD)
    grad_query = rotate(grad_qrot, cosine, sine_table, ROT, -1.0)
    grad_keys = rotate(grad_krot, cosine, sine_table, ROT, -1.0)
    grad_proj = jnp.stack([grad_query, grad_keys, grad_values], axis=1).reshape(length, 3 * D)
    grad_qkv_b = jnp.sum(grad_proj, 0)
    grad_proj_b = grad_proj.astype(jnp.bfloat16)
    proj_cols = lax.all_to_all(grad_proj_b, "shard", split_axis=1, concat_axis=0, tiled=True)
    grad_qkv = jnp.dot(attn_group.T, proj_cols, preferred_element_type=jnp.float32)
    rows_in = proj_cols
    grad_attn_in = lax.psum_scatter(
        jnp.dot(rows_in, qkv_weight.T, preferred_element_type=jnp.float32),
        "shard",
        scatter_dimension=0,
        tiled=True,
    )
    grad_gain_one = jnp.sum(grad_attn_in * normed, 0)
    grad_shift_one = jnp.sum(grad_attn_in, 0)
    grad_gain_two = jnp.sum(grad_feed_in * normed, 0)
    grad_shift_two = jnp.sum(grad_feed_in, 0)
    grad_normed = grad_attn_in * gain_one + grad_feed_in * gain_two
    input_grad = grad_top + inv_std * (
        grad_normed
        - jnp.mean(grad_normed, -1, keepdims=True)
        - normed * jnp.mean(grad_normed * normed, -1, keepdims=True)
    )
    grad_qkv_b, grad_gain_one, grad_shift_one, grad_gain_two, grad_shift_two = (
        lax.psum_scatter(grad_qkv_b, "shard", scatter_dimension=0, tiled=True),
        lax.psum_scatter(grad_gain_one, "shard", scatter_dimension=0, tiled=True),
        lax.psum_scatter(grad_shift_one, "shard", scatter_dimension=0, tiled=True),
        lax.psum_scatter(grad_gain_two, "shard", scatter_dimension=0, tiled=True),
        lax.psum_scatter(grad_shift_two, "shard", scatter_dimension=0, tiled=True),
    )
    (
        grad_gain_one,
        grad_shift_one,
        grad_gain_two,
        grad_shift_two,
        grad_qkv,
        grad_qkv_b,
        grad_out_w,
        grad_bias,
        grad_up,
        grad_up_b,
        grad_down,
    ) = lax.psum(
        (
            grad_gain_one,
            grad_shift_one,
            grad_gain_two,
            grad_shift_two,
            grad_qkv,
            grad_qkv_b,
            grad_out_w,
            grad_bias,
            grad_up,
            grad_up_b,
            grad_down,
        ),
        "rep",
    )
    return (
        outputs,
        input_grad,
        grad_gain_one,
        grad_shift_one,
        grad_gain_two,
        grad_shift_two,
        grad_qkv,
        grad_qkv_b,
        grad_out_w,
        grad_bias,
        grad_up,
        grad_up_b,
        grad_down,
        grad_bias,
    )


AXES = ("rep", "shard")
Z, Y, C, X = 4, 2, 2, 2


def moves(target):
    pairs = []
    for z in range(Z):
        for y in range(Y):
            for c in range(C):
                for x in range(X):
                    to = target(z, y, c, x)
                    if to is not None:
                        to_z, to_y, to_c, to_x = to
                        source = ((z * Y + y) * C + c) * X + x
                        pairs.append((source, ((to_z * Y + to_y) * C + to_c) * X + to_x))
    return pairs


TO_CORE = moves(lambda z, y, c, x: (z, y, 1 - c, x))
TO_X = moves(lambda z, y, c, x: (z, y, c, 1 - x))
TO_Y = moves(lambda z, y, c, x: (z, 1 - y, c, x))
TO_XY = moves(lambda z, y, c, x: (z, 1 - y, c, 1 - x))
INWARD = moves(lambda z, y, c, x: {0: (1, y, c, x), 3: (2, y, c, x)}.get(z))
MIDDLE = moves(lambda z, y, c, x: {1: (2, y, c, x), 2: (1, y, c, x)}.get(z))
OUTWARD = moves(lambda z, y, c, x: {1: (0, y, c, x), 2: (3, y, c, x)}.get(z))

WIDE = 2 * HD
BF16, F32 = jnp.bfloat16, jnp.float32
Y_RETURN = 8


def send(value, pairs):
    return lax.ppermute(value, AXES, pairs)


def dot_over(a, b, dims):
    return lax.dot_general(a, b, ((dims[:1], dims[1:]), ((), ())), preferred_element_type=F32)


def shape_of(shape, dtype):
    return jax.ShapeDtypeStruct(tuple(shape), dtype)


def room(mebibytes):
    return pltpu.CompilerParams(vmem_limit_bytes=mebibytes * 2**20)


VMEM = pl.BlockSpec(memory_space=pltpu.VMEM)
ANY = pl.BlockSpec(memory_space=pltpu.HBM)
SMEM = pl.BlockSpec(memory_space=pltpu.SMEM)


def cost(flops, moved, transcendentals=0):
    return pl.CostEstimate(flops=int(flops), bytes_accessed=int(moved), transcendentals=int(transcendentals))


def rotary_arrays(length):
    half = ROT // 2
    angles = np.arange(length, dtype=np.float32)[:, None] * np.exp(
        np.arange(half, dtype=np.float32) * np.float32(-2.0 * math.log(base_freq) / ROT)
    )
    keep = np.ones((length, HD), np.float32)
    up = np.zeros((length, HD), np.float32)
    down = np.zeros((length, HD), np.float32)
    keep[:, :half] = keep[:, half:ROT] = np.cos(angles)
    up[:, :half] = -np.sin(angles)
    down[:, half:ROT] = np.sin(angles)
    return [jnp.asarray(np.tile(t, (1, 2))) for t in (keep, up, down)]


def pack_kernel(at_ref, inputs_ref, rows_ref, *refs):
    vector_refs, (mine_ref, sent_ref), line_refs, sems = refs[:6], refs[6:8], refs[8:14], refs[14]
    part, x = at_ref[0], at_ref[1]
    length, columns = inputs_ref.shape[0], mine_ref.shape[1]
    half = WIDE // 2
    rows_of = lambda first, count: rows_ref.at[pl.ds(pl.multiple_of(first, half), count), :]
    mine_at, their_at = (4 * x + part) * WIDE, (4 * (1 - x) + part) * WIDE
    copies = [
        pltpu.make_async_copy(inputs_ref, sent_ref.at[pl.ds(0, length), :], sems.at[0]),
        pltpu.make_async_copy(rows_of(mine_at, WIDE), mine_ref.at[pl.ds(0, WIDE), :], sems.at[1]),
    ]
    for n in range(2):
        target = sent_ref.at[pl.ds(length, half), pl.ds(n * columns, columns)]
        copies.append(pltpu.make_async_copy(rows_of(their_at + n * half, half), target, sems.at[2 + n]))
    for n, ref in enumerate(vector_refs):
        copies.append(pltpu.make_async_copy(ref, line_refs[n], sems.at[4 + n]))
    for copy in copies:
        copy.start()
    for copy in copies:
        copy.wait()
    lines = [ref[...][None, :] for ref in line_refs]
    lines.append(jnp.zeros((10, columns), BF16))
    tail = jnp.concatenate(lines, 0)
    mine_ref[WIDE:, :] = tail
    sent_ref[length + half :, :columns] = tail
    sent_ref[length + half :, columns:] = jnp.zeros_like(tail)


def pack(at, inputs, out_weight, vectors):
    columns = out_weight.shape[1]
    return pl.pallas_call(
        pack_kernel,
        in_specs=[SMEM] + [ANY] * 8,
        out_specs=[VMEM] * 2,
        out_shape=[
            shape_of((WIDE + 16, columns), BF16),
            shape_of((inputs.shape[0] + WIDE // 2 + 16, 2 * columns), BF16),
        ],
        scratch_shapes=[pltpu.VMEM((columns,), BF16)] * 6 + [pltpu.SemaphoreType.DMA((10,))],
        compiler_params=room(60),
        cost_estimate=cost(0, 0),
    )(at, inputs, out_weight, *vectors)


def stack_kernel(a_ref, b_ref, c_ref, d_ref, out_ref):
    rows = a_ref.shape[0]
    for n, ref in enumerate((a_ref, b_ref, c_ref, d_ref)):
        out_ref[n * rows : (n + 1) * rows, :] = ref[:rows, :]


def stack(*parts):
    rows, columns = parts[0].shape
    return pl.pallas_call(
        stack_kernel,
        in_specs=[VMEM] * 4,
        out_specs=VMEM,
        out_shape=shape_of((4 * rows, columns), BF16),
        compiler_params=room(2),
        cost_estimate=cost(0, 0),
    )(*parts)


def weights_kernel(at_ref, up_ref, down_ref, qkv_ref, up_own_ref, down_own_ref, qkv_own_ref, sems):
    part = at_ref[0]
    own = up_own_ref.shape[1]
    at_own = pl.ds(pl.multiple_of(part * own, own), own)
    copies = [
        pltpu.make_async_copy(up_ref.at[:, at_own], up_own_ref, sems.at[0]),
        pltpu.make_async_copy(down_ref.at[at_own, :], down_own_ref, sems.at[1]),
    ]
    for n in range(3):
        at_third = pl.ds(pl.multiple_of((4 * n + part) * WIDE, WIDE), WIDE)
        to_third = pl.ds(n * WIDE, WIDE)
        copies.append(pltpu.make_async_copy(qkv_ref.at[:, at_third], qkv_own_ref.at[:, to_third], sems.at[2 + n]))
    for copy in copies:
        copy.start()
    for copy in copies:
        copy.wait()


def own_weights(at, up_weight, down_weight, qkv_weight):
    own = up_weight.shape[1] // 4
    return pl.pallas_call(
        weights_kernel,
        in_specs=[SMEM] + [ANY] * 3,
        out_specs=[VMEM] * 3,
        out_shape=[shape_of((D, own), BF16), shape_of((own, D), BF16), shape_of((D, 3 * WIDE), BF16)],
        scratch_shapes=[pltpu.SemaphoreType.DMA((5,))],
        compiler_params=room(57),
        cost_estimate=cost(0, 0),
    )(at, up_weight, down_weight, qkv_weight)


def normalise(rows):
    resid = rows.astype(F32)
    row_mean = jnp.mean(resid, -1, keepdims=True)
    centered = resid - row_mean
    inv_std = lax.rsqrt(jnp.mean(centered * centered, -1, keepdims=True) + norm_eps)
    return centered * inv_std


def chosen(rows, index):
    at = lax.broadcasted_iota(jnp.int32, rows.shape, 0)
    return jnp.sum(jnp.where(at == index, rows, 0.0), 0, keepdims=True)


def front_kernel(
    at_ref, low_ref, high_ref, mine_ref, theirs_ref, up_ref, up_bias_ref,
    attn_ref, feed_ref, hidden_ref, slope_ref, out_rows_ref, gains_ref,
):
    on_low = at_ref[1] == 0
    mine = mine_ref[...]
    columns = mine.shape[1]
    theirs = theirs_ref[theirs_ref.shape[0] - WIDE // 2 - 16 :, :]
    theirs = jnp.concatenate(
        [theirs[: WIDE // 2, :columns], theirs[: WIDE // 2, columns:], theirs[WIDE // 2 :, :columns]], 0
    )
    both = jnp.concatenate([jnp.where(on_low, mine, theirs), jnp.where(on_low, theirs, mine)], 1)
    out_rows_ref[...] = both[:WIDE]
    gains_ref[...] = both[WIDE:].astype(F32)[:8]
    up_bias = chosen(up_bias_ref[...].astype(F32), at_ref[0])
    rows = low_ref.shape[0] // 2
    for source, base in ((low_ref, 0), (high_ref, low_ref.shape[0])):
        for i in range(source.shape[0] // rows):
            at = slice(base + i * rows, base + (i + 1) * rows)
            normed = normalise(source[i * rows : (i + 1) * rows, :])
            feed_in = (normed * gains_ref[2:3] + gains_ref[3:4]).astype(BF16)
            attn_ref[at, :] = (normed * gains_ref[0:1] + gains_ref[1:2]).astype(BF16)
            feed_ref[at, :] = feed_in
            preact = jnp.dot(feed_in, up_ref[...], preferred_element_type=F32) + up_bias
            normal_cdf = 0.5 * (1.0 + lax.erf(preact * (1.0 / math.sqrt(2.0))))
            hidden_ref[at, :] = (preact * normal_cdf).astype(BF16)
            slope_ref[at, :] = normal_cdf + preact * jnp.exp(-0.5 * preact * preact) * (1.0 / math.sqrt(2.0 * math.pi))


def front(at, low, high, mine, theirs, up_own, up_bias):
    count, own = 2 * low.shape[0], up_own.shape[1]
    return pl.pallas_call(
        front_kernel,
        in_specs=[SMEM] + [VMEM] * 6,
        out_specs=[VMEM] * 6,
        out_shape=[shape_of((count, D), BF16)] * 2
        + [shape_of((count, own), BF16), shape_of((count, own), F32)]
        + [shape_of((WIDE, D), BF16), shape_of((8, D), F32)],
        compiler_params=room(8),
        cost_estimate=cost(0, 0),
    )(at, low, high, mine, theirs, up_own, up_bias)


def project_kernel(
    at_ref, rows_ref, qkv_ref, b_ref, keep_ref, turn_up_ref, turn_down_ref, first_ref, passed_ref, third_ref
):
    on_low = at_ref[1] == 0
    part = at_ref[0]
    all_bias = b_ref[...].astype(F32)
    bias = jnp.concatenate([chosen(all_bias, 4 * n + part) for n in range(3)], 1)
    half = ROT // 2
    length = keep_ref.shape[0]
    rows = 2 * length

    def turned(part):
        left = pltpu.roll(part, WIDE - half, 1)
        right = pltpu.roll(part, half, 1)
        pieces = []
        for i in range(part.shape[0] // length):
            at = slice(i * length, (i + 1) * length)
            pieces.append(part[at] * keep_ref[...] + left[at] * turn_up_ref[...] + right[at] * turn_down_ref[...])
        return jnp.concatenate(pieces, 0)

    for i in range(rows_ref.shape[0] // rows):
        at = slice(i * rows, (i + 1) * rows)
        value = jnp.dot(rows_ref[at, :], qkv_ref[...], preferred_element_type=F32) + bias
        first_ref[at, :] = turned(value[:, :WIDE]).astype(BF16)
        passed, third = value[:, WIDE : 2 * WIDE], value[:, 2 * WIDE :]
        passed_ref[at, :] = jnp.where(on_low, turned(passed), passed).astype(BF16)
        third_ref[at, :] = jnp.where(on_low, turned(third), third).astype(BF16)


def project(at, rows, qkv_own, qkv_bias, tables):
    count = rows.shape[0]
    return pl.pallas_call(
        project_kernel,
        in_specs=[SMEM] + [VMEM] * 6,
        out_specs=[VMEM] * 3,
        out_shape=[shape_of((count, WIDE), BF16)] * 3,
        compiler_params=room(8),
        cost_estimate=cost(2 * count * D * 3 * WIDE, 4 * count * D),
    )(at, rows, qkv_own, qkv_bias, *tables)


def down_kernel(hidden_ref, low_ref, high_ref, cot_ref, first_ref, second_ref):
    half, half_d = low_ref.shape[0], low_ref.shape[1] // 2
    cot_ref[:half, :] = low_ref[...]
    cot_ref[half:, :] = high_ref[...]
    first_ref[...] = dot_over(hidden_ref[...], cot_ref[:, :half_d], (0, 0)).astype(BF16)
    second_ref[...] = dot_over(hidden_ref[...], cot_ref[:, half_d:], (0, 0)).astype(BF16)


def grad_down_chunks(hidden, low, high):
    count, own = hidden.shape
    return pl.pallas_call(
        down_kernel,
        in_specs=[VMEM] * 3,
        out_specs=[VMEM] * 3,
        out_shape=[shape_of((count, D), BF16)] + [shape_of((own, D // 2), BF16)] * 2,
        compiler_params=room(10),
        cost_estimate=cost(2 * count * own * D, 6 * count * D),
    )(hidden, low, high)


def attention_kernel(
    at_ref, first_ref, third_ref, taken_ref, grad_ref, keep_ref, up_ref, down_ref, away_ref, here_ref
):
    length, width = keep_ref.shape
    on_low = at_ref[1] == 0
    lane = lax.broadcasted_iota(jnp.int32, (length, width), 1)
    causal = lax.broadcasted_iota(jnp.int32, (length, length), 0) >= lax.broadcasted_iota(
        jnp.int32, (length, length), 1
    )
    scale = 1.0 / math.sqrt(HD)
    half = ROT // 2

    def back(value):
        return (
            value * keep_ref[...]
            - pltpu.roll(value, width - half, 1) * up_ref[...]
            - pltpu.roll(value, half, 1) * down_ref[...]
        )

    for i in range(first_ref.shape[0] // length):
        rows = slice(i * length, (i + 1) * length)
        first, third, taken, grad = first_ref[rows, :], third_ref[rows, :], taken_ref[rows, :], grad_ref[rows, :]
        query = jnp.where(on_low, first, taken)
        keys = jnp.where(on_low, third, first)
        values = jnp.where(on_low, taken, third)
        zero = jnp.zeros_like(query)
        found = []
        for head in range(width // HD):
            mine = (lane >= head * HD) & (lane < (head + 1) * HD)
            scores = dot_over(jnp.where(mine, query, zero), keys, (1, 1)) * scale
            scores = jnp.where(causal, scores, -jnp.inf)
            row_max = jnp.max(scores, -1, keepdims=True)
            log_total = row_max + jnp.log(jnp.sum(jnp.exp(scores - row_max), -1, keepdims=True))
            probs = jnp.exp(scores - log_total)
            probs_b = probs.astype(BF16)
            attended = jnp.dot(probs_b, values, preferred_element_type=F32)
            grad_values = dot_over(probs_b, grad, (0, 0))
            grad_probs = dot_over(jnp.where(mine, grad, zero), values, (1, 1))
            inner = jnp.sum(probs * grad_probs, -1, keepdims=True)
            grad_scores = (probs * (grad_probs - inner) * scale).astype(BF16)
            grad_query = jnp.dot(grad_scores, keys, preferred_element_type=F32)
            grad_keys = dot_over(grad_scores, query, (0, 0))
            new = (attended, grad_query, grad_keys, grad_values)
            found = new if not found else tuple(jnp.where(mine, n, o) for n, o in zip(new, found))
        attended, grad_query, grad_keys, grad_values = found
        grad_query, grad_keys = back(grad_query), back(grad_keys)
        away_ref[rows, :width] = attended.astype(BF16)
        away_ref[rows, width:] = jnp.where(on_low, grad_values, grad_query).astype(BF16)
        here_ref[rows, :width] = jnp.where(on_low, grad_query, grad_keys).astype(BF16)
        here_ref[rows, width:] = jnp.where(on_low, grad_keys, grad_values).astype(BF16)


def swapped(i):
    return i + 1 - 2 * (i % 2)


def attention(at, first, third, taken, grad, tables):
    count, width = first.shape
    length = tables[0].shape[0]
    block = pl.BlockSpec((2 * length, width), lambda i, s: (i, 0))
    other = pl.BlockSpec((2 * length, width), lambda i, s: (swapped(i), 0))
    table = pl.BlockSpec((length, width), lambda i, s: (0, 0))
    out = pl.BlockSpec((2 * length, 2 * width), lambda i, s: (i, 0))
    return pl.pallas_call(
        attention_kernel,
        grid_spec=pltpu.PrefetchScalarGridSpec(
            num_scalar_prefetch=1,
            grid=(count // (2 * length),),
            in_specs=[block, block, other, block] + [table] * 3,
            out_specs=[out, out],
        ),
        out_shape=[shape_of((count, 2 * width), BF16)] * 2,
        compiler_params=room(12),
        cost_estimate=cost(24 * count * length * width, 16 * count * width, 4 * count * length),
    )(at, first, third, taken, grad, *tables)


def branch_kernel(hidden_ref, away_ref, down_ref, out_rows_ref, kept_ref, sent_ref):
    half = kept_ref.shape[0]
    branches = jnp.dot(hidden_ref[...], down_ref[...], preferred_element_type=F32) + jnp.dot(
        away_ref[:, :WIDE], out_rows_ref[...], preferred_element_type=F32
    )
    kept_ref[...] = branches[:half]
    sent_ref[...] = branches[half:].astype(BF16)


def branch_sums(hidden, away, down_own, out_rows):
    count, own = hidden.shape
    return pl.pallas_call(
        branch_kernel,
        in_specs=[VMEM] * 4,
        out_specs=[VMEM] * 2,
        out_shape=[shape_of((count // 2, D), F32), shape_of((count // 2, D), BF16)],
        compiler_params=room(10),
        cost_estimate=cost(2 * count * D * (own + WIDE), 6 * count * D),
    )(hidden, away, down_own, out_rows)


def group_kernel(
    at_ref, low_ref, high_ref, cotangent_ref, gp_ref, away_ref, here_ref, other_ref, up_ref, qkv_ref, gains_ref,
    kept_ref, sent_ref, sums_ref, proj_ref, att_ref,
):
    on_low = at_ref[1] == 0
    gains = gains_ref[...]
    own = gp_ref.shape[1]
    rows = low_ref.shape[0] // 2
    total = lambda v: jnp.sum(v.astype(F32), 0, keepdims=True)
    sums = None
    for i in range(4):
        at, swap = slice(i * rows, (i + 1) * rows), swapped(i)
        away, here, other = away_ref[at, :], here_ref[at, :], other_ref[swap * rows : (swap + 1) * rows, :]
        attended, attended_other = away[:, :WIDE], other[:, :WIDE]
        proj = jnp.concatenate([here[:, :WIDE], other[:, WIDE:], here[:, WIDE:]], 1)
        proj_ref[at, :] = proj
        att_ref[at, :] = jnp.concatenate(
            [jnp.where(on_low, attended, attended_other), jnp.where(on_low, attended_other, attended)], 1
        )
        gp = gp_ref[at, :]
        grad_attn = dot_over(proj, qkv_ref[...], (1, 1))
        grad_feed = dot_over(gp, up_ref[...], (1, 1))
        source = low_ref if i < 2 else high_ref
        local = slice((i % 2) * rows, (i % 2 + 1) * rows)
        normed = normalise(source[local, :])
        grad_normed = grad_attn * gains[0:1] + grad_feed * gains[2:3]
        new = [
            total(grad_attn * normed),
            total(grad_attn),
            total(grad_feed * normed),
            total(grad_feed),
            total(gp),
            total(proj),
        ]
        sums = new if sums is None else [a + b for a, b in zip(sums, new)]
        if i < 2:
            kept_ref[local, :] = grad_normed
        else:
            sent_ref[local, :] = grad_normed.astype(BF16)
    last = jnp.concatenate([sums[4], sums[5], jnp.zeros((1, D - own - 3 * WIDE), F32)], 1)
    sums_ref[...] = jnp.concatenate(sums[:4] + [total(cotangent_ref[...]), last, jnp.zeros((2, D), F32)], 0)


def group_sums(at, low, high, cotangent, gp, away, here, other, up_own, qkv_own, gains):
    count, own = gp.shape
    return pl.pallas_call(
        group_kernel,
        in_specs=[SMEM] + [VMEM] * 10,
        out_specs=[VMEM] * 5,
        out_shape=[
            shape_of((count // 2, D), F32),
            shape_of((count // 2, D), BF16),
            shape_of((8, D), F32),
            shape_of((count, 3 * WIDE), BF16),
            shape_of((count, 2 * WIDE), BF16),
        ],
        compiler_params=room(12),
        cost_estimate=cost(2 * count * D * (own + 3 * WIDE), 16 * count * D),
    )(at, low, high, cotangent, gp, away, here, other, up_own, qkv_own, gains)


def mixed_kernel(at_ref, rows_ref, proj_ref, att_ref, cot_ref, *refs):
    out_ref = refs[-1]
    out_ref[: 4 * WIDE, : 3 * WIDE] = dot_over(rows_ref[...], proj_ref[...], (0, 0)).astype(BF16)
    heads = dot_over(att_ref[...], cot_ref[...], (0, 0)).astype(BF16)
    out_ref[: 2 * WIDE, 3 * WIDE :] = heads[:, :WIDE]
    out_ref[2 * WIDE : 4 * WIDE, 3 * WIDE :] = heads[:, WIDE:]
    if len(refs) > 1:
        sums, other = refs[0][...], refs[1][...]
        row = lax.broadcasted_iota(jnp.int32, sums.shape, 0)
        sums = jnp.where(row < 5, sums + other, sums).astype(BF16)
        out_ref[4 * WIDE :, :] = jnp.concatenate([sums[:, : D // 2], sums[:, D // 2 :]], 0)


def mixed(at, half, rows, proj, att, cot, small):
    count = rows.shape[0]
    fixed = lambda i, s: (0, 0)
    tall = 4 * WIDE + (16 if small else 0)
    return pl.pallas_call(
        mixed_kernel,
        grid_spec=pltpu.PrefetchScalarGridSpec(
            num_scalar_prefetch=1,
            grid=(1,),
            in_specs=[
                pl.BlockSpec((count, 4 * WIDE), lambda i, s: (0, half)),
                pl.BlockSpec(proj.shape, fixed),
                pl.BlockSpec(att.shape, fixed),
                pl.BlockSpec((count, 2 * WIDE), lambda i, s: (0, 2 * s[1] + half)),
            ]
            + [pl.BlockSpec((8, D), fixed)] * len(small),
            out_specs=pl.BlockSpec((tall, 4 * WIDE), fixed),
        ),
        out_shape=shape_of((tall, 4 * WIDE), BF16),
        compiler_params=room(12),
        cost_estimate=cost(2 * count * 16 * WIDE * WIDE, 4 * count * D),
    )(at, rows, proj, att, cot, *small)


TALL = 528


def turn(at, grad, from_z, first, from_middle, following, carried, from_y):
    outs = []
    given = dict(
        grad=grad, from_z=from_z, first=first, from_middle=from_middle, following=following, carried=carried, from_y=from_y
    )
    names = [n for n, v in given.items() if v is not None]
    if grad is not None:
        outs.append(("first", grad.shape))
    if first is not None or following is not None:
        outs.append(("next", (following if following is not None else first).shape))
    if carried is not None:
        plain = carried.shape[0] < TALL or following is not None or grad is not None
        outs.append(("total", (512, 512) if plain else carried.shape))
    if carried is not None or from_y is not None:
        outs.append(("pair", (2 * TALL, 512)))

    def kernel(at_ref, *refs):
        values = dict(zip(names, refs))
        results = dict(zip([n for n, _ in outs], refs[len(names) :]))
        middle = at_ref[2] == 1
        if "first" in results:
            results["first"][...] = values["grad"][...] + values["from_z"][...]
        if "next" in results:
            out = results["next"]
            if "first" in values:
                tall = values["first"].shape[0]
                summed = values["first"][...] + values["from_middle"][...]
                if "following" in values:
                    out[:tall, :] = jnp.where(middle, summed, values["following"][:tall, :])
                    if out.shape[0] > tall:
                        out[tall:, :] = values["following"][tall:, :]
                else:
                    out[...] = summed
            else:
                out[...] = values["following"][...]
        if "total" in results:
            tall = results["total"].shape[0]
            total = jnp.where(middle, values["carried"][:tall, :], values["from_z"][:tall, :])
            results["total"][...] = total
            results["pair"][:tall, :] = total
            if tall < TALL:
                results["pair"][tall:TALL, :] = jnp.zeros((TALL - tall, 512), BF16)
        elif "pair" in results:
            results["pair"][:TALL, :] = jnp.zeros((TALL, 512), BF16)
        if "pair" in results:
            tall = values["from_y"].shape[0] if "from_y" in values else 0
            if tall:
                results["pair"][TALL : TALL + tall, :] = values["from_y"][...]
            if tall < TALL:
                results["pair"][TALL + tall :, :] = jnp.zeros((TALL - tall, 512), BF16)

    made = pl.pallas_call(
        kernel,
        in_specs=[SMEM] + [VMEM] * len(names),
        out_specs=[VMEM] * len(outs),
        out_shape=[shape_of(s, BF16) for _, s in outs],
        compiler_params=room(6),
        cost_estimate=cost(len(names) * 2**18, (len(names) + len(outs)) * 2**19),
    )(at, *[given[n] for n in names])
    return dict(zip([n for n, _ in outs], made))


def place(at, pieces, into, shapes, copies):
    count = len(shapes)
    each = len(copies(0))
    tall = 4 * WIDE

    def kernel(at_ref, *refs):
        piece_refs = refs[:4]
        out_refs = refs[4 + (count if into else 0) :][:count]
        wide_ref, sems = refs[-2:]
        started = []
        for i in range(4):
            base = TALL if i == 3 else 0
            wide_ref[i] = piece_refs[i][base : base + tall, :].astype(F32)
            for n, (which, at, part) in enumerate(copies(at_ref[3 + i])):
                copy = pltpu.make_async_copy(wide_ref.at[i].at[part], out_refs[which].at[at], sems.at[i * each + n])
                copy.start()
                started.append(copy)
        for copy in started:
            copy.wait()

    any_space = pl.BlockSpec(memory_space=pl.ANY)
    return pl.pallas_call(
        kernel,
        in_specs=[SMEM] + [VMEM] * 4 + [any_space] * len(into or ()),
        out_specs=[any_space] * count,
        scratch_shapes=[pltpu.VMEM((4, tall, tall), F32), pltpu.SemaphoreType.DMA((4 * each,))],
        out_shape=[shape_of(s, F32) for s in shapes],
        compiler_params=room(8),
        input_output_aliases={5 + k: k for k in range(count)} if into else {},
        cost_estimate=cost(0, 24 * tall * tall),
    )(at, *pieces, *(into or ()))


def fold_kernel(kept_ref, got_ref, stay_ref, go_ref):
    rows = stay_ref.shape[0]
    stay_ref[...] = kept_ref[:rows, :] + got_ref[:rows, :].astype(F32)
    go_ref[...] = (kept_ref[rows:, :] + got_ref[rows:, :].astype(F32)).astype(BF16)


def fold(kept, got):
    rows = kept.shape[0] // 2
    return pl.pallas_call(
        fold_kernel,
        in_specs=[VMEM] * 2,
        out_specs=[VMEM] * 2,
        out_shape=[shape_of((rows, D), F32), shape_of((rows, D), BF16)],
        compiler_params=room(4),
        cost_estimate=cost(kept.size, 9 * kept.size),
    )(kept, got)


def last_kernel(inputs_ref, cotangent_ref, gains_ref, a_ref, b_ref, c_ref, d_ref, outputs_ref, grad_ref):
    resid = inputs_ref[...].astype(F32)
    row_mean = jnp.mean(resid, -1, keepdims=True)
    centered = resid - row_mean
    inv_std = lax.rsqrt(jnp.mean(centered * centered, -1, keepdims=True) + norm_eps)
    normed = centered * inv_std
    branches = a_ref[...] + b_ref[...].astype(F32)
    outputs_ref[...] = (resid + branches + (gains_ref[4:5] + gains_ref[5:6])).astype(BF16)
    grad_normed = c_ref[...] + d_ref[...].astype(F32)
    grad_ref[...] = cotangent_ref[...].astype(F32) + inv_std * (
        grad_normed
        - jnp.mean(grad_normed, -1, keepdims=True)
        - normed * jnp.mean(grad_normed * normed, -1, keepdims=True)
    )


def last(inputs, cotangent, gains, *sums):
    return pl.pallas_call(
        last_kernel,
        in_specs=[VMEM] * 7,
        out_specs=[VMEM] * 2,
        out_shape=[shape_of(inputs.shape, BF16), shape_of(inputs.shape, F32)],
        compiler_params=room(4),
        cost_estimate=cost(inputs.size * 20, inputs.size * 20),
    )(inputs, cotangent, gains, *sums)


def at_blocks(first, size):
    return pl.ds(pl.multiple_of(first, size), size)


def small_kernel(at_ref, a_ref, b_ref, c_ref, d_ref, g1, s1, g2, s2, ob, up_ref, qkv_ref):
    on_low = at_ref[1] == 0
    parts = [r[...].astype(F32) for r in (a_ref, b_ref, c_ref, d_ref)]
    sums = (parts[0] + parts[1]) + (parts[2] + parts[3])
    sums = jnp.where(on_low, sums[:8], sums[8:])
    for row, ref in enumerate((g1, s1, g2, s2, ob)):
        ref[...] = sums[row : row + 1]
    for i, part in enumerate(parts):
        p = at_ref[3 + i]
        up_ref[pl.ds(p, 1), :] = part[5:6]
        for n in range(3):
            qkv_ref[pl.ds(4 * n + p, 1), :] = part[13:14, n * WIDE : (n + 1) * WIDE]


def small_outputs(at, pieces):
    fixed = lambda i, s: (0, 0)
    half_d = D // 2
    return pl.pallas_call(
        small_kernel,
        grid_spec=pltpu.PrefetchScalarGridSpec(
            num_scalar_prefetch=1,
            grid=(1,),
            in_specs=[pl.BlockSpec((16, half_d), lambda i, s: (32, 0))] * 3
            + [pl.BlockSpec((16, half_d), lambda i, s: (TALL // 16 + 32, 0))],
            out_specs=[pl.BlockSpec((1, half_d), fixed)] * 5
            + [pl.BlockSpec((4, half_d), fixed), pl.BlockSpec((12, WIDE), fixed)],
        ),
        compiler_params=room(2),
        out_shape=[shape_of((1, half_d), F32)] * 5 + [shape_of((4, half_d), F32), shape_of((12, WIDE), F32)],
    )(at, *pieces)


def fast_body(
    inputs,
    attn_gain,
    attn_shift,
    feed_gain,
    feed_shift,
    qkv_weight,
    qkv_bias,
    out_weight,
    out_bias,
    up_weight,
    up_bias,
    down_weight,
    down_bias,
    cotangent,
):
    length = inputs.shape[0]
    rep, x = lax.axis_index("rep"), lax.axis_index("shard")
    z, y, c = rep // 4, rep // 2 % 2, rep % 2
    part = y * 2 + c
    middle = ((z == 1) | (z == 2)).astype(jnp.int32)
    at = jnp.stack([part, x, middle, part, part ^ 2, part ^ 1, part ^ 3, part]).astype(jnp.int32)
    fence = lax.optimization_barrier
    half_d = D // 2
    tables = rotary_arrays(length)
    vectors = [attn_gain, attn_shift, feed_gain, feed_shift, out_bias, down_bias]
    own = up_weight.shape[1] // 4

    from_y, from_xy = send(inputs, TO_Y), send(inputs, TO_XY)
    mine, packed = pack(at, inputs, out_weight, vectors)
    from_x = send(packed, TO_X)
    cot_first, mine = fence((cotangent, mine))
    cot_parts = [send(cot_first, p) for p in (TO_Y, TO_X, TO_XY)]
    up_own, down_own, qkv_own = own_weights(at, up_weight, down_weight, qkv_weight)
    from_x, from_y, from_xy, up_own, down_own, qkv_own = fence((from_x, from_y, from_xy, up_own, down_own, qkv_own))
    low = stack(inputs, from_y, from_x, from_xy)
    theirs = from_x
    high = send(low, TO_CORE)
    cot_parts, low = fence((cot_parts, low))
    low_cot = stack(cotangent, *cot_parts)
    high_cot = send(low_cot, TO_CORE)
    attn_in, feed_in, hidden, slope, out_rows, gains = front(
        at, low, high, mine, theirs, up_own, up_bias.reshape(4, -1)
    )
    cot, chunk0, chunk1 = grad_down_chunks(hidden, low_cot, high_cot)

    env = dict(
        attn_in=attn_in, feed_in=feed_in, hidden=hidden, slope=slope, cot=cot,
        qkv_own=qkv_own, out_rows=out_rows, gains=gains, low=low, high=high, down_own=down_own, up_own=up_own,
    )
    chunks = {0: chunk0, 1: chunk1}
    loose = {}

    def after(step, env):
        e = dict(env)
        if step == 0:
            e["first"], passed, e["third"] = project(
                at, e["attn_in"], e["qkv_own"], qkv_bias.reshape(12, -1), tables
            )
            e["taken"] = send(passed, TO_X)
            gp = dot_over(e["cot"], e["down_own"], (1, 1)) * e.pop("slope")
            e["gp"] = gp.astype(BF16)
            e["grad_attended"] = dot_over(e["cot"], e["out_rows"], (1, 1)).astype(BF16)
            chunks[2] = dot_over(e["feed_in"][:, :half_d], e["gp"], (0, 0)).astype(BF16)
        if step == 1:
            e["away"], e["here"] = attention(
                at, e.pop("first"), e.pop("third"), e.pop("taken"), e.pop("grad_attended"), tables
            )
            chunks[3] = dot_over(e.pop("feed_in")[:, half_d:], e["gp"], (0, 0)).astype(BF16)
            e["kept_b"], e["sent_b"] = branch_sums(e.pop("hidden"), e["away"], e.pop("down_own"), e.pop("out_rows"))
        if step == 2:
            e["other"] = send(e["away"], TO_X)
            e["kept_b"], e["sent_b"] = fold(e["kept_b"], send(e["sent_b"], TO_CORE))
        if step == 3:
            e["kept_g"], e["sent_g"], e["sums"], e["proj"], e["att"] = group_sums(
                at, e.pop("low"), e.pop("high"), cotangent, e.pop("gp"), e.pop("away"), e.pop("here"),
                e.pop("other"), e.pop("up_own"), e.pop("qkv_own"), e["gains"],
            )
            chunks[4] = mixed(at, 0, e["attn_in"], e["proj"], e["att"], e["cot"], ())
            e["kept_b"], e["sent_b"] = fold(e["kept_b"], send(e["sent_b"], TO_X))
        if step == 4:
            other = send(e["sums"], TO_X)
            chunks[5] = mixed(
                at, 1, e.pop("attn_in"), e.pop("proj"), e.pop("att"), e.pop("cot"), (e.pop("sums"), other)
            )
        if step == 5:
            e["kept_g"], e["sent_g"] = fold(e["kept_g"], send(e["sent_g"], TO_CORE))
        if step == 6:
            e["kept_g"], e["sent_g"] = fold(e["kept_g"], send(e["sent_g"], TO_X))
        if step == Y_RETURN - 1:
            e["got_b"] = send(e.pop("sent_b"), TO_Y)
        if step == Y_RETURN:
            loose["g"] = send(e.pop("sent_g"), TO_Y)
        return e

    count = 6
    operand, one, total, over_y, pair, got_pair = {}, {}, {}, {}, {}, {}
    outs = {}
    operand[0] = chunks[0]

    def finish(k):
        pieces = [total.pop(k), over_y.pop(k), got_pair.pop(k), got_pair[k + 1]]
        h = k % 2
        rows, columns = pl.ds(h * half_d, half_d), pl.ds(h * half_d, half_d)
        everything = (slice(None), slice(None))
        if k < 2:
            outs["down"] = place(
                at, pieces, outs.get("down"), [down_weight.shape],
                lambda p: [(0, (at_blocks(own * p, own), columns), everything)],
            )
        elif k < 4:
            outs["up"] = place(
                at, pieces, outs.get("up"), [up_weight.shape],
                lambda p: [(0, (rows, at_blocks(own * p, own)), everything)],
            )
        else:
            outs["attn"] = place(
                at, pieces, outs.get("attn"), [qkv_weight.shape, out_weight.shape],
                lambda p: [
                    (0, (rows, at_blocks(half_d * n + WIDE * p, WIDE)), (slice(None), pl.ds(n * WIDE, WIDE)))
                    for n in range(3)
                ]
                + [
                    (
                        1,
                        (at_blocks(half_d * side + WIDE * p, WIDE), pl.ds((2 * h + b) * WIDE, WIDE)),
                        (pl.ds((2 * b + side) * WIDE, WIDE), pl.ds(3 * WIDE, WIDE)),
                    )
                    for b in range(2)
                    for side in range(2)
                ],
            )
        if k == count - 1:
            outs["small"] = small_outputs(at, pieces)

    for step in range(count + 5):
        live = (env, chunks, operand, one, total, over_y, pair, got_pair, outs)
        env, chunks, operand, one, total, over_y, pair, got_pair, outs = fence(live)
        got = {}
        if 0 <= step - 1 < count:
            got["m"] = send(one[step - 1], MIDDLE)
        if step < count + 2:
            pairs = (INWARD if step < count else []) + (OUTWARD if step >= 2 else [])
            got["z"] = send(operand[step], pairs)
        if 0 <= step - 3 < count:
            got["y"] = send(total[step - 3], TO_Y)
        if step - 3 in pair:
            got["c"] = send(pair.pop(step - 3), TO_CORE)
        env = after(step, env)
        if 0 <= step - 5 < count:
            finish(step - 5)
        if step < count + 3:
            made = turn(
                at,
                chunks.pop(step) if step < count else None,
                got.get("z"),
                one.pop(step - 1) if 0 <= step - 1 < count else None,
                got.get("m"),
                chunks.get(step + 1),
                operand.pop(step) if 2 <= step < count + 2 else None,
                got.get("y"),
            )
            if "first" in made:
                one[step] = made["first"]
            if "next" in made:
                operand[step + 1] = made["next"]
            if "total" in made:
                total[step - 2] = made["total"]
            if "pair" in made:
                pair[step - 2] = made["pair"]
        if "y" in got:
            over_y[step - 3] = got["y"]
        if "c" in got:
            got_pair[step - 3] = got["c"]

    outputs, input_grad = last(inputs, cotangent, env["gains"], env["kept_b"], env["got_b"], env["kept_g"], loose["g"])
    g1, s1, g2, s2, ob, up_b, qkv_b = outs["small"]
    flat = lambda a: a.reshape(-1)
    return (
        outputs,
        input_grad,
        flat(g1),
        flat(s1),
        flat(g2),
        flat(s2),
        outs["attn"][0],
        flat(qkv_b),
        outs["attn"][1],
        flat(ob),
        outs["up"][0],
        flat(up_b),
        outs["down"][0],
        flat(ob),
    )


def choose_body(mesh):
    known = {"rep": Z * Y * C, "shard": X}
    return fast_body if dict(mesh.shape) == known else general_body


def solution(mesh):
    return jax.shard_map(
        choose_body(mesh),
        mesh=mesh,
        in_specs=(
            P(("rep", "shard"), None),
            P("shard"),
            P("shard"),
            P("shard"),
            P("shard"),
            P(None, "shard"),
            P("shard"),
            P(None, "shard"),
            P("shard"),
            P(None, "shard"),
            P("shard"),
            P("shard", None),
            P("shard"),
            P(("rep", "shard"), None),
        ),
        out_specs=(
            P(("rep", "shard"), None),
            P(("rep", "shard"), None),
            P("shard"),
            P("shard"),
            P("shard"),
            P("shard"),
            P(None, "shard"),
            P("shard"),
            P(None, "shard"),
            P("shard"),
            P(None, "shard"),
            P("shard"),
            P("shard", None),
            P("shard"),
        ),
        check_vma=False,
    )
```

```python
import math

import jax
import jax.numpy as jnp
import numpy as np
from jax import lax
from jax.experimental import pallas as pl
from jax.experimental.pallas import tpu as pltpu
from jax.sharding import PartitionSpec as P

D = 1024
H = 16
HD = 64
ROT = 16


norm_eps = 1e-05
base_freq = 10000.0


def rotary_tables(length, rotary_dims):
    half_dims = rotary_dims // 2
    positions = jnp.arange(length).astype(jnp.float32)
    inverse = jnp.exp(
        jnp.arange(half_dims).astype(jnp.float32) * (-2.0 * math.log(base_freq) / rotary_dims)
    )
    angles = positions[:, None] * inverse[None, :]
    return (jnp.cos(angles), jnp.sin(angles))


def rotate(values, cosine, sine_table, rotary_dims, direction):
    half_dims = rotary_dims // 2
    lower_half = values[..., :half_dims]
    upper_half = values[..., half_dims:rotary_dims]
    cosine_row = cosine[:, None, :]
    sine_row = sine_table[:, None, :] * direction
    return jnp.concatenate(
        [
            lower_half * cosine_row - upper_half * sine_row,
            upper_half * cosine_row + lower_half * sine_row,
            values[..., rotary_dims:],
        ],
        axis=-1,
    )


def gelu_slope(preact):
    normal_cdf = 0.5 * (1.0 + jax.scipy.special.erf(preact * (1.0 / math.sqrt(2.0))))
    return normal_cdf + preact * jnp.exp(-0.5 * preact * preact) * (1.0 / math.sqrt(2.0 * math.pi))


def general_body(
    inputs,
    attn_gain,
    attn_shift,
    feed_gain,
    feed_shift,
    qkv_weight,
    qkv_bias,
    out_weight,
    out_bias,
    up_weight,
    up_bias,
    down_weight,
    down_bias,
    cotangent,
):
    (
        gain_one,
        shift_one,
        gain_two,
        shift_two,
        out_bias_all,
        down_bias_all,
        qkv_all,
        qkv_bias_all,
        out_all,
    ) = (
        lax.all_gather(attn_gain, "shard", axis=0, tiled=True),
        lax.all_gather(attn_shift, "shard", axis=0, tiled=True),
        lax.all_gather(feed_gain, "shard", axis=0, tiled=True),
        lax.all_gather(feed_shift, "shard", axis=0, tiled=True),
        lax.all_gather(out_bias, "shard", axis=0, tiled=True),
        lax.all_gather(down_bias, "shard", axis=0, tiled=True),
        lax.all_gather(qkv_weight, "shard", axis=1, tiled=True),
        lax.all_gather(qkv_bias, "shard", axis=0, tiled=True),
        lax.all_gather(out_weight, "shard", axis=1, tiled=True),
    )
    gain_one = gain_one.astype(jnp.float32)
    gain_two = gain_two.astype(jnp.float32)
    length = inputs.shape[0]
    resid = inputs.astype(jnp.float32)
    row_mean = jnp.mean(resid, -1, keepdims=True)
    centered = resid - row_mean
    inv_std = lax.rsqrt(jnp.mean(centered * centered, -1, keepdims=True) + norm_eps)
    normed = centered * inv_std
    attn_in = (normed * gain_one + shift_one.astype(jnp.float32)).astype(jnp.bfloat16)
    feed_in = (normed * gain_two + shift_two.astype(jnp.float32)).astype(jnp.bfloat16)
    projected = jnp.dot(attn_in, qkv_all, preferred_element_type=jnp.float32) + qkv_bias_all.astype(
        jnp.float32
    )
    projected = projected.reshape(length, 3, H, HD)
    cosine, sine_table = rotary_tables(length, ROT)
    query_rot = rotate(projected[:, 0], cosine, sine_table, ROT, 1.0).astype(jnp.bfloat16)
    keys_rot = rotate(projected[:, 1], cosine, sine_table, ROT, 1.0).astype(jnp.bfloat16)
    values_b = projected[:, 2].astype(jnp.bfloat16)
    score_scale = 1.0 / math.sqrt(HD)
    row_block = min(512, length)
    block_count = length // row_block
    key_positions = jnp.arange(length)

    def block_scores(row_start, q_rows):
        scores = (
            jnp.einsum("qhd,khd->hqk", q_rows, keys_rot, preferred_element_type=jnp.float32)
            * score_scale
        )
        causal = (row_start + jnp.arange(row_block))[:, None] >= key_positions[None, :]
        return jnp.where(causal[None], scores, -jnp.inf)

    def forward_block(block_index):
        row_start = block_index * row_block
        scores = block_scores(row_start, query_rot)
        row_max = jnp.max(scores, -1, keepdims=True)
        log_total = row_max + jnp.log(jnp.sum(jnp.exp(scores - row_max), -1, keepdims=True))
        attn_probs = jnp.exp(scores - log_total).astype(jnp.bfloat16)
        block_out = jnp.einsum(
            "hqk,khd->qhd", attn_probs, values_b, preferred_element_type=jnp.float32
        )
        return (block_out.astype(jnp.bfloat16), log_total)

    attended, log_totals = lax.map(forward_block, jnp.arange(block_count))
    attended = attended.reshape(length, D)
    attn_out = jnp.dot(attended, out_all, preferred_element_type=jnp.float32) + out_bias_all.astype(
        jnp.float32
    )
    group_in = lax.all_gather(feed_in, "shard", axis=0, tiled=True)
    preact = jnp.dot(group_in, up_weight, preferred_element_type=jnp.float32) + up_bias.astype(
        jnp.float32
    )
    hidden = jax.nn.gelu(preact, approximate=False).astype(jnp.bfloat16)
    rows_in = hidden
    feed_out = lax.psum_scatter(
        jnp.dot(rows_in, down_weight, preferred_element_type=jnp.float32),
        "shard",
        scatter_dimension=0,
        tiled=True,
    ) + down_bias_all.astype(jnp.float32)
    outputs = (resid + attn_out + feed_out).astype(jnp.bfloat16)
    grad_top = cotangent.astype(jnp.float32)
    attn_group, attended_group, out_back = (
        lax.all_gather(attn_in, "shard", axis=0, tiled=True),
        lax.all_gather(attended, "shard", axis=0, tiled=True),
        lax.all_gather(out_weight, "shard", axis=1, tiled=True),
    )
    grad_cols = lax.all_to_all(cotangent, "shard", split_axis=1, concat_axis=0, tiled=True)
    grad_bias = jnp.sum(grad_cols.astype(jnp.float32), 0)
    grad_out_w = jnp.dot(attended_group.T, grad_cols, preferred_element_type=jnp.float32)
    grad_attended = (
        jnp.dot(cotangent, out_back.T, preferred_element_type=jnp.float32)
        .astype(jnp.bfloat16)
        .reshape(length, H, HD)
    )
    group_grad = lax.all_gather(cotangent, "shard", axis=0, tiled=True)
    grad_down = jnp.dot(hidden.T, group_grad, preferred_element_type=jnp.float32)
    grad_preact = jnp.dot(
        group_grad, down_weight.T, preferred_element_type=jnp.float32
    ) * gelu_slope(preact)
    grad_up_b = jnp.sum(grad_preact, 0)
    grad_preact_b = grad_preact.astype(jnp.bfloat16)
    grad_up = jnp.dot(group_in.T, grad_preact_b, preferred_element_type=jnp.float32)
    rows_in = grad_preact_b
    grad_feed_in = lax.psum_scatter(
        jnp.dot(rows_in, up_weight.T, preferred_element_type=jnp.float32),
        "shard",
        scatter_dimension=0,
        tiled=True,
    )

    def backward_block(carry, block_index):
        grad_keys, grad_values = carry
        row_start = block_index * row_block
        scores = block_scores(row_start, query_rot)
        probs_f = jnp.exp(scores - log_totals[block_index])
        probs_b = probs_f.astype(jnp.bfloat16)
        grad_values = grad_values + jnp.einsum(
            "hqk,qhd->khd", probs_b, grad_attended, preferred_element_type=jnp.float32
        )
        grad_probs = jnp.einsum(
            "qhd,khd->hqk", grad_attended, values_b, preferred_element_type=jnp.float32
        )
        grad_scores = (
            probs_f * (grad_probs - jnp.sum(probs_f * grad_probs, -1, keepdims=True)) * score_scale
        )
        grad_scores_b = grad_scores.astype(jnp.bfloat16)
        grad_qrot = jnp.einsum(
            "hqk,khd->qhd", grad_scores_b, keys_rot, preferred_element_type=jnp.float32
        )
        grad_keys = grad_keys + jnp.einsum(
            "hqk,qhd->khd", grad_scores_b, query_rot, preferred_element_type=jnp.float32
        )
        return ((grad_keys, grad_values), grad_qrot)

    empty_heads = jnp.zeros((length, H, HD), jnp.float32)
    (grad_krot, grad_values), grad_qrot = lax.scan(
        backward_block, (empty_heads, empty_heads), jnp.arange(block_count)
    )
    grad_qrot = grad_qrot.reshape(length, H, HD)
    grad_query = rotate(grad_qrot, cosine, sine_table, ROT, -1.0)
    grad_keys = rotate(grad_krot, cosine, sine_table, ROT, -1.0)
    grad_proj = jnp.stack([grad_query, grad_keys, grad_values], axis=1).reshape(length, 3 * D)
    grad_qkv_b = jnp.sum(grad_proj, 0)
    grad_proj_b = grad_proj.astype(jnp.bfloat16)
    proj_cols = lax.all_to_all(grad_proj_b, "shard", split_axis=1, concat_axis=0, tiled=True)
    grad_qkv = jnp.dot(attn_group.T, proj_cols, preferred_element_type=jnp.float32)
    rows_in = proj_cols
    grad_attn_in = lax.psum_scatter(
        jnp.dot(rows_in, qkv_weight.T, preferred_element_type=jnp.float32),
        "shard",
        scatter_dimension=0,
        tiled=True,
    )
    grad_gain_one = jnp.sum(grad_attn_in * normed, 0)
    grad_shift_one = jnp.sum(grad_attn_in, 0)
    grad_gain_two = jnp.sum(grad_feed_in * normed, 0)
    grad_shift_two = jnp.sum(grad_feed_in, 0)
    grad_normed = grad_attn_in * gain_one + grad_feed_in * gain_two
    input_grad = grad_top + inv_std * (
        grad_normed
        - jnp.mean(grad_normed, -1, keepdims=True)
        - normed * jnp.mean(grad_normed * normed, -1, keepdims=True)
    )
    grad_qkv_b, grad_gain_one, grad_shift_one, grad_gain_two, grad_shift_two = (
        lax.psum_scatter(grad_qkv_b, "shard", scatter_dimension=0, tiled=True),
        lax.psum_scatter(grad_gain_one, "shard", scatter_dimension=0, tiled=True),
        lax.psum_scatter(grad_shift_one, "shard", scatter_dimension=0, tiled=True),
        lax.psum_scatter(grad_gain_two, "shard", scatter_dimension=0, tiled=True),
        lax.psum_scatter(grad_shift_two, "shard", scatter_dimension=0, tiled=True),
    )
    (
        grad_gain_one,
        grad_shift_one,
        grad_gain_two,
        grad_shift_two,
        grad_qkv,
        grad_qkv_b,
        grad_out_w,
        grad_bias,
        grad_up,
        grad_up_b,
        grad_down,
    ) = lax.psum(
        (
            grad_gain_one,
            grad_shift_one,
            grad_gain_two,
            grad_shift_two,
            grad_qkv,
            grad_qkv_b,
            grad_out_w,
            grad_bias,
            grad_up,
            grad_up_b,
            grad_down,
        ),
        "rep",
    )
    return (
        outputs,
        input_grad,
        grad_gain_one,
        grad_shift_one,
        grad_gain_two,
        grad_shift_two,
        grad_qkv,
        grad_qkv_b,
        grad_out_w,
        grad_bias,
        grad_up,
        grad_up_b,
        grad_down,
        grad_bias,
    )


AXES = ("rep", "shard")
Z, Y, C, X = 4, 2, 2, 2


def moves(target):
    pairs = []
    for z in range(Z):
        for y in range(Y):
            for c in range(C):
                for x in range(X):
                    to = target(z, y, c, x)
                    if to is not None:
                        to_z, to_y, to_c, to_x = to
                        source = ((z * Y + y) * C + c) * X + x
                        pairs.append((source, ((to_z * Y + to_y) * C + to_c) * X + to_x))
    return pairs


TO_CORE = moves(lambda z, y, c, x: (z, y, 1 - c, x))
TO_X = moves(lambda z, y, c, x: (z, y, c, 1 - x))
TO_Y = moves(lambda z, y, c, x: (z, 1 - y, c, x))
TO_XY = moves(lambda z, y, c, x: (z, 1 - y, c, 1 - x))
INWARD = moves(lambda z, y, c, x: {0: (1, y, c, x), 3: (2, y, c, x)}.get(z))
MIDDLE = moves(lambda z, y, c, x: {1: (2, y, c, x), 2: (1, y, c, x)}.get(z))
OUTWARD = moves(lambda z, y, c, x: {1: (0, y, c, x), 2: (3, y, c, x)}.get(z))

WIDE = 2 * HD
BF16, F32 = jnp.bfloat16, jnp.float32
Y_RETURN = 8


def send(value, pairs):
    return lax.ppermute(value, AXES, pairs)


def dot_over(a, b, dims):
    return lax.dot_general(a, b, ((dims[:1], dims[1:]), ((), ())), preferred_element_type=F32)


def shape_of(shape, dtype):
    return jax.ShapeDtypeStruct(tuple(shape), dtype)


def room(mebibytes):
    return pltpu.CompilerParams(vmem_limit_bytes=mebibytes * 2**20)


VMEM = pl.BlockSpec(memory_space=pltpu.VMEM)
ANY = pl.BlockSpec(memory_space=pltpu.HBM)
SMEM = pl.BlockSpec(memory_space=pltpu.SMEM)


def cost(flops, moved, transcendentals=0):
    return pl.CostEstimate(flops=int(flops), bytes_accessed=int(moved), transcendentals=int(transcendentals))


def rotary_arrays(length):
    half = ROT // 2
    angles = np.arange(length, dtype=np.float32)[:, None] * np.exp(
        np.arange(half, dtype=np.float32) * np.float32(-2.0 * math.log(base_freq) / ROT)
    )
    keep = np.ones((length, HD), np.float32)
    up = np.zeros((length, HD), np.float32)
    down = np.zeros((length, HD), np.float32)
    keep[:, :half] = keep[:, half:ROT] = np.cos(angles)
    up[:, :half] = -np.sin(angles)
    down[:, half:ROT] = np.sin(angles)
    return [jnp.asarray(np.tile(t, (1, 2))) for t in (keep, up, down)]


def pack_kernel(at_ref, inputs_ref, rows_ref, *refs):
    vector_refs, (mine_ref, sent_ref, rows_out_ref), line_refs, sems = refs[:6], refs[6:9], refs[9:15], refs[15]
    part, x = at_ref[0], at_ref[1]
    length, columns = inputs_ref.shape[0], mine_ref.shape[1]
    rows_of = lambda first, count: rows_ref.at[pl.ds(pl.multiple_of(first, WIDE), count), :]
    mine_at, their_at = (4 * x + part) * WIDE, (4 * (1 - x) + part) * WIDE
    copies = [
        pltpu.make_async_copy(inputs_ref, sent_ref.at[pl.ds(0, length), :], sems.at[0]),
        pltpu.make_async_copy(rows_of(mine_at, WIDE), mine_ref.at[pl.ds(0, WIDE), :], sems.at[1]),
    ]
    copies.append(pltpu.make_async_copy(rows_of(their_at, WIDE), rows_out_ref, sems.at[2]))
    for n, ref in enumerate(vector_refs):
        copies.append(pltpu.make_async_copy(ref, line_refs[n], sems.at[3 + n]))
    for copy in copies:
        copy.start()
    for copy in copies:
        copy.wait()
    lines = [ref[...][None, :] for ref in line_refs]
    lines.append(jnp.zeros((10, columns), BF16))
    tail = jnp.concatenate(lines, 0)
    mine_ref[WIDE:, :] = tail
    sent_ref[length:, :columns] = tail
    sent_ref[length:, columns:] = jnp.zeros_like(tail)


def pack(at, inputs, out_weight, vectors):
    columns = out_weight.shape[1]
    return pl.pallas_call(
        pack_kernel,
        in_specs=[SMEM] + [ANY] * 8,
        out_specs=[VMEM] * 3,
        out_shape=[
            shape_of((WIDE + 16, columns), BF16),
            shape_of((inputs.shape[0] + 16, 2 * columns), BF16),
            shape_of((WIDE, columns), BF16),
        ],
        scratch_shapes=[pltpu.VMEM((columns,), BF16)] * 6 + [pltpu.SemaphoreType.DMA((9,))],
        compiler_params=room(60),
        cost_estimate=cost(0, 0),
    )(at, inputs, out_weight, *vectors)


def stack_kernel(a_ref, b_ref, c_ref, d_ref, out_ref):
    rows = a_ref.shape[0]
    for n, ref in enumerate((a_ref, b_ref, c_ref, d_ref)):
        out_ref[n * rows : (n + 1) * rows, :] = ref[:rows, :]


def stack(*parts):
    rows, columns = parts[0].shape
    return pl.pallas_call(
        stack_kernel,
        in_specs=[VMEM] * 4,
        out_specs=VMEM,
        out_shape=shape_of((4 * rows, columns), BF16),
        compiler_params=room(2),
        cost_estimate=cost(0, 0),
    )(*parts)


def weights_kernel(at_ref, up_ref, down_ref, qkv_ref, up_own_ref, down_own_ref, qkv_own_ref, sems):
    part = at_ref[0]
    own = up_own_ref.shape[1]
    at_own = pl.ds(pl.multiple_of(part * own, own), own)
    copies = [
        pltpu.make_async_copy(up_ref.at[:, at_own], up_own_ref, sems.at[0]),
        pltpu.make_async_copy(down_ref.at[at_own, :], down_own_ref, sems.at[1]),
    ]
    for n in range(3):
        at_third = pl.ds(pl.multiple_of((4 * n + part) * WIDE, WIDE), WIDE)
        to_third = pl.ds(n * WIDE, WIDE)
        copies.append(pltpu.make_async_copy(qkv_ref.at[:, at_third], qkv_own_ref.at[:, to_third], sems.at[2 + n]))
    for copy in copies:
        copy.start()
    for copy in copies:
        copy.wait()


def own_weights(at, up_weight, down_weight, qkv_weight):
    own = up_weight.shape[1] // 4
    return pl.pallas_call(
        weights_kernel,
        in_specs=[SMEM] + [ANY] * 3,
        out_specs=[VMEM] * 3,
        out_shape=[shape_of((D, own), BF16), shape_of((own, D), BF16), shape_of((D, 3 * WIDE), BF16)],
        scratch_shapes=[pltpu.SemaphoreType.DMA((5,))],
        compiler_params=room(57),
        cost_estimate=cost(0, 0),
    )(at, up_weight, down_weight, qkv_weight)


def normalise(rows):
    resid = rows.astype(F32)
    row_mean = jnp.mean(resid, -1, keepdims=True)
    centered = resid - row_mean
    inv_std = lax.rsqrt(jnp.mean(centered * centered, -1, keepdims=True) + norm_eps)
    return centered * inv_std


def chosen(rows, index):
    at = lax.broadcasted_iota(jnp.int32, rows.shape, 0)
    return jnp.sum(jnp.where(at == index, rows, 0.0), 0, keepdims=True)


def front_kernel(
    at_ref, low_ref, high_ref, mine_ref, theirs_ref, up_ref, up_bias_ref,
    attn_ref, feed_ref, hidden_ref, slope_ref, gains_ref,
):
    on_low = at_ref[1] == 0
    mine = mine_ref[WIDE:, :]
    theirs = theirs_ref[theirs_ref.shape[0] - 16 :, :]
    theirs = theirs[:, : mine.shape[1]]
    both = jnp.concatenate([jnp.where(on_low, mine, theirs), jnp.where(on_low, theirs, mine)], 1)
    gains_ref[...] = both.astype(F32)[:8]
    up_bias = chosen(up_bias_ref[...].astype(F32), at_ref[0])
    rows = low_ref.shape[0] // 2
    for source, base in ((low_ref, 0), (high_ref, low_ref.shape[0])):
        for i in range(source.shape[0] // rows):
            at = slice(base + i * rows, base + (i + 1) * rows)
            normed = normalise(source[i * rows : (i + 1) * rows, :])
            feed_in = (normed * gains_ref[2:3] + gains_ref[3:4]).astype(BF16)
            attn_ref[at, :] = (normed * gains_ref[0:1] + gains_ref[1:2]).astype(BF16)
            feed_ref[at, :] = feed_in
            preact = jnp.dot(feed_in, up_ref[...], preferred_element_type=F32) + up_bias
            normal_cdf = 0.5 * (1.0 + lax.erf(preact * (1.0 / math.sqrt(2.0))))
            hidden_ref[at, :] = (preact * normal_cdf).astype(BF16)
            slope_ref[at, :] = normal_cdf + preact * jnp.exp(-0.5 * preact * preact) * (1.0 / math.sqrt(2.0 * math.pi))


def front(at, low, high, mine, theirs, up_own, up_bias):
    count, own = 2 * low.shape[0], up_own.shape[1]
    return pl.pallas_call(
        front_kernel,
        in_specs=[SMEM] + [VMEM] * 6,
        out_specs=[VMEM] * 5,
        out_shape=[shape_of((count, D), BF16)] * 2
        + [shape_of((count, own), BF16), shape_of((count, own), F32), shape_of((8, D), F32)],
        compiler_params=room(8),
        cost_estimate=cost(0, 0),
    )(at, low, high, mine, theirs, up_own, up_bias)


def project_kernel(
    at_ref, rows_ref, qkv_ref, b_ref, keep_ref, turn_up_ref, turn_down_ref, first_ref, passed_ref, third_ref
):
    on_low = at_ref[1] == 0
    part = at_ref[0]
    all_bias = b_ref[...].astype(F32)
    bias = jnp.concatenate([chosen(all_bias, 4 * n + part) for n in range(3)], 1)
    half = ROT // 2
    length = keep_ref.shape[0]
    rows = 2 * length

    def turned(part):
        left = pltpu.roll(part, WIDE - half, 1)
        right = pltpu.roll(part, half, 1)
        pieces = []
        for i in range(part.shape[0] // length):
            at = slice(i * length, (i + 1) * length)
            pieces.append(part[at] * keep_ref[...] + left[at] * turn_up_ref[...] + right[at] * turn_down_ref[...])
        return jnp.concatenate(pieces, 0)

    for i in range(rows_ref.shape[0] // rows):
        at = slice(i * rows, (i + 1) * rows)
        value = jnp.dot(rows_ref[at, :], qkv_ref[...], preferred_element_type=F32) + bias
        first_ref[at, :] = turned(value[:, :WIDE]).astype(BF16)
        passed, third = value[:, WIDE : 2 * WIDE], value[:, 2 * WIDE :]
        passed_ref[at, :] = jnp.where(on_low, turned(passed), passed).astype(BF16)
        third_ref[at, :] = jnp.where(on_low, turned(third), third).astype(BF16)


def project(at, rows, qkv_own, qkv_bias, tables):
    count = rows.shape[0]
    return pl.pallas_call(
        project_kernel,
        in_specs=[SMEM] + [VMEM] * 6,
        out_specs=[VMEM] * 3,
        out_shape=[shape_of((count, WIDE), BF16)] * 3,
        compiler_params=room(8),
        cost_estimate=cost(2 * count * D * 3 * WIDE, 4 * count * D),
    )(at, rows, qkv_own, qkv_bias, *tables)


def down_kernel(hidden_ref, low_ref, high_ref, cot_ref, first_ref, second_ref):
    half, half_d = low_ref.shape[0], low_ref.shape[1] // 2
    cot_ref[:half, :] = low_ref[...]
    cot_ref[half:, :] = high_ref[...]
    first_ref[...] = dot_over(hidden_ref[...], cot_ref[:, :half_d], (0, 0)).astype(BF16)
    second_ref[...] = dot_over(hidden_ref[...], cot_ref[:, half_d:], (0, 0)).astype(BF16)


def grad_down_chunks(hidden, low, high):
    count, own = hidden.shape
    return pl.pallas_call(
        down_kernel,
        in_specs=[VMEM] * 3,
        out_specs=[VMEM] * 3,
        out_shape=[shape_of((count, D), BF16)] + [shape_of((own, D // 2), BF16)] * 2,
        compiler_params=room(10),
        cost_estimate=cost(2 * count * own * D, 6 * count * D),
    )(hidden, low, high)


def attention_kernel(
    at_ref, first_ref, third_ref, taken_ref, grad_ref, keep_ref, up_ref, down_ref, away_ref, here_ref
):
    length, width = keep_ref.shape
    on_low = at_ref[1] == 0
    lane = lax.broadcasted_iota(jnp.int32, (length, width), 1)
    causal = lax.broadcasted_iota(jnp.int32, (length, length), 0) >= lax.broadcasted_iota(
        jnp.int32, (length, length), 1
    )
    scale = 1.0 / math.sqrt(HD)
    half = ROT // 2

    def back(value):
        return (
            value * keep_ref[...]
            - pltpu.roll(value, width - half, 1) * up_ref[...]
            - pltpu.roll(value, half, 1) * down_ref[...]
        )

    for i in range(first_ref.shape[0] // length):
        rows = slice(i * length, (i + 1) * length)
        first, third, taken, grad = first_ref[rows, :], third_ref[rows, :], taken_ref[rows, :], grad_ref[rows, :]
        query = jnp.where(on_low, first, taken)
        keys = jnp.where(on_low, third, first)
        values = jnp.where(on_low, taken, third)
        zero = jnp.zeros_like(query)
        found = []
        for head in range(width // HD):
            mine = (lane >= head * HD) & (lane < (head + 1) * HD)
            scores = dot_over(jnp.where(mine, query, zero), keys, (1, 1)) * scale
            scores = jnp.where(causal, scores, -jnp.inf)
            row_max = jnp.max(scores, -1, keepdims=True)
            log_total = row_max + jnp.log(jnp.sum(jnp.exp(scores - row_max), -1, keepdims=True))
            probs = jnp.exp(scores - log_total)
            probs_b = probs.astype(BF16)
            attended = jnp.dot(probs_b, values, preferred_element_type=F32)
            grad_values = dot_over(probs_b, grad, (0, 0))
            grad_probs = dot_over(jnp.where(mine, grad, zero), values, (1, 1))
            inner = jnp.sum(probs * grad_probs, -1, keepdims=True)
            grad_scores = (probs * (grad_probs - inner) * scale).astype(BF16)
            grad_query = jnp.dot(grad_scores, keys, preferred_element_type=F32)
            grad_keys = dot_over(grad_scores, query, (0, 0))
            new = (attended, grad_query, grad_keys, grad_values)
            found = new if not found else tuple(jnp.where(mine, n, o) for n, o in zip(new, found))
        attended, grad_query, grad_keys, grad_values = found
        grad_query, grad_keys = back(grad_query), back(grad_keys)
        away_ref[rows, :width] = attended.astype(BF16)
        away_ref[rows, width:] = jnp.where(on_low, grad_values, grad_query).astype(BF16)
        here_ref[rows, :width] = jnp.where(on_low, grad_query, grad_keys).astype(BF16)
        here_ref[rows, width:] = jnp.where(on_low, grad_keys, grad_values).astype(BF16)


def heads_kernel(at_ref, mine_ref, theirs_ref, cot_ref, rows_ref, grad_ref):
    on_low = at_ref[1] == 0
    mine, theirs = mine_ref[:WIDE, :], theirs_ref[...]
    rows = jnp.concatenate([jnp.where(on_low, mine, theirs), jnp.where(on_low, theirs, mine)], 1)
    rows_ref[...] = rows
    grad_ref[...] = dot_over(cot_ref[...], rows, (1, 1)).astype(BF16)


def back_to_heads(at, mine, theirs, cot):
    return pl.pallas_call(
        heads_kernel,
        in_specs=[SMEM] + [VMEM] * 3,
        out_specs=[VMEM] * 2,
        out_shape=[shape_of((WIDE, D), BF16), shape_of((cot.shape[0], WIDE), BF16)],
        compiler_params=room(6),
        cost_estimate=cost(2 * cot.size * WIDE, 2 * cot.size),
    )(at, mine, theirs, cot)


def swapped(i):
    return i + 1 - 2 * (i % 2)


def attention(at, first, third, taken, grad, tables):
    count, width = first.shape
    length = tables[0].shape[0]
    block = pl.BlockSpec((2 * length, width), lambda i, s: (i, 0))
    other = pl.BlockSpec((2 * length, width), lambda i, s: (swapped(i), 0))
    table = pl.BlockSpec((length, width), lambda i, s: (0, 0))
    out = pl.BlockSpec((2 * length, 2 * width), lambda i, s: (i, 0))
    return pl.pallas_call(
        attention_kernel,
        grid_spec=pltpu.PrefetchScalarGridSpec(
            num_scalar_prefetch=1,
            grid=(count // (2 * length),),
            in_specs=[block, block, other, block] + [table] * 3,
            out_specs=[out, out],
        ),
        out_shape=[shape_of((count, 2 * width), BF16)] * 2,
        compiler_params=room(12),
        cost_estimate=cost(24 * count * length * width, 16 * count * width, 4 * count * length),
    )(at, first, third, taken, grad, *tables)


def branch_kernel(hidden_ref, away_ref, down_ref, out_rows_ref, kept_ref, sent_ref):
    half = kept_ref.shape[0]
    branches = jnp.dot(hidden_ref[...], down_ref[...], preferred_element_type=F32) + jnp.dot(
        away_ref[:, :WIDE], out_rows_ref[...], preferred_element_type=F32
    )
    kept_ref[...] = branches[:half]
    sent_ref[...] = branches[half:].astype(BF16)


def branch_sums(hidden, away, down_own, out_rows):
    count, own = hidden.shape
    return pl.pallas_call(
        branch_kernel,
        in_specs=[VMEM] * 4,
        out_specs=[VMEM] * 2,
        out_shape=[shape_of((count // 2, D), F32), shape_of((count // 2, D), BF16)],
        compiler_params=room(10),
        cost_estimate=cost(2 * count * D * (own + WIDE), 6 * count * D),
    )(hidden, away, down_own, out_rows)


def group_kernel(
    at_ref, low_ref, high_ref, cotangent_ref, gp_ref, away_ref, here_ref, other_ref, up_ref, qkv_ref, gains_ref,
    kept_ref, sent_ref, sums_ref, proj_ref, att_ref,
):
    on_low = at_ref[1] == 0
    gains = gains_ref[...]
    own = gp_ref.shape[1]
    rows = low_ref.shape[0] // 2
    total = lambda v: jnp.sum(v.astype(F32), 0, keepdims=True)
    sums = None
    for i in range(4):
        at, swap = slice(i * rows, (i + 1) * rows), swapped(i)
        away, here, other = away_ref[at, :], here_ref[at, :], other_ref[swap * rows : (swap + 1) * rows, :]
        attended, attended_other = away[:, :WIDE], other[:, :WIDE]
        proj = jnp.concatenate([here[:, :WIDE], other[:, WIDE:], here[:, WIDE:]], 1)
        proj_ref[at, :] = proj
        att_ref[at, :] = jnp.concatenate(
            [jnp.where(on_low, attended, attended_other), jnp.where(on_low, attended_other, attended)], 1
        )
        gp = gp_ref[at, :]
        grad_attn = dot_over(proj, qkv_ref[...], (1, 1))
        grad_feed = dot_over(gp, up_ref[...], (1, 1))
        source = low_ref if i < 2 else high_ref
        local = slice((i % 2) * rows, (i % 2 + 1) * rows)
        normed = normalise(source[local, :])
        grad_normed = grad_attn * gains[0:1] + grad_feed * gains[2:3]
        new = [
            total(grad_attn * normed),
            total(grad_attn),
            total(grad_feed * normed),
            total(grad_feed),
            total(gp),
            total(proj),
        ]
        sums = new if sums is None else [a + b for a, b in zip(sums, new)]
        if i < 2:
            kept_ref[local, :] = grad_normed
        else:
            sent_ref[local, :] = grad_normed.astype(BF16)
    last = jnp.concatenate([sums[4], sums[5], jnp.zeros((1, D - own - 3 * WIDE), F32)], 1)
    sums_ref[...] = jnp.concatenate(sums[:4] + [total(cotangent_ref[...]), last, jnp.zeros((2, D), F32)], 0)


def group_sums(at, low, high, cotangent, gp, away, here, other, up_own, qkv_own, gains):
    count, own = gp.shape
    return pl.pallas_call(
        group_kernel,
        in_specs=[SMEM] + [VMEM] * 10,
        out_specs=[VMEM] * 5,
        out_shape=[
            shape_of((count // 2, D), F32),
            shape_of((count // 2, D), BF16),
            shape_of((8, D), F32),
            shape_of((count, 3 * WIDE), BF16),
            shape_of((count, 2 * WIDE), BF16),
        ],
        compiler_params=room(12),
        cost_estimate=cost(2 * count * D * (own + 3 * WIDE), 16 * count * D),
    )(at, low, high, cotangent, gp, away, here, other, up_own, qkv_own, gains)


def mixed_kernel(at_ref, rows_ref, proj_ref, att_ref, cot_ref, *refs):
    out_ref = refs[-1]
    out_ref[: 4 * WIDE, : 3 * WIDE] = dot_over(rows_ref[...], proj_ref[...], (0, 0)).astype(BF16)
    heads = dot_over(att_ref[...], cot_ref[...], (0, 0)).astype(BF16)
    out_ref[: 2 * WIDE, 3 * WIDE :] = heads[:, :WIDE]
    out_ref[2 * WIDE : 4 * WIDE, 3 * WIDE :] = heads[:, WIDE:]
    if len(refs) > 1:
        sums, other = refs[0][...], refs[1][...]
        row = lax.broadcasted_iota(jnp.int32, sums.shape, 0)
        sums = jnp.where(row < 5, sums + other, sums).astype(BF16)
        out_ref[4 * WIDE :, :] = jnp.concatenate([sums[:, : D // 2], sums[:, D // 2 :]], 0)


def mixed(at, half, rows, proj, att, cot, small):
    count = rows.shape[0]
    fixed = lambda i, s: (0, 0)
    tall = 4 * WIDE + (16 if small else 0)
    return pl.pallas_call(
        mixed_kernel,
        grid_spec=pltpu.PrefetchScalarGridSpec(
            num_scalar_prefetch=1,
            grid=(1,),
            in_specs=[
                pl.BlockSpec((count, 4 * WIDE), lambda i, s: (0, half)),
                pl.BlockSpec(proj.shape, fixed),
                pl.BlockSpec(att.shape, fixed),
                pl.BlockSpec((count, 2 * WIDE), lambda i, s: (0, 2 * s[1] + half)),
            ]
            + [pl.BlockSpec((8, D), fixed)] * len(small),
            out_specs=pl.BlockSpec((tall, 4 * WIDE), fixed),
        ),
        out_shape=shape_of((tall, 4 * WIDE), BF16),
        compiler_params=room(12),
        cost_estimate=cost(2 * count * 16 * WIDE * WIDE, 4 * count * D),
    )(at, rows, proj, att, cot, *small)


TALL = 528


def turn(at, grad, from_z, first, from_middle, following, carried, from_y):
    outs = []
    given = dict(
        grad=grad, from_z=from_z, first=first, from_middle=from_middle, following=following, carried=carried, from_y=from_y
    )
    names = [n for n, v in given.items() if v is not None]
    if grad is not None:
        outs.append(("first", grad.shape))
    if first is not None or following is not None:
        outs.append(("next", (following if following is not None else first).shape))
    if carried is not None:
        plain = carried.shape[0] < TALL or following is not None or grad is not None
        outs.append(("total", (512, 512) if plain else carried.shape))
    if carried is not None or from_y is not None:
        outs.append(("pair", (2 * TALL, 512)))

    def kernel(at_ref, *refs):
        values = dict(zip(names, refs))
        results = dict(zip([n for n, _ in outs], refs[len(names) :]))
        middle = at_ref[2] == 1
        if "first" in results:
            results["first"][...] = values["grad"][...] + values["from_z"][...]
        if "next" in results:
            out = results["next"]
            if "first" in values:
                tall = values["first"].shape[0]
                summed = values["first"][...] + values["from_middle"][...]
                if "following" in values:
                    out[:tall, :] = jnp.where(middle, summed, values["following"][:tall, :])
                    if out.shape[0] > tall:
                        out[tall:, :] = values["following"][tall:, :]
                else:
                    out[...] = summed
            else:
                out[...] = values["following"][...]
        if "total" in results:
            tall = results["total"].shape[0]
            total = jnp.where(middle, values["carried"][:tall, :], values["from_z"][:tall, :])
            results["total"][...] = total
            results["pair"][:tall, :] = total
            if tall < TALL:
                results["pair"][tall:TALL, :] = jnp.zeros((TALL - tall, 512), BF16)
        elif "pair" in results:
            results["pair"][:TALL, :] = jnp.zeros((TALL, 512), BF16)
        if "pair" in results:
            tall = values["from_y"].shape[0] if "from_y" in values else 0
            if tall:
                results["pair"][TALL : TALL + tall, :] = values["from_y"][...]
            if tall < TALL:
                results["pair"][TALL + tall :, :] = jnp.zeros((TALL - tall, 512), BF16)

    made = pl.pallas_call(
        kernel,
        in_specs=[SMEM] + [VMEM] * len(names),
        out_specs=[VMEM] * len(outs),
        out_shape=[shape_of(s, BF16) for _, s in outs],
        compiler_params=room(6),
        cost_estimate=cost(len(names) * 2**18, (len(names) + len(outs)) * 2**19),
    )(at, *[given[n] for n in names])
    return dict(zip([n for n, _ in outs], made))


def place(at, pieces, into, shapes, copies):
    count = len(shapes)
    each = len(copies(0))
    tall = 4 * WIDE

    def kernel(at_ref, *refs):
        piece_refs = refs[:4]
        out_refs = refs[4 + (count if into else 0) :][:count]
        wide_ref, sems = refs[-2:]
        started = []
        for i in range(4):
            base = TALL if i == 3 else 0
            wide_ref[i] = piece_refs[i][base : base + tall, :].astype(F32)
            for n, (which, at, part) in enumerate(copies(at_ref[3 + i])):
                copy = pltpu.make_async_copy(wide_ref.at[i].at[part], out_refs[which].at[at], sems.at[i * each + n])
                copy.start()
                started.append(copy)
        for copy in started:
            copy.wait()

    any_space = pl.BlockSpec(memory_space=pl.ANY)
    return pl.pallas_call(
        kernel,
        in_specs=[SMEM] + [VMEM] * 4 + [any_space] * len(into or ()),
        out_specs=[any_space] * count,
        scratch_shapes=[pltpu.VMEM((4, tall, tall), F32), pltpu.SemaphoreType.DMA((4 * each,))],
        out_shape=[shape_of(s, F32) for s in shapes],
        compiler_params=room(8),
        input_output_aliases={5 + k: k for k in range(count)} if into else {},
        cost_estimate=cost(0, 24 * tall * tall),
    )(at, *pieces, *(into or ()))


def fold_kernel(kept_ref, got_ref, stay_ref, go_ref):
    rows = stay_ref.shape[0]
    stay_ref[...] = kept_ref[:rows, :] + got_ref[:rows, :].astype(F32)
    go_ref[...] = (kept_ref[rows:, :] + got_ref[rows:, :].astype(F32)).astype(BF16)


def fold(kept, got):
    rows = kept.shape[0] // 2
    return pl.pallas_call(
        fold_kernel,
        in_specs=[VMEM] * 2,
        out_specs=[VMEM] * 2,
        out_shape=[shape_of((rows, D), F32), shape_of((rows, D), BF16)],
        compiler_params=room(4),
        cost_estimate=cost(kept.size, 9 * kept.size),
    )(kept, got)


def last_kernel(inputs_ref, cotangent_ref, gains_ref, a_ref, b_ref, c_ref, d_ref, outputs_ref, grad_ref):
    resid = inputs_ref[...].astype(F32)
    row_mean = jnp.mean(resid, -1, keepdims=True)
    centered = resid - row_mean
    inv_std = lax.rsqrt(jnp.mean(centered * centered, -1, keepdims=True) + norm_eps)
    normed = centered * inv_std
    branches = a_ref[...] + b_ref[...].astype(F32)
    outputs_ref[...] = (resid + branches + (gains_ref[4:5] + gains_ref[5:6])).astype(BF16)
    grad_normed = c_ref[...] + d_ref[...].astype(F32)
    grad_ref[...] = cotangent_ref[...].astype(F32) + inv_std * (
        grad_normed
        - jnp.mean(grad_normed, -1, keepdims=True)
        - normed * jnp.mean(grad_normed * normed, -1, keepdims=True)
    )


def last(inputs, cotangent, gains, *sums):
    return pl.pallas_call(
        last_kernel,
        in_specs=[VMEM] * 7,
        out_specs=[VMEM] * 2,
        out_shape=[shape_of(inputs.shape, BF16), shape_of(inputs.shape, F32)],
        compiler_params=room(4),
        cost_estimate=cost(inputs.size * 20, inputs.size * 20),
    )(inputs, cotangent, gains, *sums)


def at_blocks(first, size):
    return pl.ds(pl.multiple_of(first, size), size)


def small_kernel(at_ref, a_ref, b_ref, c_ref, d_ref, g1, s1, g2, s2, ob, up_ref, qkv_ref):
    on_low = at_ref[1] == 0
    parts = [r[...].astype(F32) for r in (a_ref, b_ref, c_ref, d_ref)]
    sums = (parts[0] + parts[1]) + (parts[2] + parts[3])
    sums = jnp.where(on_low, sums[:8], sums[8:])
    for row, ref in enumerate((g1, s1, g2, s2, ob)):
        ref[...] = sums[row : row + 1]
    for i, part in enumerate(parts):
        p = at_ref[3 + i]
        up_ref[pl.ds(p, 1), :] = part[5:6]
        for n in range(3):
            qkv_ref[pl.ds(4 * n + p, 1), :] = part[13:14, n * WIDE : (n + 1) * WIDE]


def small_outputs(at, pieces):
    fixed = lambda i, s: (0, 0)
    half_d = D // 2
    return pl.pallas_call(
        small_kernel,
        grid_spec=pltpu.PrefetchScalarGridSpec(
            num_scalar_prefetch=1,
            grid=(1,),
            in_specs=[pl.BlockSpec((16, half_d), lambda i, s: (32, 0))] * 3
            + [pl.BlockSpec((16, half_d), lambda i, s: (TALL // 16 + 32, 0))],
            out_specs=[pl.BlockSpec((1, half_d), fixed)] * 5
            + [pl.BlockSpec((4, half_d), fixed), pl.BlockSpec((12, WIDE), fixed)],
        ),
        compiler_params=room(2),
        out_shape=[shape_of((1, half_d), F32)] * 5 + [shape_of((4, half_d), F32), shape_of((12, WIDE), F32)],
    )(at, *pieces)


def fast_body(
    inputs,
    attn_gain,
    attn_shift,
    feed_gain,
    feed_shift,
    qkv_weight,
    qkv_bias,
    out_weight,
    out_bias,
    up_weight,
    up_bias,
    down_weight,
    down_bias,
    cotangent,
):
    length = inputs.shape[0]
    rep, x = lax.axis_index("rep"), lax.axis_index("shard")
    z, y, c = rep // 4, rep // 2 % 2, rep % 2
    part = y * 2 + c
    middle = ((z == 1) | (z == 2)).astype(jnp.int32)
    at = jnp.stack([part, x, middle, part, part ^ 2, part ^ 1, part ^ 3, part]).astype(jnp.int32)
    fence = lax.optimization_barrier
    half_d = D // 2
    tables = rotary_arrays(length)
    vectors = [attn_gain, attn_shift, feed_gain, feed_shift, out_bias, down_bias]
    own = up_weight.shape[1] // 4

    from_y, from_xy = send(inputs, TO_Y), send(inputs, TO_XY)
    mine, packed, their_rows = pack(at, inputs, out_weight, vectors)
    from_x = send(packed, TO_X)
    cot_first, mine = fence((cotangent, mine))
    cot_parts = [send(cot_first, p) for p in (TO_Y, TO_X, TO_XY)]
    up_own, down_own, qkv_own = own_weights(at, up_weight, down_weight, qkv_weight)
    from_x, from_y, from_xy, up_own, down_own, qkv_own = fence((from_x, from_y, from_xy, up_own, down_own, qkv_own))
    low = stack(inputs, from_y, from_x, from_xy)
    theirs = from_x
    high = send(low, TO_CORE)
    cot_parts, low = fence((cot_parts, low))
    low_cot = stack(cotangent, *cot_parts)
    high_cot = send(low_cot, TO_CORE)
    attn_in, feed_in, hidden, slope, gains = front(
        at, low, high, mine, theirs, up_own, up_bias.reshape(4, -1)
    )
    cot, chunk0, chunk1 = grad_down_chunks(hidden, low_cot, high_cot)

    env = dict(
        attn_in=attn_in, feed_in=feed_in, hidden=hidden, slope=slope, cot=cot,
        qkv_own=qkv_own, mine=mine, their_rows=their_rows, gains=gains, low=low, high=high, down_own=down_own, up_own=up_own,
    )
    chunks = {0: chunk0, 1: chunk1}
    loose = {}

    def after(step, env):
        e = dict(env)
        if step == 0:
            e["first"], passed, e["third"] = project(
                at, e["attn_in"], e["qkv_own"], qkv_bias.reshape(12, -1), tables
            )
            e["taken"] = send(passed, TO_X)
            e["rows"] = send(e.pop("their_rows"), TO_X)
            gp = dot_over(e["cot"], e["down_own"], (1, 1)) * e.pop("slope")
            e["gp"] = gp.astype(BF16)
            chunks[2] = dot_over(e["feed_in"][:, :half_d], e["gp"], (0, 0)).astype(BF16)
        if step == 1:
            e["out_rows"], e["ga"] = back_to_heads(at, e.pop("mine"), e.pop("rows"), e["cot"])
            e["away"], e["here"] = attention(
                at, e.pop("first"), e.pop("third"), e.pop("taken"), e.pop("ga"), tables
            )
            chunks[3] = dot_over(e.pop("feed_in")[:, half_d:], e["gp"], (0, 0)).astype(BF16)
            e["kb"], e["sb"] = branch_sums(e.pop("hidden"), e["away"], e.pop("down_own"), e.pop("out_rows"))
        if step == 2:
            e["other"] = send(e["away"], TO_X)
            e["kb"], e["sb"] = fold(e["kb"], send(e["sb"], TO_CORE))
        if step == 3:
            e["kg"], e["sg"], e["sums"], e["proj"], e["att"] = group_sums(
                at, e.pop("low"), e.pop("high"), cotangent, e.pop("gp"), e.pop("away"), e.pop("here"),
                e.pop("other"), e.pop("up_own"), e.pop("qkv_own"), e["gains"],
            )
            chunks[4] = mixed(at, 0, e["attn_in"], e["proj"], e["att"], e["cot"], ())
            e["kb"], e["sb"] = fold(e["kb"], send(e["sb"], TO_X))
        if step == 4:
            other = send(e["sums"], TO_X)
            chunks[5] = mixed(
                at, 1, e.pop("attn_in"), e.pop("proj"), e.pop("att"), e.pop("cot"), (e.pop("sums"), other)
            )
        if step == 5:
            e["kg"], e["sg"] = fold(e["kg"], send(e["sg"], TO_CORE))
        if step == 6:
            e["kg"], e["sg"] = fold(e["kg"], send(e["sg"], TO_X))
        if step == Y_RETURN - 1:
            e["gb"] = send(e.pop("sb"), TO_Y)
        if step == Y_RETURN:
            loose["g"] = send(e.pop("sg"), TO_Y)
        return e

    count = 6
    operand, one, total, over_y, pair, got_pair = {}, {}, {}, {}, {}, {}
    outs = {}
    operand[0] = chunks[0]

    def finish(k):
        pieces = [total.pop(k), over_y.pop(k), got_pair.pop(k), got_pair[k + 1]]
        h = k % 2
        rows, columns = pl.ds(h * half_d, half_d), pl.ds(h * half_d, half_d)
        everything = (slice(None), slice(None))
        if k < 2:
            outs["down"] = place(
                at, pieces, outs.get("down"), [down_weight.shape],
                lambda p: [(0, (at_blocks(own * p, own), columns), everything)],
            )
        elif k < 4:
            outs["up"] = place(
                at, pieces, outs.get("up"), [up_weight.shape],
                lambda p: [(0, (rows, at_blocks(own * p, own)), everything)],
            )
        else:
            outs["attn"] = place(
                at, pieces, outs.get("attn"), [qkv_weight.shape, out_weight.shape],
                lambda p: [
                    (0, (rows, at_blocks(half_d * n + WIDE * p, WIDE)), (slice(None), pl.ds(n * WIDE, WIDE)))
                    for n in range(3)
                ]
                + [
                    (
                        1,
                        (at_blocks(half_d * side + WIDE * p, WIDE), pl.ds((2 * h + b) * WIDE, WIDE)),
                        (pl.ds((2 * b + side) * WIDE, WIDE), pl.ds(3 * WIDE, WIDE)),
                    )
                    for b in range(2)
                    for side in range(2)
                ],
            )
        if k == count - 1:
            outs["small"] = small_outputs(at, pieces)

    for step in range(count + 5):
        live = (env, chunks, operand, one, total, over_y, pair, got_pair, outs)
        env, chunks, operand, one, total, over_y, pair, got_pair, outs = fence(live)
        got = {}
        if 0 <= step - 1 < count:
            got["m"] = send(one[step - 1], MIDDLE)
        if step < count + 2:
            pairs = (INWARD if step < count else []) + (OUTWARD if step >= 2 else [])
            got["z"] = send(operand[step], pairs)
        if 0 <= step - 3 < count:
            got["y"] = send(total[step - 3], TO_Y)
        if step - 3 in pair:
            got["c"] = send(pair.pop(step - 3), TO_CORE)
        env = after(step, env)
        if 0 <= step - 5 < count:
            finish(step - 5)
        if step < count + 3:
            made = turn(
                at,
                chunks.pop(step) if step < count else None,
                got.get("z"),
                one.pop(step - 1) if 0 <= step - 1 < count else None,
                got.get("m"),
                chunks.get(step + 1),
                operand.pop(step) if 2 <= step < count + 2 else None,
                got.get("y"),
            )
            if "first" in made:
                one[step] = made["first"]
            if "next" in made:
                operand[step + 1] = made["next"]
            if "total" in made:
                total[step - 2] = made["total"]
            if "pair" in made:
                pair[step - 2] = made["pair"]
        if "y" in got:
            over_y[step - 3] = got["y"]
        if "c" in got:
            got_pair[step - 3] = got["c"]

    outputs, input_grad = last(inputs, cotangent, env["gains"], env["kb"], env["gb"], env["kg"], loose["g"])
    g1, s1, g2, s2, ob, up_b, qkv_b = outs["small"]
    flat = lambda a: a.reshape(-1)
    return (
        outputs,
        input_grad,
        flat(g1),
        flat(s1),
        flat(g2),
        flat(s2),
        outs["attn"][0],
        flat(qkv_b),
        outs["attn"][1],
        flat(ob),
        outs["up"][0],
        flat(up_b),
        outs["down"][0],
        flat(ob),
    )


def choose_body(mesh):
    known = {"rep": Z * Y * C, "shard": X}
    return fast_body if dict(mesh.shape) == known else general_body


def solution(mesh):
    return jax.shard_map(
        choose_body(mesh),
        mesh=mesh,
        in_specs=(
            P(("rep", "shard"), None),
            P("shard"),
            P("shard"),
            P("shard"),
            P("shard"),
            P(None, "shard"),
            P("shard"),
            P(None, "shard"),
            P("shard"),
            P(None, "shard"),
            P("shard"),
            P("shard", None),
            P("shard"),
            P(("rep", "shard"), None),
        ),
        out_specs=(
            P(("rep", "shard"), None),
            P(("rep", "shard"), None),
            P("shard"),
            P("shard"),
            P("shard"),
            P("shard"),
            P(None, "shard"),
            P("shard"),
            P(None, "shard"),
            P("shard"),
            P(None, "shard"),
            P("shard"),
            P("shard", None),
            P("shard"),
        ),
        check_vma=False,
    )
```

```python
import math

import jax
import jax.numpy as jnp
import numpy as np
from jax import lax
from jax.experimental import pallas as pl
from jax.experimental.pallas import tpu as pltpu
from jax.sharding import PartitionSpec as P

D = 1024
H = 16
HD = 64
ROT = 16


norm_eps = 1e-05
base_freq = 10000.0


def rotary_tables(length, rotary_dims):
    half_dims = rotary_dims // 2
    positions = jnp.arange(length).astype(jnp.float32)
    inverse = jnp.exp(
        jnp.arange(half_dims).astype(jnp.float32) * (-2.0 * math.log(base_freq) / rotary_dims)
    )
    angles = positions[:, None] * inverse[None, :]
    return (jnp.cos(angles), jnp.sin(angles))


def rotate(values, cosine, sine_table, rotary_dims, direction):
    half_dims = rotary_dims // 2
    lower_half = values[..., :half_dims]
    upper_half = values[..., half_dims:rotary_dims]
    cosine_row = cosine[:, None, :]
    sine_row = sine_table[:, None, :] * direction
    return jnp.concatenate(
        [
            lower_half * cosine_row - upper_half * sine_row,
            upper_half * cosine_row + lower_half * sine_row,
            values[..., rotary_dims:],
        ],
        axis=-1,
    )


def gelu_slope(preact):
    normal_cdf = 0.5 * (1.0 + jax.scipy.special.erf(preact * (1.0 / math.sqrt(2.0))))
    return normal_cdf + preact * jnp.exp(-0.5 * preact * preact) * (1.0 / math.sqrt(2.0 * math.pi))


def general_body(
    inputs,
    attn_gain,
    attn_shift,
    feed_gain,
    feed_shift,
    qkv_weight,
    qkv_bias,
    out_weight,
    out_bias,
    up_weight,
    up_bias,
    down_weight,
    down_bias,
    cotangent,
):
    (
        gain_one,
        shift_one,
        gain_two,
        shift_two,
        out_bias_all,
        down_bias_all,
        qkv_all,
        qkv_bias_all,
        out_all,
    ) = (
        lax.all_gather(attn_gain, "shard", axis=0, tiled=True),
        lax.all_gather(attn_shift, "shard", axis=0, tiled=True),
        lax.all_gather(feed_gain, "shard", axis=0, tiled=True),
        lax.all_gather(feed_shift, "shard", axis=0, tiled=True),
        lax.all_gather(out_bias, "shard", axis=0, tiled=True),
        lax.all_gather(down_bias, "shard", axis=0, tiled=True),
        lax.all_gather(qkv_weight, "shard", axis=1, tiled=True),
        lax.all_gather(qkv_bias, "shard", axis=0, tiled=True),
        lax.all_gather(out_weight, "shard", axis=1, tiled=True),
    )
    gain_one = gain_one.astype(jnp.float32)
    gain_two = gain_two.astype(jnp.float32)
    length = inputs.shape[0]
    resid = inputs.astype(jnp.float32)
    row_mean = jnp.mean(resid, -1, keepdims=True)
    centered = resid - row_mean
    inv_std = lax.rsqrt(jnp.mean(centered * centered, -1, keepdims=True) + norm_eps)
    normed = centered * inv_std
    attn_in = (normed * gain_one + shift_one.astype(jnp.float32)).astype(jnp.bfloat16)
    feed_in = (normed * gain_two + shift_two.astype(jnp.float32)).astype(jnp.bfloat16)
    projected = jnp.dot(attn_in, qkv_all, preferred_element_type=jnp.float32) + qkv_bias_all.astype(
        jnp.float32
    )
    projected = projected.reshape(length, 3, H, HD)
    cosine, sine_table = rotary_tables(length, ROT)
    query_rot = rotate(projected[:, 0], cosine, sine_table, ROT, 1.0).astype(jnp.bfloat16)
    keys_rot = rotate(projected[:, 1], cosine, sine_table, ROT, 1.0).astype(jnp.bfloat16)
    values_b = projected[:, 2].astype(jnp.bfloat16)
    score_scale = 1.0 / math.sqrt(HD)
    row_block = min(512, length)
    block_count = length // row_block
    key_positions = jnp.arange(length)

    def block_scores(row_start, q_rows):
        scores = (
            jnp.einsum("qhd,khd->hqk", q_rows, keys_rot, preferred_element_type=jnp.float32)
            * score_scale
        )
        causal = (row_start + jnp.arange(row_block))[:, None] >= key_positions[None, :]
        return jnp.where(causal[None], scores, -jnp.inf)

    def forward_block(block_index):
        row_start = block_index * row_block
        scores = block_scores(row_start, query_rot)
        row_max = jnp.max(scores, -1, keepdims=True)
        log_total = row_max + jnp.log(jnp.sum(jnp.exp(scores - row_max), -1, keepdims=True))
        attn_probs = jnp.exp(scores - log_total).astype(jnp.bfloat16)
        block_out = jnp.einsum(
            "hqk,khd->qhd", attn_probs, values_b, preferred_element_type=jnp.float32
        )
        return (block_out.astype(jnp.bfloat16), log_total)

    attended, log_totals = lax.map(forward_block, jnp.arange(block_count))
    attended = attended.reshape(length, D)
    attn_out = jnp.dot(attended, out_all, preferred_element_type=jnp.float32) + out_bias_all.astype(
        jnp.float32
    )
    group_in = lax.all_gather(feed_in, "shard", axis=0, tiled=True)
    preact = jnp.dot(group_in, up_weight, preferred_element_type=jnp.float32) + up_bias.astype(
        jnp.float32
    )
    hidden = jax.nn.gelu(preact, approximate=False).astype(jnp.bfloat16)
    rows_in = hidden
    feed_out = lax.psum_scatter(
        jnp.dot(rows_in, down_weight, preferred_element_type=jnp.float32),
        "shard",
        scatter_dimension=0,
        tiled=True,
    ) + down_bias_all.astype(jnp.float32)
    outputs = (resid + attn_out + feed_out).astype(jnp.bfloat16)
    grad_top = cotangent.astype(jnp.float32)
    attn_group, attended_group, out_back = (
        lax.all_gather(attn_in, "shard", axis=0, tiled=True),
        lax.all_gather(attended, "shard", axis=0, tiled=True),
        lax.all_gather(out_weight, "shard", axis=1, tiled=True),
    )
    grad_cols = lax.all_to_all(cotangent, "shard", split_axis=1, concat_axis=0, tiled=True)
    grad_bias = jnp.sum(grad_cols.astype(jnp.float32), 0)
    grad_out_w = jnp.dot(attended_group.T, grad_cols, preferred_element_type=jnp.float32)
    grad_attended = (
        jnp.dot(cotangent, out_back.T, preferred_element_type=jnp.float32)
        .astype(jnp.bfloat16)
        .reshape(length, H, HD)
    )
    group_grad = lax.all_gather(cotangent, "shard", axis=0, tiled=True)
    grad_down = jnp.dot(hidden.T, group_grad, preferred_element_type=jnp.float32)
    grad_preact = jnp.dot(
        group_grad, down_weight.T, preferred_element_type=jnp.float32
    ) * gelu_slope(preact)
    grad_up_b = jnp.sum(grad_preact, 0)
    grad_preact_b = grad_preact.astype(jnp.bfloat16)
    grad_up = jnp.dot(group_in.T, grad_preact_b, preferred_element_type=jnp.float32)
    rows_in = grad_preact_b
    grad_feed_in = lax.psum_scatter(
        jnp.dot(rows_in, up_weight.T, preferred_element_type=jnp.float32),
        "shard",
        scatter_dimension=0,
        tiled=True,
    )

    def backward_block(carry, block_index):
        grad_keys, grad_values = carry
        row_start = block_index * row_block
        scores = block_scores(row_start, query_rot)
        probs_f = jnp.exp(scores - log_totals[block_index])
        probs_b = probs_f.astype(jnp.bfloat16)
        grad_values = grad_values + jnp.einsum(
            "hqk,qhd->khd", probs_b, grad_attended, preferred_element_type=jnp.float32
        )
        grad_probs = jnp.einsum(
            "qhd,khd->hqk", grad_attended, values_b, preferred_element_type=jnp.float32
        )
        grad_scores = (
            probs_f * (grad_probs - jnp.sum(probs_f * grad_probs, -1, keepdims=True)) * score_scale
        )
        grad_scores_b = grad_scores.astype(jnp.bfloat16)
        grad_qrot = jnp.einsum(
            "hqk,khd->qhd", grad_scores_b, keys_rot, preferred_element_type=jnp.float32
        )
        grad_keys = grad_keys + jnp.einsum(
            "hqk,qhd->khd", grad_scores_b, query_rot, preferred_element_type=jnp.float32
        )
        return ((grad_keys, grad_values), grad_qrot)

    empty_heads = jnp.zeros((length, H, HD), jnp.float32)
    (grad_krot, grad_values), grad_qrot = lax.scan(
        backward_block, (empty_heads, empty_heads), jnp.arange(block_count)
    )
    grad_qrot = grad_qrot.reshape(length, H, HD)
    grad_query = rotate(grad_qrot, cosine, sine_table, ROT, -1.0)
    grad_keys = rotate(grad_krot, cosine, sine_table, ROT, -1.0)
    grad_proj = jnp.stack([grad_query, grad_keys, grad_values], axis=1).reshape(length, 3 * D)
    grad_qkv_b = jnp.sum(grad_proj, 0)
    grad_proj_b = grad_proj.astype(jnp.bfloat16)
    proj_cols = lax.all_to_all(grad_proj_b, "shard", split_axis=1, concat_axis=0, tiled=True)
    grad_qkv = jnp.dot(attn_group.T, proj_cols, preferred_element_type=jnp.float32)
    rows_in = proj_cols
    grad_attn_in = lax.psum_scatter(
        jnp.dot(rows_in, qkv_weight.T, preferred_element_type=jnp.float32),
        "shard",
        scatter_dimension=0,
        tiled=True,
    )
    grad_gain_one = jnp.sum(grad_attn_in * normed, 0)
    grad_shift_one = jnp.sum(grad_attn_in, 0)
    grad_gain_two = jnp.sum(grad_feed_in * normed, 0)
    grad_shift_two = jnp.sum(grad_feed_in, 0)
    grad_normed = grad_attn_in * gain_one + grad_feed_in * gain_two
    input_grad = grad_top + inv_std * (
        grad_normed
        - jnp.mean(grad_normed, -1, keepdims=True)
        - normed * jnp.mean(grad_normed * normed, -1, keepdims=True)
    )
    grad_qkv_b, grad_gain_one, grad_shift_one, grad_gain_two, grad_shift_two = (
        lax.psum_scatter(grad_qkv_b, "shard", scatter_dimension=0, tiled=True),
        lax.psum_scatter(grad_gain_one, "shard", scatter_dimension=0, tiled=True),
        lax.psum_scatter(grad_shift_one, "shard", scatter_dimension=0, tiled=True),
        lax.psum_scatter(grad_gain_two, "shard", scatter_dimension=0, tiled=True),
        lax.psum_scatter(grad_shift_two, "shard", scatter_dimension=0, tiled=True),
    )
    (
        grad_gain_one,
        grad_shift_one,
        grad_gain_two,
        grad_shift_two,
        grad_qkv,
        grad_qkv_b,
        grad_out_w,
        grad_bias,
        grad_up,
        grad_up_b,
        grad_down,
    ) = lax.psum(
        (
            grad_gain_one,
            grad_shift_one,
            grad_gain_two,
            grad_shift_two,
            grad_qkv,
            grad_qkv_b,
            grad_out_w,
            grad_bias,
            grad_up,
            grad_up_b,
            grad_down,
        ),
        "rep",
    )
    return (
        outputs,
        input_grad,
        grad_gain_one,
        grad_shift_one,
        grad_gain_two,
        grad_shift_two,
        grad_qkv,
        grad_qkv_b,
        grad_out_w,
        grad_bias,
        grad_up,
        grad_up_b,
        grad_down,
        grad_bias,
    )


AXES = ("rep", "shard")
Z, Y, C, X = 4, 2, 2, 2


def moves(target):
    pairs = []
    for z in range(Z):
        for y in range(Y):
            for c in range(C):
                for x in range(X):
                    to = target(z, y, c, x)
                    if to is not None:
                        to_z, to_y, to_c, to_x = to
                        source = ((z * Y + y) * C + c) * X + x
                        pairs.append((source, ((to_z * Y + to_y) * C + to_c) * X + to_x))
    return pairs


TO_CORE = moves(lambda z, y, c, x: (z, y, 1 - c, x))
TO_X = moves(lambda z, y, c, x: (z, y, c, 1 - x))
TO_Y = moves(lambda z, y, c, x: (z, 1 - y, c, x))
TO_XY = moves(lambda z, y, c, x: (z, 1 - y, c, 1 - x))
INWARD = moves(lambda z, y, c, x: {0: (1, y, c, x), 3: (2, y, c, x)}.get(z))
MIDDLE = moves(lambda z, y, c, x: {1: (2, y, c, x), 2: (1, y, c, x)}.get(z))
OUTWARD = moves(lambda z, y, c, x: {1: (0, y, c, x), 2: (3, y, c, x)}.get(z))

WIDE = 2 * HD
BF16, F32 = jnp.bfloat16, jnp.float32
Y_RETURN = 8


def send(value, pairs):
    return lax.ppermute(value, AXES, pairs)


def dot_over(a, b, dims):
    return lax.dot_general(a, b, ((dims[:1], dims[1:]), ((), ())), preferred_element_type=F32)


def shape_of(shape, dtype):
    return jax.ShapeDtypeStruct(tuple(shape), dtype)


def room(mebibytes):
    return pltpu.CompilerParams(vmem_limit_bytes=mebibytes * 2**20)


VMEM = pl.BlockSpec(memory_space=pltpu.VMEM)
ANY = pl.BlockSpec(memory_space=pltpu.HBM)
SMEM = pl.BlockSpec(memory_space=pltpu.SMEM)


def cost(flops, moved, transcendentals=0):
    return pl.CostEstimate(flops=int(flops), bytes_accessed=int(moved), transcendentals=int(transcendentals))


def rotary_arrays(length):
    half = ROT // 2
    angles = np.arange(length, dtype=np.float32)[:, None] * np.exp(
        np.arange(half, dtype=np.float32) * np.float32(-2.0 * math.log(base_freq) / ROT)
    )
    keep = np.ones((length, HD), np.float32)
    up = np.zeros((length, HD), np.float32)
    down = np.zeros((length, HD), np.float32)
    keep[:, :half] = keep[:, half:ROT] = np.cos(angles)
    up[:, :half] = -np.sin(angles)
    down[:, half:ROT] = np.sin(angles)
    return [jnp.asarray(np.tile(t, (1, 2))) for t in (keep, up, down)]


def pack_kernel(at_ref, inputs_ref, rows_ref, *refs):
    vector_refs, (mine_ref, sent_ref, rows_out_ref), line_refs, sems = refs[:6], refs[6:9], refs[9:15], refs[15]
    part, x = at_ref[0], at_ref[1]
    length, columns = inputs_ref.shape[0], mine_ref.shape[1]
    rows_of = lambda first, count: rows_ref.at[pl.ds(pl.multiple_of(first, WIDE), count), :]
    mine_at, their_at = (4 * x + part) * WIDE, (4 * (1 - x) + part) * WIDE
    copies = [
        pltpu.make_async_copy(inputs_ref, sent_ref.at[pl.ds(0, length), :], sems.at[0]),
        pltpu.make_async_copy(rows_of(mine_at, WIDE), mine_ref.at[pl.ds(0, WIDE), :], sems.at[1]),
    ]
    copies.append(pltpu.make_async_copy(rows_of(their_at, WIDE), rows_out_ref, sems.at[2]))
    for n, ref in enumerate(vector_refs):
        copies.append(pltpu.make_async_copy(ref, line_refs[n], sems.at[3 + n]))
    for copy in copies:
        copy.start()
    for copy in copies:
        copy.wait()
    lines = [ref[...][None, :] for ref in line_refs]
    lines.append(jnp.zeros((10, columns), BF16))
    tail = jnp.concatenate(lines, 0)
    mine_ref[WIDE:, :] = tail
    sent_ref[length:, :columns] = tail
    sent_ref[length:, columns:] = jnp.zeros_like(tail)


def pack(at, inputs, out_weight, vectors):
    columns = out_weight.shape[1]
    return pl.pallas_call(
        pack_kernel,
        in_specs=[SMEM] + [ANY] * 8,
        out_specs=[VMEM] * 3,
        out_shape=[
            shape_of((WIDE + 16, columns), BF16),
            shape_of((inputs.shape[0] + 16, 2 * columns), BF16),
            shape_of((WIDE, columns), BF16),
        ],
        scratch_shapes=[pltpu.VMEM((columns,), BF16)] * 6 + [pltpu.SemaphoreType.DMA((9,))],
        compiler_params=room(60),
        cost_estimate=cost(0, 0),
    )(at, inputs, out_weight, *vectors)


def stack_kernel(a_ref, b_ref, c_ref, d_ref, out_ref):
    rows = a_ref.shape[0]
    for n, ref in enumerate((a_ref, b_ref, c_ref, d_ref)):
        out_ref[n * rows : (n + 1) * rows, :] = ref[:rows, :]


def stack(*parts):
    rows, columns = parts[0].shape
    return pl.pallas_call(
        stack_kernel,
        in_specs=[VMEM] * 4,
        out_specs=VMEM,
        out_shape=shape_of((4 * rows, columns), BF16),
        compiler_params=room(2),
        cost_estimate=cost(0, 0),
    )(*parts)


def weights_kernel(at_ref, up_ref, down_ref, qkv_ref, up_own_ref, down_own_ref, qkv_own_ref, sems):
    part = at_ref[0]
    own = up_own_ref.shape[1]
    at_own = pl.ds(pl.multiple_of(part * own, own), own)
    copies = [
        pltpu.make_async_copy(up_ref.at[:, at_own], up_own_ref, sems.at[0]),
        pltpu.make_async_copy(down_ref.at[at_own, :], down_own_ref, sems.at[1]),
    ]
    for n in range(3):
        at_third = pl.ds(pl.multiple_of((4 * n + part) * WIDE, WIDE), WIDE)
        to_third = pl.ds(n * WIDE, WIDE)
        copies.append(pltpu.make_async_copy(qkv_ref.at[:, at_third], qkv_own_ref.at[:, to_third], sems.at[2 + n]))
    for copy in copies:
        copy.start()
    for copy in copies:
        copy.wait()


def own_weights(at, up_weight, down_weight, qkv_weight):
    own = up_weight.shape[1] // 4
    return pl.pallas_call(
        weights_kernel,
        in_specs=[SMEM] + [ANY] * 3,
        out_specs=[VMEM] * 3,
        out_shape=[shape_of((D, own), BF16), shape_of((own, D), BF16), shape_of((D, 3 * WIDE), BF16)],
        scratch_shapes=[pltpu.SemaphoreType.DMA((5,))],
        compiler_params=room(57),
        cost_estimate=cost(0, 0),
    )(at, up_weight, down_weight, qkv_weight)


def normalise(rows):
    resid = rows.astype(F32)
    row_mean = jnp.mean(resid, -1, keepdims=True)
    centered = resid - row_mean
    inv_std = lax.rsqrt(jnp.mean(centered * centered, -1, keepdims=True) + norm_eps)
    return centered * inv_std


def chosen(rows, index):
    at = lax.broadcasted_iota(jnp.int32, rows.shape, 0)
    return jnp.sum(jnp.where(at == index, rows, 0.0), 0, keepdims=True)


def front_kernel(
    at_ref, low_ref, high_ref, mine_ref, theirs_ref, up_ref, up_bias_ref,
    attn_ref, feed_ref, hidden_ref, slope_ref, gains_ref,
):
    on_low = at_ref[1] == 0
    mine = mine_ref[WIDE:, :]
    theirs = theirs_ref[theirs_ref.shape[0] - 16 :, :]
    theirs = theirs[:, : mine.shape[1]]
    both = jnp.concatenate([jnp.where(on_low, mine, theirs), jnp.where(on_low, theirs, mine)], 1)
    gains_ref[...] = both.astype(F32)[:8]
    up_bias = chosen(up_bias_ref[...].astype(F32), at_ref[0])
    rows = low_ref.shape[0] // 2
    for source, base in ((low_ref, 0), (high_ref, low_ref.shape[0])):
        for i in range(source.shape[0] // rows):
            at = slice(base + i * rows, base + (i + 1) * rows)
            normed = normalise(source[i * rows : (i + 1) * rows, :])
            feed_in = (normed * gains_ref[2:3] + gains_ref[3:4]).astype(BF16)
            attn_ref[at, :] = (normed * gains_ref[0:1] + gains_ref[1:2]).astype(BF16)
            feed_ref[at, :] = feed_in
            preact = jnp.dot(feed_in, up_ref[...], preferred_element_type=F32) + up_bias
            normal_cdf = 0.5 * (1.0 + lax.erf(preact * (1.0 / math.sqrt(2.0))))
            hidden_ref[at, :] = (preact * normal_cdf).astype(BF16)
            slope_ref[at, :] = normal_cdf + preact * jnp.exp(-0.5 * preact * preact) * (1.0 / math.sqrt(2.0 * math.pi))


def front(at, low, high, mine, theirs, up_own, up_bias):
    count, own = 2 * low.shape[0], up_own.shape[1]
    return pl.pallas_call(
        front_kernel,
        in_specs=[SMEM] + [VMEM] * 6,
        out_specs=[VMEM] * 5,
        out_shape=[shape_of((count, D), BF16)] * 2
        + [shape_of((count, own), BF16), shape_of((count, own), F32), shape_of((8, D), F32)],
        compiler_params=room(8),
        cost_estimate=cost(0, 0),
    )(at, low, high, mine, theirs, up_own, up_bias)


def project_kernel(
    at_ref, rows_ref, qkv_ref, b_ref, keep_ref, turn_up_ref, turn_down_ref, first_ref, passed_ref, third_ref
):
    on_low = at_ref[1] == 0
    part = at_ref[0]
    all_bias = b_ref[...].astype(F32)
    bias = jnp.concatenate([chosen(all_bias, 4 * n + part) for n in range(3)], 1)
    half = ROT // 2
    length = keep_ref.shape[0]
    rows = 2 * length

    def turned(part):
        left = pltpu.roll(part, WIDE - half, 1)
        right = pltpu.roll(part, half, 1)
        pieces = []
        for i in range(part.shape[0] // length):
            at = slice(i * length, (i + 1) * length)
            pieces.append(part[at] * keep_ref[...] + left[at] * turn_up_ref[...] + right[at] * turn_down_ref[...])
        return jnp.concatenate(pieces, 0)

    for i in range(rows_ref.shape[0] // rows):
        at = slice(i * rows, (i + 1) * rows)
        value = jnp.dot(rows_ref[at, :], qkv_ref[...], preferred_element_type=F32) + bias
        first_ref[at, :] = turned(value[:, :WIDE]).astype(BF16)
        passed, third = value[:, WIDE : 2 * WIDE], value[:, 2 * WIDE :]
        passed_ref[at, :] = jnp.where(on_low, turned(passed), passed).astype(BF16)
        third_ref[at, :] = jnp.where(on_low, turned(third), third).astype(BF16)


def project(at, rows, qkv_own, qkv_bias, tables):
    count = rows.shape[0]
    return pl.pallas_call(
        project_kernel,
        in_specs=[SMEM] + [VMEM] * 6,
        out_specs=[VMEM] * 3,
        out_shape=[shape_of((count, WIDE), BF16)] * 3,
        compiler_params=room(8),
        cost_estimate=cost(2 * count * D * 3 * WIDE, 4 * count * D),
    )(at, rows, qkv_own, qkv_bias, *tables)


def down_kernel(hidden_ref, low_ref, high_ref, cot_ref, first_ref, second_ref):
    half, half_d = low_ref.shape[0], low_ref.shape[1] // 2
    cot_ref[:half, :] = low_ref[...]
    cot_ref[half:, :] = high_ref[...]
    first_ref[...] = dot_over(hidden_ref[...], cot_ref[:, :half_d], (0, 0)).astype(BF16)
    second_ref[...] = dot_over(hidden_ref[...], cot_ref[:, half_d:], (0, 0)).astype(BF16)


def grad_down_chunks(hidden, low, high):
    count, own = hidden.shape
    return pl.pallas_call(
        down_kernel,
        in_specs=[VMEM] * 3,
        out_specs=[VMEM] * 3,
        out_shape=[shape_of((count, D), BF16)] + [shape_of((own, D // 2), BF16)] * 2,
        compiler_params=room(10),
        cost_estimate=cost(2 * count * own * D, 6 * count * D),
    )(hidden, low, high)


def attention_kernel(
    at_ref, first_ref, third_ref, taken_ref, grad_ref, keep_ref, up_ref, down_ref, away_ref, here_ref
):
    length, width = keep_ref.shape
    on_low = at_ref[1] == 0
    lane = lax.broadcasted_iota(jnp.int32, (length, width), 1)
    causal = lax.broadcasted_iota(jnp.int32, (length, length), 0) >= lax.broadcasted_iota(
        jnp.int32, (length, length), 1
    )
    scale = 1.0 / math.sqrt(HD)
    half = ROT // 2

    def back(value):
        return (
            value * keep_ref[...]
            - pltpu.roll(value, width - half, 1) * up_ref[...]
            - pltpu.roll(value, half, 1) * down_ref[...]
        )

    for i in range(first_ref.shape[0] // length):
        rows = slice(i * length, (i + 1) * length)
        first, third, taken, grad = first_ref[rows, :], third_ref[rows, :], taken_ref[rows, :], grad_ref[rows, :]
        query = jnp.where(on_low, first, taken)
        keys = jnp.where(on_low, third, first)
        values = jnp.where(on_low, taken, third)
        zero = jnp.zeros_like(query)
        found = []
        for head in range(width // HD):
            mine = (lane >= head * HD) & (lane < (head + 1) * HD)
            scores = dot_over(jnp.where(mine, query, zero), keys, (1, 1)) * scale
            scores = jnp.where(causal, scores, -jnp.inf)
            row_max = jnp.max(scores, -1, keepdims=True)
            log_total = row_max + jnp.log(jnp.sum(jnp.exp(scores - row_max), -1, keepdims=True))
            probs = jnp.exp(scores - log_total)
            probs_b = probs.astype(BF16)
            attended = jnp.dot(probs_b, values, preferred_element_type=F32)
            grad_values = dot_over(probs_b, grad, (0, 0))
            grad_probs = dot_over(jnp.where(mine, grad, zero), values, (1, 1))
            inner = jnp.sum(probs * grad_probs, -1, keepdims=True)
            grad_scores = (probs * (grad_probs - inner) * scale).astype(BF16)
            grad_query = jnp.dot(grad_scores, keys, preferred_element_type=F32)
            grad_keys = dot_over(grad_scores, query, (0, 0))
            new = (attended, grad_query, grad_keys, grad_values)
            found = new if not found else tuple(jnp.where(mine, n, o) for n, o in zip(new, found))
        attended, grad_query, grad_keys, grad_values = found
        grad_query, grad_keys = back(grad_query), back(grad_keys)
        away_ref[rows, :width] = attended.astype(BF16)
        away_ref[rows, width:] = jnp.where(on_low, grad_values, grad_query).astype(BF16)
        here_ref[rows, :width] = jnp.where(on_low, grad_query, grad_keys).astype(BF16)
        here_ref[rows, width:] = jnp.where(on_low, grad_keys, grad_values).astype(BF16)


def heads_kernel(at_ref, mine_ref, theirs_ref, cot_ref, rows_ref, grad_ref):
    on_low = at_ref[1] == 0
    mine, theirs = mine_ref[:WIDE, :], theirs_ref[...]
    rows = jnp.concatenate([jnp.where(on_low, mine, theirs), jnp.where(on_low, theirs, mine)], 1)
    rows_ref[...] = rows
    grad_ref[...] = dot_over(cot_ref[...], rows, (1, 1)).astype(BF16)


def back_to_heads(at, mine, theirs, cot):
    return pl.pallas_call(
        heads_kernel,
        in_specs=[SMEM] + [VMEM] * 3,
        out_specs=[VMEM] * 2,
        out_shape=[shape_of((WIDE, D), BF16), shape_of((cot.shape[0], WIDE), BF16)],
        compiler_params=room(6),
        cost_estimate=cost(2 * cot.size * WIDE, 2 * cot.size),
    )(at, mine, theirs, cot)


def swapped(i):
    return i + 1 - 2 * (i % 2)


def attention(at, first, third, taken, grad, tables):
    count, width = first.shape
    length = tables[0].shape[0]
    block = pl.BlockSpec((2 * length, width), lambda i, s: (i, 0))
    other = pl.BlockSpec((2 * length, width), lambda i, s: (swapped(i), 0))
    table = pl.BlockSpec((length, width), lambda i, s: (0, 0))
    out = pl.BlockSpec((2 * length, 2 * width), lambda i, s: (i, 0))
    return pl.pallas_call(
        attention_kernel,
        grid_spec=pltpu.PrefetchScalarGridSpec(
            num_scalar_prefetch=1,
            grid=(count // (2 * length),),
            in_specs=[block, block, other, block] + [table] * 3,
            out_specs=[out, out],
        ),
        out_shape=[shape_of((count, 2 * width), BF16)] * 2,
        compiler_params=room(12),
        cost_estimate=cost(24 * count * length * width, 16 * count * width, 4 * count * length),
    )(at, first, third, taken, grad, *tables)


def branch_kernel(hidden_ref, away_ref, down_ref, out_rows_ref, kept_ref, sent_ref):
    half = kept_ref.shape[0]
    branches = jnp.dot(hidden_ref[...], down_ref[...], preferred_element_type=F32) + jnp.dot(
        away_ref[:, :WIDE], out_rows_ref[...], preferred_element_type=F32
    )
    kept_ref[...] = branches[:half]
    sent_ref[...] = branches[half:].astype(BF16)


def branch_sums(hidden, away, down_own, out_rows):
    count, own = hidden.shape
    return pl.pallas_call(
        branch_kernel,
        in_specs=[VMEM] * 4,
        out_specs=[VMEM] * 2,
        out_shape=[shape_of((count // 2, D), F32), shape_of((count // 2, D), BF16)],
        compiler_params=room(10),
        cost_estimate=cost(2 * count * D * (own + WIDE), 6 * count * D),
    )(hidden, away, down_own, out_rows)


def group_kernel(
    at_ref, low_ref, high_ref, cotangent_ref, gp_ref, away_ref, here_ref, other_ref, up_ref, qkv_ref, gains_ref,
    kept_ref, sent_ref, sums_ref, proj_ref, att_ref,
):
    on_low = at_ref[1] == 0
    gains = gains_ref[...]
    own = gp_ref.shape[1]
    rows = low_ref.shape[0] // 2
    total = lambda v: jnp.sum(v.astype(F32), 0, keepdims=True)
    sums = None
    for i in range(4):
        at, swap = slice(i * rows, (i + 1) * rows), swapped(i)
        away, here, other = away_ref[at, :], here_ref[at, :], other_ref[swap * rows : (swap + 1) * rows, :]
        attended, attended_other = away[:, :WIDE], other[:, :WIDE]
        proj = jnp.concatenate([here[:, :WIDE], other[:, WIDE:], here[:, WIDE:]], 1)
        proj_ref[at, :] = proj
        att_ref[at, :] = jnp.concatenate(
            [jnp.where(on_low, attended, attended_other), jnp.where(on_low, attended_other, attended)], 1
        )
        gp = gp_ref[at, :]
        grad_attn = dot_over(proj, qkv_ref[...], (1, 1))
        grad_feed = dot_over(gp, up_ref[...], (1, 1))
        source = low_ref if i < 2 else high_ref
        local = slice((i % 2) * rows, (i % 2 + 1) * rows)
        normed = normalise(source[local, :])
        grad_normed = grad_attn * gains[0:1] + grad_feed * gains[2:3]
        new = [
            total(grad_attn * normed),
            total(grad_attn),
            total(grad_feed * normed),
            total(grad_feed),
            total(gp),
            total(proj),
        ]
        sums = new if sums is None else [a + b for a, b in zip(sums, new)]
        if i < 2:
            kept_ref[local, :] = grad_normed
        else:
            sent_ref[local, :] = grad_normed.astype(BF16)
    last = jnp.concatenate([sums[4], sums[5], jnp.zeros((1, D - own - 3 * WIDE), F32)], 1)
    sums_ref[...] = jnp.concatenate(sums[:4] + [total(cotangent_ref[...]), last, jnp.zeros((2, D), F32)], 0)


def group_sums(at, low, high, cotangent, gp, away, here, other, up_own, qkv_own, gains):
    count, own = gp.shape
    return pl.pallas_call(
        group_kernel,
        in_specs=[SMEM] + [VMEM] * 10,
        out_specs=[VMEM] * 5,
        out_shape=[
            shape_of((count // 2, D), F32),
            shape_of((count // 2, D), BF16),
            shape_of((8, D), F32),
            shape_of((count, 3 * WIDE), BF16),
            shape_of((count, 2 * WIDE), BF16),
        ],
        compiler_params=room(12),
        cost_estimate=cost(2 * count * D * (own + 3 * WIDE), 16 * count * D),
    )(at, low, high, cotangent, gp, away, here, other, up_own, qkv_own, gains)


def mixed_kernel(at_ref, rows_ref, proj_ref, att_ref, cot_ref, *refs):
    out_ref = refs[-1]
    out_ref[: 4 * WIDE, : 3 * WIDE] = dot_over(rows_ref[...], proj_ref[...], (0, 0)).astype(BF16)
    heads = dot_over(att_ref[...], cot_ref[...], (0, 0)).astype(BF16)
    out_ref[: 2 * WIDE, 3 * WIDE :] = heads[:, :WIDE]
    out_ref[2 * WIDE : 4 * WIDE, 3 * WIDE :] = heads[:, WIDE:]
    if len(refs) > 1:
        sums, other = refs[0][...], refs[1][...]
        row = lax.broadcasted_iota(jnp.int32, sums.shape, 0)
        sums = jnp.where(row < 5, sums + other, sums).astype(BF16)
        out_ref[4 * WIDE :, :] = jnp.concatenate([sums[:, : D // 2], sums[:, D // 2 :]], 0)


def mixed(at, half, rows, proj, att, cot, small):
    count = rows.shape[0]
    fixed = lambda i, s: (0, 0)
    tall = 4 * WIDE + (16 if small else 0)
    return pl.pallas_call(
        mixed_kernel,
        grid_spec=pltpu.PrefetchScalarGridSpec(
            num_scalar_prefetch=1,
            grid=(1,),
            in_specs=[
                pl.BlockSpec((count, 4 * WIDE), lambda i, s: (0, half)),
                pl.BlockSpec(proj.shape, fixed),
                pl.BlockSpec(att.shape, fixed),
                pl.BlockSpec((count, 2 * WIDE), lambda i, s: (0, 2 * s[1] + half)),
            ]
            + [pl.BlockSpec((8, D), fixed)] * len(small),
            out_specs=pl.BlockSpec((tall, 4 * WIDE), fixed),
        ),
        out_shape=shape_of((tall, 4 * WIDE), BF16),
        compiler_params=room(12),
        cost_estimate=cost(2 * count * 16 * WIDE * WIDE, 4 * count * D),
    )(at, rows, proj, att, cot, *small)


TALL = 528


def turn(at, grad, from_z, first, from_middle, following, carried, from_y):
    outs = []
    given = dict(
        grad=grad, from_z=from_z, first=first, from_middle=from_middle, following=following, carried=carried, from_y=from_y
    )
    names = [n for n, v in given.items() if v is not None]
    if grad is not None:
        outs.append(("first", grad.shape))
    if first is not None or following is not None:
        outs.append(("next", (following if following is not None else first).shape))
    if carried is not None:
        plain = carried.shape[0] < TALL or following is not None or grad is not None
        outs.append(("total", (512, 512) if plain else carried.shape))
    if carried is not None or from_y is not None:
        outs.append(("pair", (2 * TALL, 512)))

    def kernel(at_ref, *refs):
        values = dict(zip(names, refs))
        results = dict(zip([n for n, _ in outs], refs[len(names) :]))
        middle = at_ref[2] == 1
        if "first" in results:
            results["first"][...] = values["grad"][...] + values["from_z"][...]
        if "next" in results:
            out = results["next"]
            if "first" in values:
                tall = values["first"].shape[0]
                summed = values["first"][...] + values["from_middle"][...]
                if "following" in values:
                    out[:tall, :] = jnp.where(middle, summed, values["following"][:tall, :])
                    if out.shape[0] > tall:
                        out[tall:, :] = values["following"][tall:, :]
                else:
                    out[...] = summed
            else:
                out[...] = values["following"][...]
        if "total" in results:
            tall = results["total"].shape[0]
            total = jnp.where(middle, values["carried"][:tall, :], values["from_z"][:tall, :])
            results["total"][...] = total
            results["pair"][:tall, :] = total
            if tall < TALL:
                results["pair"][tall:TALL, :] = jnp.zeros((TALL - tall, 512), BF16)
        elif "pair" in results:
            results["pair"][:TALL, :] = jnp.zeros((TALL, 512), BF16)
        if "pair" in results:
            tall = values["from_y"].shape[0] if "from_y" in values else 0
            if tall:
                results["pair"][TALL : TALL + tall, :] = values["from_y"][...]
            if tall < TALL:
                results["pair"][TALL + tall :, :] = jnp.zeros((TALL - tall, 512), BF16)

    made = pl.pallas_call(
        kernel,
        in_specs=[SMEM] + [VMEM] * len(names),
        out_specs=[VMEM] * len(outs),
        out_shape=[shape_of(s, BF16) for _, s in outs],
        compiler_params=room(6),
        cost_estimate=cost(len(names) * 2**18, (len(names) + len(outs)) * 2**19),
    )(at, *[given[n] for n in names])
    return dict(zip([n for n, _ in outs], made))


def place(at, pieces, into, shapes, copies):
    count = len(shapes)
    each = len(copies(0))
    tall = 4 * WIDE

    def kernel(at_ref, *refs):
        piece_refs = refs[:4]
        out_refs = refs[4 + (count if into else 0) :][:count]
        wide_ref, sems = refs[-2:]
        started = []
        for i in range(4):
            base = TALL if i == 3 else 0
            wide_ref[i] = piece_refs[i][base : base + tall, :].astype(F32)
            for n, (which, at, part) in enumerate(copies(at_ref[3 + i])):
                copy = pltpu.make_async_copy(wide_ref.at[i].at[part], out_refs[which].at[at], sems.at[i * each + n])
                copy.start()
                started.append(copy)
        for copy in started:
            copy.wait()

    any_space = pl.BlockSpec(memory_space=pl.ANY)
    return pl.pallas_call(
        kernel,
        in_specs=[SMEM] + [VMEM] * 4 + [any_space] * len(into or ()),
        out_specs=[any_space] * count,
        scratch_shapes=[pltpu.VMEM((4, tall, tall), F32), pltpu.SemaphoreType.DMA((4 * each,))],
        out_shape=[shape_of(s, F32) for s in shapes],
        compiler_params=room(8),
        input_output_aliases={5 + k: k for k in range(count)} if into else {},
        cost_estimate=cost(0, 24 * tall * tall),
    )(at, *pieces, *(into or ()))


def fold_kernel(kept_ref, got_ref, stay_ref, go_ref):
    rows = stay_ref.shape[0]
    stay_ref[...] = kept_ref[:rows, :] + got_ref[:rows, :].astype(F32)
    go_ref[...] = (kept_ref[rows:, :] + got_ref[rows:, :].astype(F32)).astype(BF16)


def fold(kept, got):
    rows = kept.shape[0] // 2
    return pl.pallas_call(
        fold_kernel,
        in_specs=[VMEM] * 2,
        out_specs=[VMEM] * 2,
        out_shape=[shape_of((rows, D), F32), shape_of((rows, D), BF16)],
        compiler_params=room(4),
        cost_estimate=cost(kept.size, 9 * kept.size),
    )(kept, got)


def last_kernel(inputs_ref, cotangent_ref, gains_ref, a_ref, b_ref, c_ref, d_ref, outputs_ref, grad_ref):
    resid = inputs_ref[...].astype(F32)
    row_mean = jnp.mean(resid, -1, keepdims=True)
    centered = resid - row_mean
    inv_std = lax.rsqrt(jnp.mean(centered * centered, -1, keepdims=True) + norm_eps)
    normed = centered * inv_std
    branches = a_ref[...] + b_ref[...].astype(F32)
    outputs_ref[...] = (resid + branches + (gains_ref[4:5] + gains_ref[5:6])).astype(BF16)
    grad_normed = c_ref[...] + d_ref[...].astype(F32)
    grad_ref[...] = cotangent_ref[...].astype(F32) + inv_std * (
        grad_normed
        - jnp.mean(grad_normed, -1, keepdims=True)
        - normed * jnp.mean(grad_normed * normed, -1, keepdims=True)
    )


def last(inputs, cotangent, gains, *sums):
    return pl.pallas_call(
        last_kernel,
        in_specs=[VMEM] * 7,
        out_specs=[VMEM] * 2,
        out_shape=[shape_of(inputs.shape, BF16), shape_of(inputs.shape, F32)],
        compiler_params=room(4),
        cost_estimate=cost(inputs.size * 20, inputs.size * 20),
    )(inputs, cotangent, gains, *sums)


def at_blocks(first, size):
    return pl.ds(pl.multiple_of(first, size), size)


def small_kernel(at_ref, a_ref, b_ref, c_ref, d_ref, g1, s1, g2, s2, ob, up_ref, qkv_ref):
    on_low = at_ref[1] == 0
    parts = [r[...].astype(F32) for r in (a_ref, b_ref, c_ref, d_ref)]
    sums = (parts[0] + parts[1]) + (parts[2] + parts[3])
    sums = jnp.where(on_low, sums[:8], sums[8:])
    for row, ref in enumerate((g1, s1, g2, s2, ob)):
        ref[...] = sums[row : row + 1]
    for i, part in enumerate(parts):
        p = at_ref[3 + i]
        up_ref[pl.ds(p, 1), :] = part[5:6]
        for n in range(3):
            qkv_ref[pl.ds(4 * n + p, 1), :] = part[13:14, n * WIDE : (n + 1) * WIDE]


def small_outputs(at, pieces):
    fixed = lambda i, s: (0, 0)
    half_d = D // 2
    return pl.pallas_call(
        small_kernel,
        grid_spec=pltpu.PrefetchScalarGridSpec(
            num_scalar_prefetch=1,
            grid=(1,),
            in_specs=[pl.BlockSpec((16, half_d), lambda i, s: (32, 0))] * 3
            + [pl.BlockSpec((16, half_d), lambda i, s: (TALL // 16 + 32, 0))],
            out_specs=[pl.BlockSpec((1, half_d), fixed)] * 5
            + [pl.BlockSpec((4, half_d), fixed), pl.BlockSpec((12, WIDE), fixed)],
        ),
        compiler_params=room(2),
        out_shape=[shape_of((1, half_d), F32)] * 5 + [shape_of((4, half_d), F32), shape_of((12, WIDE), F32)],
    )(at, *pieces)


def fast_body(
    inputs,
    attn_gain,
    attn_shift,
    feed_gain,
    feed_shift,
    qkv_weight,
    qkv_bias,
    out_weight,
    out_bias,
    up_weight,
    up_bias,
    down_weight,
    down_bias,
    cotangent,
):
    length = inputs.shape[0]
    rep, x = lax.axis_index("rep"), lax.axis_index("shard")
    z, y, c = rep // 4, rep // 2 % 2, rep % 2
    part = y * 2 + c
    middle = ((z == 1) | (z == 2)).astype(jnp.int32)
    at = jnp.stack([part, x, middle, part, part ^ 2, part ^ 1, part ^ 3, part]).astype(jnp.int32)
    fence = lax.optimization_barrier
    half_d = D // 2
    tables = rotary_arrays(length)
    vectors = [attn_gain, attn_shift, feed_gain, feed_shift, out_bias, down_bias]
    own = up_weight.shape[1] // 4

    from_y, from_xy = send(inputs, TO_Y), send(inputs, TO_XY)
    mine, packed, their_rows = pack(at, inputs, out_weight, vectors)
    from_x = send(packed, TO_X)
    cot_first, mine = fence((cotangent, mine))
    cot_parts = [send(cot_first, p) for p in (TO_Y, TO_X, TO_XY)]
    up_own, down_own, qkv_own = own_weights(at, up_weight, down_weight, qkv_weight)
    from_x, from_y, from_xy, up_own, down_own, qkv_own = fence((from_x, from_y, from_xy, up_own, down_own, qkv_own))
    low = stack(inputs, from_y, from_x, from_xy)
    theirs = from_x
    high = send(low, TO_CORE)
    cot_parts, low = fence((cot_parts, low))
    low_cot = stack(cotangent, *cot_parts)
    high_cot = send(low_cot, TO_CORE)
    attn_in, feed_in, hidden, slope, gains = front(
        at, low, high, mine, theirs, up_own, up_bias.reshape(4, -1)
    )
    cot, chunk0, chunk1 = grad_down_chunks(hidden, low_cot, high_cot)

    env = dict(
        attn_in=attn_in, feed_in=feed_in, hidden=hidden, slope=slope, cot=cot,
        qkv_own=qkv_own, mine=mine, their_rows=their_rows, gains=gains, low=low, high=high, down_own=down_own, up_own=up_own,
    )
    chunks = {0: chunk0, 1: chunk1}
    loose = {}

    def after(step, env):
        e = dict(env)
        if step == 0:
            e["first"], passed, e["third"] = project(
                at, e["attn_in"], e["qkv_own"], qkv_bias.reshape(12, -1), tables
            )
            e["taken"] = send(passed, TO_X)
            their_rows, e["first"] = fence((e.pop("their_rows"), e["first"]))
            e["rows"] = send(their_rows, TO_X)
            gp = dot_over(e["cot"], e["down_own"], (1, 1)) * e.pop("slope")
            e["gp"] = gp.astype(BF16)
            chunks[2] = dot_over(e["feed_in"][:, :half_d], e["gp"], (0, 0)).astype(BF16)
        if step == 1:
            e["out_rows"], e["ga"] = back_to_heads(at, e.pop("mine"), e.pop("rows"), e["cot"])
            e["away"], e["here"] = attention(
                at, e.pop("first"), e.pop("third"), e.pop("taken"), e.pop("ga"), tables
            )
            chunks[3] = dot_over(e.pop("feed_in")[:, half_d:], e["gp"], (0, 0)).astype(BF16)
            e["kb"], e["sb"] = branch_sums(e.pop("hidden"), e["away"], e.pop("down_own"), e.pop("out_rows"))
        if step == 2:
            e["other"] = send(e["away"], TO_X)
            e["kb"], e["sb"] = fold(e["kb"], send(e["sb"], TO_CORE))
        if step == 3:
            e["kg"], e["sg"], e["sums"], e["proj"], e["att"] = group_sums(
                at, e.pop("low"), e.pop("high"), cotangent, e.pop("gp"), e.pop("away"), e.pop("here"),
                e.pop("other"), e.pop("up_own"), e.pop("qkv_own"), e["gains"],
            )
            chunks[4] = mixed(at, 0, e["attn_in"], e["proj"], e["att"], e["cot"], ())
            e["kb"], e["sb"] = fold(e["kb"], send(e["sb"], TO_X))
        if step == 4:
            other = send(e["sums"], TO_X)
            chunks[5] = mixed(
                at, 1, e.pop("attn_in"), e.pop("proj"), e.pop("att"), e.pop("cot"), (e.pop("sums"), other)
            )
        if step == 5:
            e["kg"], e["sg"] = fold(e["kg"], send(e["sg"], TO_CORE))
        if step == 6:
            e["kg"], e["sg"] = fold(e["kg"], send(e["sg"], TO_X))
        if step == Y_RETURN - 1:
            e["gb"] = send(e.pop("sb"), TO_Y)
        if step == Y_RETURN:
            loose["g"] = send(e.pop("sg"), TO_Y)
        return e

    count = 6
    operand, one, total, over_y, pair, got_pair = {}, {}, {}, {}, {}, {}
    outs = {}
    operand[0] = chunks[0]

    def finish(k):
        pieces = [total.pop(k), over_y.pop(k), got_pair.pop(k), got_pair[k + 1]]
        h = k % 2
        rows, columns = pl.ds(h * half_d, half_d), pl.ds(h * half_d, half_d)
        everything = (slice(None), slice(None))
        if k < 2:
            outs["down"] = place(
                at, pieces, outs.get("down"), [down_weight.shape],
                lambda p: [(0, (at_blocks(own * p, own), columns), everything)],
            )
        elif k < 4:
            outs["up"] = place(
                at, pieces, outs.get("up"), [up_weight.shape],
                lambda p: [(0, (rows, at_blocks(own * p, own)), everything)],
            )
        else:
            outs["attn"] = place(
                at, pieces, outs.get("attn"), [qkv_weight.shape, out_weight.shape],
                lambda p: [
                    (0, (rows, at_blocks(half_d * n + WIDE * p, WIDE)), (slice(None), pl.ds(n * WIDE, WIDE)))
                    for n in range(3)
                ]
                + [
                    (
                        1,
                        (at_blocks(half_d * side + WIDE * p, WIDE), pl.ds((2 * h + b) * WIDE, WIDE)),
                        (pl.ds((2 * b + side) * WIDE, WIDE), pl.ds(3 * WIDE, WIDE)),
                    )
                    for b in range(2)
                    for side in range(2)
                ],
            )
        if k == count - 1:
            outs["small"] = small_outputs(at, pieces)

    for step in range(count + 5):
        live = (env, chunks, operand, one, total, over_y, pair, got_pair, outs)
        env, chunks, operand, one, total, over_y, pair, got_pair, outs = fence(live)
        got = {}
        if 0 <= step - 1 < count:
            got["m"] = send(one[step - 1], MIDDLE)
        if step < count + 2:
            pairs = (INWARD if step < count else []) + (OUTWARD if step >= 2 else [])
            got["z"] = send(operand[step], pairs)
        if 0 <= step - 3 < count:
            got["y"] = send(total[step - 3], TO_Y)
        if step - 3 in pair:
            got["c"] = send(pair.pop(step - 3), TO_CORE)
        env = after(step, env)
        if 0 <= step - 5 < count:
            finish(step - 5)
        if step < count + 3:
            made = turn(
                at,
                chunks.pop(step) if step < count else None,
                got.get("z"),
                one.pop(step - 1) if 0 <= step - 1 < count else None,
                got.get("m"),
                chunks.get(step + 1),
                operand.pop(step) if 2 <= step < count + 2 else None,
                got.get("y"),
            )
            if "first" in made:
                one[step] = made["first"]
            if "next" in made:
                operand[step + 1] = made["next"]
            if "total" in made:
                total[step - 2] = made["total"]
            if "pair" in made:
                pair[step - 2] = made["pair"]
        if "y" in got:
            over_y[step - 3] = got["y"]
        if "c" in got:
            got_pair[step - 3] = got["c"]

    outputs, input_grad = last(inputs, cotangent, env["gains"], env["kb"], env["gb"], env["kg"], loose["g"])
    g1, s1, g2, s2, ob, up_b, qkv_b = outs["small"]
    flat = lambda a: a.reshape(-1)
    return (
        outputs,
        input_grad,
        flat(g1),
        flat(s1),
        flat(g2),
        flat(s2),
        outs["attn"][0],
        flat(qkv_b),
        outs["attn"][1],
        flat(ob),
        outs["up"][0],
        flat(up_b),
        outs["down"][0],
        flat(ob),
    )


def choose_body(mesh):
    known = {"rep": Z * Y * C, "shard": X}
    return fast_body if dict(mesh.shape) == known else general_body


def solution(mesh):
    return jax.shard_map(
        choose_body(mesh),
        mesh=mesh,
        in_specs=(
            P(("rep", "shard"), None),
            P("shard"),
            P("shard"),
            P("shard"),
            P("shard"),
            P(None, "shard"),
            P("shard"),
            P(None, "shard"),
            P("shard"),
            P(None, "shard"),
            P("shard"),
            P("shard", None),
            P("shard"),
            P(("rep", "shard"), None),
        ),
        out_specs=(
            P(("rep", "shard"), None),
            P(("rep", "shard"), None),
            P("shard"),
            P("shard"),
            P("shard"),
            P("shard"),
            P(None, "shard"),
            P("shard"),
            P(None, "shard"),
            P("shard"),
            P(None, "shard"),
            P("shard"),
            P("shard", None),
            P("shard"),
        ),
        check_vma=False,
    )
```
